128 devices in a mesh: space: 32 (over z, y, core), mode: 4 (over x).
Axes of the slice: x: 4, y: 4, z: 4, core: 2. Of those that a mesh axis runs over, the one named last changes fastest.
Arguments:
- velocity: float32 [3, 512, 512, 256], P(None, 'space', 'mode'), may hold values from -6 to 6
- basis: float32 [32, 3145728], P('mode', 'space'), may hold values from -42 to 42
- levels: float32 [8], replicated, may hold values from 0.02 to 0.15
- profile_index: int32 [256], replicated, may hold values from 0 to 7
- advect: float32 [256], replicated, may hold values from 0 to 0.4
Outputs:
- modes: float32 [32, 3145728], P('mode', 'space')
- sigma: float32 [32], replicated
The draws below stay inside these ranges and needn't reach their ends.
Inputs may be any that keep to these rules, and one draw needn't show every extreme that they name: `profile_index`: each entry picks one of the 8 viscosity levels.
All inputs are finite; a program needn't handle non-finite values.
Results may differ from the reference program's by a relative error of at most 0.0055.
Values sent between devices are 32-bit elements; how exact they have to be, the bound alone decides.
No kernel may reach another device: no remote copies, remote signals or barrier semaphores. Data moves between devices by JAX's collectives and lax.ppermute only.
A program may use at most 128 MiB of HBM per device.

```python
import math
import jax
import jax.numpy as jnp
import numpy as np
from jax import lax

CX = 16
CZ = 128
NY = 256
STRIDE = 4
MODES = 32
SWEEPS = 2
LEVELS = 8
NX = 512
NZ = 512
ROWS = 3145728
N_SPACE = 32
N_MODE = 4


def draw_basis(key, part):
    key_noise = jax.random.fold_in(key, 11)
    key_rows = jax.random.fold_in(key, 12)
    key_cols = jax.random.fold_in(key, 13)
    noise = jnp.clip(jax.random.normal(key_noise, (MODES, ROWS), jnp.float32), -4.0, 4.0)
    mixed = noise + 0.4 * jnp.roll(noise, -1, axis=0)
    row_scale = jnp.exp(jax.random.uniform(key_rows, (1, ROWS), jnp.float32, math.log(0.25), math.log(2.5)))
    trend = 0.5 + jnp.arange(ROWS, dtype=jnp.float32)[None, :] / ROWS
    col_scale = jnp.exp(jax.random.uniform(key_cols, (MODES, 1), jnp.float32, math.log(0.5), math.log(2.0)))
    return mixed * row_scale * trend * col_scale


def touch_ends(entries, rng, smallest, top_value):
    dims = entries.shape
    index_at = [jax.random.randint(jax.random.fold_in(rng, axis), (), 0, dims[axis]) for axis in range(len(dims))]
    entries = entries.at[tuple(index_at)].set(smallest)
    longest = dims.index(max(dims))
    index_at[longest] = (index_at[longest] + 1) % dims[longest]
    return entries.at[tuple(index_at)].set(top_value)


def steps_of(key, dims, split, smallest, top_value):
    gain = 1.0
    for dim, blocks in split:
        draws = jax.random.uniform(jax.random.fold_in(jax.random.fold_in(key, 6), dim), (blocks,), jnp.float32, smallest / len(split), top_value / len(split))
        gain = gain * jnp.repeat(jnp.exp(draws), dims[dim] // blocks).reshape((-1,) + (1,) * (len(dims) - 1 - dim))
    return gain


def bell_draw(key, extent, deviation, reach, cuts=(), kind=jnp.bfloat16):
    drawn = deviation * jax.random.normal(key, extent, jnp.float32)
    if cuts:
        drawn = drawn * steps_of(key, extent, cuts, -0.22, 0.18)
    return jnp.clip(drawn, -reach, reach).astype(kind)


def setup_inputs(seed: int = 0) -> dict:
    arg_keys = jax.random.split(jax.random.key(seed), 6)
    velocity = bell_draw(arg_keys[0], (3, NX, NZ, NY), 1.0, 6.0, ((1, 32), (2, 4)), jnp.float32)
    basis = draw_basis(jax.random.fold_in(arg_keys[5], 71), 0)
    levels = jnp.clip(jnp.exp(jax.random.uniform(arg_keys[2], (LEVELS,), jnp.float32, math.log(0.02), math.log(0.15))), 0.02, 0.15)
    profile_index = touch_ends(jax.random.randint(arg_keys[3], (NY,), 0, LEVELS), jax.random.fold_in(arg_keys[3], 1), 0, LEVELS - 1).astype(jnp.int32)
    advect = jnp.clip(jax.random.uniform(arg_keys[4], (NY,), jnp.float32, 0.0, 0.4), 0.0, 0.4)
    return {"velocity": velocity, "basis": basis, "levels": levels, "profile_index": profile_index, "advect": advect}


def profile(levels, profile_index):
    table = (profile_index[:, None] == jnp.arange(levels.shape[0], dtype=jnp.int32)[None, :]).astype(jnp.float32)
    viscosity = lax.optimization_barrier(jnp.sum(table * levels[None, :], axis=1))
    middle = 0.5 * (viscosity[:-1] + viscosity[1:])
    face_up = jnp.concatenate([middle, viscosity[-1:]])
    face_down = jnp.concatenate([viscosity[:1], middle])
    return (viscosity, face_down, face_up)

def advance(field, viscosity, face_down, face_up, advect):
    center = field[:, 1:-1, 1:-1, :]
    east = field[:, 2:, 1:-1, :]
    west = field[:, :-2, 1:-1, :]
    north = field[:, 1:-1, 2:, :]
    south = field[:, 1:-1, :-2, :]
    walled = jnp.pad(center, ((0, 0), (0, 0), (0, 0), (1, 1)))
    upward = walled[..., 2:]
    downward = walled[..., :-2]
    lateral = east + west + north + south - 4.0 * center
    vertical = face_up * (upward - center) - face_down * (center - downward)
    return center + viscosity * lateral + vertical - 0.5 * advect * (east - west)

def box_sums(field):
    components, x_cells, z_cells, y_cells = field.shape
    boxes = field.reshape(components, x_cells // STRIDE, STRIDE, z_cells // STRIDE, STRIDE, y_cells // STRIDE, STRIDE)
    return lax.optimization_barrier(jnp.sum(boxes, axis=(2, 4, 6))) / math.sqrt(STRIDE ** 3)

def arrange(field):
    coarse = box_sums(field)
    blocks = coarse.reshape(3, N_SPACE, CX // STRIDE, N_MODE, CZ // STRIDE, NY // STRIDE)
    return blocks.transpose(1, 3, 0, 2, 4, 5).reshape(-1)

def pairing(count, turn):
    players = [0] + [1 + (i_pos - 1 + turn) % (count - 1) for i_pos in range(1, count)]
    leading = np.array(players[:count // 2])
    trailing = np.array([players[count - 1 - k_pos] for k_pos in range(count // 2)])
    return (leading, trailing)

def apply_pair(matrix, leading, trailing, cosine, sine_part):
    col_lead = matrix[:, leading]
    col_trail = matrix[:, trailing]
    matrix = matrix.at[:, leading].set(cosine * col_lead - sine_part * col_trail)
    return matrix.at[:, trailing].set(sine_part * col_lead + cosine * col_trail)

def jacobi_sweep(state):
    rotated, right_vecs = state
    count = rotated.shape[1]
    for turn in range(count - 1):
        leading, trailing = pairing(count, turn)
        col_lead = rotated[:, leading]
        col_trail = rotated[:, trailing]
        norm_lead = lax.optimization_barrier(jnp.sum(col_lead * col_lead, axis=0))
        norm_trail = lax.optimization_barrier(jnp.sum(col_trail * col_trail, axis=0))
        inner = lax.optimization_barrier(jnp.sum(col_lead * col_trail, axis=0))
        contrast = norm_trail - norm_lead
        orient = jnp.where(contrast >= 0.0, 1.0, -1.0)
        denominator = jnp.abs(contrast) + jnp.sqrt(contrast * contrast + 4.0 * inner * inner)
        positive = denominator > 0.0
        tangent = jnp.where(positive, 2.0 * inner * orient / jnp.where(positive, denominator, 1.0), 0.0)
        cosine = 1.0 / jnp.sqrt(1.0 + tangent * tangent)
        sine_part = cosine * tangent
        rotated = apply_pair(rotated, leading, trailing, cosine, sine_part)
        right_vecs = apply_pair(right_vecs, leading, trailing, cosine, sine_part)
    return (rotated, right_vecs)

def jacobi(upper):
    count = upper.shape[1]
    start = (upper, jnp.eye(count, dtype=jnp.float32))
    return lax.fori_loop(0, SWEEPS, lambda sweep_index, state: jacobi_sweep(state), start)

def reference(velocity, basis, levels, profile_index, advect):
    viscosity, face_down, face_up = profile(levels, profile_index)
    wrapped = jnp.pad(velocity, ((0, 0), (1, 1), (1, 1), (0, 0)), mode='wrap')
    first = advance(wrapped, viscosity, face_down, face_up, advect)
    wrapped = jnp.pad(first, ((0, 0), (1, 1), (1, 1), (0, 0)), mode='wrap')
    second = advance(wrapped, viscosity, face_down, face_up, advect)
    stack = jnp.concatenate([arrange(first)[None, :], arrange(second)[None, :], basis], axis=0)
    gram = lax.dot_general(stack.astype(jnp.float32), stack.astype(jnp.float32), (((1,), (1,)), ((), ())), precision=lax.Precision.HIGHEST, preferred_element_type=jnp.float32)
    lower = jnp.linalg.cholesky(gram)
    rotated, right_vecs = jacobi(lower.T)
    modes = jnp.dot(right_vecs[:, :MODES].T.astype(jnp.float32), stack.astype(jnp.float32), precision=lax.Precision.HIGHEST, preferred_element_type=jnp.float32)
    kept = rotated[:, :MODES]
    sigma = jnp.sqrt(lax.optimization_barrier(jnp.sum(kept * kept, axis=0)))
    return (modes, sigma)
```

```python
import jax
import jax.numpy as jnp
import numpy as np
from jax import lax
from jax.experimental import pallas as pl
from jax.experimental.pallas import tpu as pltpu
from jax.sharding import PartitionSpec as P

STRIDE = 4
MODES = 32
SWEEPS = 2
COUNT = 34
ROWS = 40
LANES = 128
PAD = 8
COLS = 24576


PLACE = np.array([0, 1] + list(range(PAD, PAD + MODES)))


def pair_tables():
    rounds = COUNT - 1
    partner = np.tile(np.arange(LANES, dtype=np.int32), (ROWS, 1))
    orient = np.ones((ROWS, LANES), np.float32)
    for turn in range(rounds):
        players = [0] + [1 + (i - 1 + turn) % rounds for i in range(1, COUNT)]
        for k in range(COUNT // 2):
            lead, trail = PLACE[players[k]], PLACE[players[COUNT - 1 - k]]
            partner[turn, lead] = trail
            partner[turn, trail] = lead
            orient[turn, lead] = -1.0
    keep = np.zeros((1, LANES), np.int32)
    keep[0, :MODES] = PLACE[:MODES]
    return partner, orient, keep


def coefficients(levels_ref, index_ref, advect_ref):
    index = index_ref[...]
    visc = jnp.zeros(index.shape, jnp.float32)
    for level in range(levels_ref.shape[0]):
        visc = jnp.where(index == level, levels_ref[level], visc)
    cells = index.shape[1]
    lane = lax.broadcasted_iota(jnp.int32, index.shape, 1)
    first, last = lane == 0, lane == cells - 1
    up = jnp.where(last, visc, 0.5 * (visc + pltpu.roll(visc, cells - 1, 1)))
    down = jnp.where(first, visc, 0.5 * (visc + pltpu.roll(visc, 1, 1)))
    half = 0.5 * advect_ref[...]
    return (
        1.0 - 4.0 * visc - up - down,
        visc,
        visc - half,
        visc + half,
        jnp.where(last, 0.0, up),
        jnp.where(first, 0.0, down),
    )


def step(coefs, center, east, west, north, south):
    mid, visc, c_east, c_west, c_up, c_down = coefs
    cells = center.shape[-1]
    upward = pltpu.roll(center, cells - 1, 1)
    downward = pltpu.roll(center, 1, 1)
    return (
        mid * center
        + visc * (north + south)
        + c_east * east
        + c_west * west
        + c_up * upward
        + c_down * downward
    )


def split3(x):
    high = x.astype(jnp.bfloat16)
    rest = x - high.astype(jnp.float32)
    middle = rest.astype(jnp.bfloat16)
    low = (rest - middle.astype(jnp.float32)).astype(jnp.bfloat16)
    return high, middle, low


def stencil_kernel(
    levels_ref,
    index_ref,
    advect_ref,
    sum_ref,
    zlo_ref,
    zhi_ref,
    face_lo_ref,
    face_hi_ref,
    corner_lo_ref,
    corner_hi_ref,
    vel_hbm,
    xlo_hbm,
    xhi_hbm,
    out_ref,
    field,
    first,
    boxed,
    sems,
):
    comp = pl.program_id(0)
    cx, cz, ny = vel_hbm.shape[1:]
    inner = pl.ds(PAD, cz)

    def copies(c):
        return (
            pltpu.make_async_copy(
                vel_hbm.at[c], field.at[c, pl.ds(2, cx), inner, :], sems.at[c, 0]
            ),
            pltpu.make_async_copy(
                xlo_hbm.at[c], field.at[c, pl.ds(0, 2), inner, :], sems.at[c, 1]
            ),
            pltpu.make_async_copy(
                xhi_hbm.at[c], field.at[c, pl.ds(cx + 2, 2), inner, :], sems.at[c, 2]
            ),
        )

    @pl.when(comp == 0)
    def _():
        for c in range(3):
            for copy in copies(c):
                copy.start()

    coefs = coefficients(levels_ref, index_ref, advect_ref)

    zlo2, zlo1 = zlo_ref[0, 0], zlo_ref[0, 1]
    zhi1, zhi2 = zhi_ref[0, 0], zhi_ref[0, 1]
    lo_before, lo_after = corner_lo_ref[0, 0:1], corner_hi_ref[0, 0:1]
    hi_before, hi_after = corner_lo_ref[0, 1:2], corner_hi_ref[0, 1:2]
    plane = lax.broadcasted_iota(jnp.int32, (cx, ny), 0)

    def edge(row, before, after, north, south):
        east = jnp.where(plane == cx - 1, after, pltpu.roll(row, cx - 1, 0))
        west = jnp.where(plane == 0, before, pltpu.roll(row, 1, 0))
        return step(coefs, row, east, west, north, south)

    edge_lo = edge(zlo1, lo_before, lo_after, zlo2, face_lo_ref[0, 0])
    edge_hi = edge(zhi1, hi_before, hi_after, face_hi_ref[0, 1], zhi2)
    for i in range(cx):
        field[comp, 2 + i, PAD - 1 : PAD, :] = zlo1[i : i + 1]
        field[comp, 2 + i, PAD + cz : PAD + cz + 1, :] = zhi1[i : i + 1]
        first[1 + i, PAD - 1 : PAD, :] = edge_lo[i : i + 1]
        first[1 + i, PAD + cz : PAD + cz + 1, :] = edge_hi[i : i + 1]
    field[comp, 1, PAD - 1 : PAD, :] = lo_before
    field[comp, 1, PAD + cz : PAD + cz + 1, :] = hi_before
    field[comp, cx + 2, PAD - 1 : PAD, :] = lo_after
    field[comp, cx + 2, PAD + cz : PAD + cz + 1, :] = hi_after

    for copy in copies(comp):
        copy.wait()

    chunk = 16

    def first_plane(p, carry):
        for k in range(cz // chunk):
            at = PAD + k * chunk
            rows = pl.ds(at, chunk)
            first[p, rows, :] = step(
                coefs,
                field[comp, p + 1, rows, :],
                field[comp, p + 2, rows, :],
                field[comp, p, rows, :],
                field[comp, p + 1, pl.ds(at - 1, chunk), :],
                field[comp, p + 1, pl.ds(at + 1, chunk), :],
            )
        return carry

    lax.fori_loop(0, cx + 2, first_plane, 0)

    sums = sum_ref[...]
    lane = lax.broadcasted_iota(jnp.int32, (cz, LANES), 1)
    row = lax.broadcasted_iota(jnp.int32, (cz, LANES), 0)
    wanted = (lane // (LANES // 2)) == ((row // STRIDE) % 2)
    out_ref[...] = jnp.zeros(out_ref.shape, jnp.float32)

    def coarse(which, box):
        total = sum(
            jnp.dot(part, sums, preferred_element_type=jnp.float32)
            for part in split3(boxed[...])
        )
        total = jnp.where(wanted, total, 0.0)
        base = box * (cz // 8 * LANES)
        for r in range(cz // 8):
            line = jnp.sum(total[8 * r : 8 * r + 8], axis=0, keepdims=True) * 0.125
            at = pl.multiple_of(base + r * LANES, LANES)
            out_ref[which : which + 1, pl.ds(at, LANES)] = line

    def box_step(box, carry):
        start = 1 + STRIDE * box
        for k in range(cz // chunk):
            rows = pl.ds(PAD + k * chunk, chunk)
            boxed[pl.ds(k * chunk, chunk), :] = (
                first[start, rows, :] + first[start + 1, rows, :]
            ) + (first[start + 2, rows, :] + first[start + 3, rows, :])
        coarse(0, box)
        for k in range(cz // chunk):
            at = PAD + k * chunk
            rows = pl.ds(at, chunk)
            total = None
            for i in range(STRIDE):
                p = start + i
                value = step(
                    coefs,
                    first[p, rows, :],
                    first[p + 1, rows, :],
                    first[p - 1, rows, :],
                    first[p, pl.ds(at - 1, chunk), :],
                    first[p, pl.ds(at + 1, chunk), :],
                )
                total = value if total is None else total + value
            boxed[pl.ds(k * chunk, chunk), :] = total
        coarse(1, box)
        return carry

    lax.fori_loop(0, cx // STRIDE, box_step, 0)


def snapshots(velocity, levels, profile_index, advect, halos):
    comps, cx, cz, ny = velocity.shape
    cols = (cx // STRIDE) * (cz // STRIDE) * (ny // STRIDE)
    half = LANES // 2
    sums = np.zeros((ny, LANES), np.float32)
    for y in range(ny):
        sums[y, y // STRIDE] = 1.0
        sums[y, half + y // STRIDE] = 1.0
    block = pl.BlockSpec((1, 2, cx, ny), lambda c: (c, 0, 0, 0))
    corner = pl.BlockSpec((1, 2, ny), lambda c: (c, 0, 0))
    whole = pl.BlockSpec(memory_space=pl.ANY)
    return pl.pallas_call(
        stencil_kernel,
        grid=(comps,),
        in_specs=[
            pl.BlockSpec(memory_space=pltpu.SMEM),
            pl.BlockSpec((1, ny), lambda c: (0, 0)),
            pl.BlockSpec((1, ny), lambda c: (0, 0)),
            pl.BlockSpec((ny, LANES), lambda c: (0, 0)),
            block,
            block,
            block,
            block,
            corner,
            corner,
            whole,
            whole,
            whole,
        ],
        out_specs=pl.BlockSpec((PAD, cols), lambda c: (0, c)),
        out_shape=jax.ShapeDtypeStruct((PAD, comps * cols), jnp.float32),
        scratch_shapes=[
            pltpu.VMEM((comps, cx + 4, cz + 2 * PAD, ny), jnp.float32),
            pltpu.VMEM((cx + 2, cz + 2 * PAD, ny), jnp.float32),
            pltpu.VMEM((cz, ny), jnp.float32),
            pltpu.SemaphoreType.DMA((comps, 3)),
        ],
        name="stencil",
    )(
        levels,
        profile_index.reshape(1, ny),
        advect.reshape(1, ny),
        jnp.asarray(sums, jnp.bfloat16),
        *halos,
    )


def gram_kernel(snap_ref, basis_ref, out_ref, acc):
    at = pl.program_id(0)

    @pl.when(at == 0)
    def _():
        acc[...] = jnp.zeros(acc.shape, jnp.float32)

    groups, width, cols = basis_ref.shape
    stack = jnp.concatenate(
        [snap_ref[...]] + [basis_ref[g] for g in range(groups)], axis=0
    )
    parts = [part.astype(jnp.float32) for part in split3(stack)]
    joined = jnp.concatenate(parts, axis=0).astype(jnp.bfloat16)
    acc[...] += lax.dot_general(
        joined, joined, (((1,), (1,)), ((), ())), preferred_element_type=jnp.float32
    )

    @pl.when(at == pl.num_programs(0) - 1)
    def _():
        n = ROWS
        total = acc[0:n, 0:n]
        cross = acc[...][0:n, n : 2 * n] + acc[n : 2 * n, 0:n]
        fine = acc[n : 2 * n, n : 2 * n] + (
            acc[...][0:n, 2 * n : 3 * n] + acc[2 * n : 3 * n, 0:n]
        )
        out_ref[...] = jnp.zeros(out_ref.shape, jnp.float32)
        out_ref[:, 0:n] = total + (cross + fine)


def gram(snap, basis, chunk=4096):
    cols = snap.shape[1]
    return pl.pallas_call(
        gram_kernel,
        grid=(cols // chunk,),
        in_specs=[
            pl.BlockSpec((PAD, chunk), lambda i: (0, i)),
            pl.BlockSpec((4, PAD, chunk), lambda i: (0, 0, i)),
        ],
        out_specs=pl.BlockSpec((ROWS, LANES), lambda i: (0, 0)),
        out_shape=jax.ShapeDtypeStruct((ROWS, LANES), jnp.float32),
        scratch_shapes=[pltpu.VMEM((3 * ROWS, 3 * ROWS), jnp.float32)],
        name="gram",
    )(snap, basis)


def ring_moves(size, stride, width):
    moves = []
    for shift in range(1, width):
        pairs = []
        for i in range(size):
            k = (i // stride) % width
            pairs.append((i, i + ((k + shift) % width - k) * stride))
        moves.append(pairs)
    return moves


def ring_parts(x, axis, size, stride, width):
    return [lax.ppermute(x, axis, pairs) for pairs in ring_moves(size, stride, width)]


def ring_sum(x, parts):
    if len(parts) == 1:
        return x + parts[0]
    one, two, three = parts
    return (x + two) + (one + three)


def lane_sum(x):
    total = x[0:8]
    for k in range(1, ROWS // 8):
        total = total + x[8 * k : 8 * k + 8]
    total = total + pltpu.roll(total, 4, 0)
    total = total + pltpu.roll(total, 2, 0)
    return total + pltpu.roll(total, 1, 0)


def spread(x):
    return jnp.concatenate([x] * (ROWS // 8), axis=0)


def factor_kernel(
    g0_ref, g1_ref, g2_ref, g3_ref, partner_ref, orient_ref, keep_ref, mix_ref, sigma_ref
):
    a = (g0_ref[...] + g2_ref[...]) + (g1_ref[...] + g3_ref[...])
    lane = lax.broadcasted_iota(jnp.int32, (ROWS, LANES), 1)
    row = lax.broadcasted_iota(jnp.int32, (ROWS, LANES), 0)
    upper = jnp.zeros((ROWS, LANES), jnp.float32)
    for j in (int(k) for k in PLACE):
        line = jnp.broadcast_to(a[j : j + 1, :], (ROWS, LANES))
        column = jnp.broadcast_to(a[:, j : j + 1], (ROWS, LANES))
        pivot = jnp.broadcast_to(line[:, j : j + 1], (ROWS, LANES))
        scale = lax.rsqrt(pivot)
        line = line * scale
        a = a - (column * scale) * line
        upper = jnp.where((row == j) & (lane >= j), line, upper)

    def turn_step(i, state):
        x, v = state
        turn = lax.rem(i, COUNT - 1)
        other = jnp.broadcast_to(partner_ref[pl.ds(turn, 1), :], (ROWS, LANES))
        sign = jnp.broadcast_to(orient_ref[pl.ds(turn, 1), :], (8, LANES))
        y = jnp.take_along_axis(x, other, axis=1)
        vy = jnp.take_along_axis(v, other, axis=1)
        contrast = lane_sum(y * y) - lane_sum(x * x)
        inner = lane_sum(x * y)
        toward = jnp.where(contrast > 0.0, -1.0, jnp.where(contrast < 0.0, 1.0, sign))
        d = jnp.abs(contrast) + jnp.sqrt(contrast * contrast + 4.0 * inner * inner)
        positive = d > 0.0
        tangent = jnp.where(
            positive, 2.0 * inner * toward / jnp.where(positive, d, 1.0), 0.0
        )
        cosine = 1.0 / jnp.sqrt(1.0 + tangent * tangent)
        sine = spread(cosine * tangent)
        cosine = spread(cosine)
        return cosine * x + sine * y, cosine * v + sine * vy

    eye = jnp.where(row == lane, 1.0, 0.0)
    x, v = lax.fori_loop(0, SWEEPS * (COUNT - 1), turn_step, (upper, eye))
    keep = jnp.broadcast_to(keep_ref[...], (ROWS, LANES))
    sigma_ref[...] = jnp.take_along_axis(jnp.sqrt(lane_sum(x * x)), keep[0:8], axis=1)
    v = jnp.take_along_axis(v, keep, axis=1)
    high = v.astype(jnp.bfloat16).astype(jnp.float32)
    low = v - high
    mix = jnp.concatenate([high, high, low, jnp.zeros((8, LANES), jnp.float32)], axis=0)
    mix_ref[...] = jnp.transpose(mix)[0:MODES].astype(jnp.bfloat16)


def factor(parts):
    partner, orient, keep = pair_tables()
    return pl.pallas_call(
        factor_kernel,
        out_shape=(
            jax.ShapeDtypeStruct((MODES, LANES), jnp.bfloat16),
            jax.ShapeDtypeStruct((8, LANES), jnp.float32),
        ),
        name="factor",
    )(*parts, jnp.asarray(partner), jnp.asarray(orient), jnp.asarray(keep))


def update_kernel(mix_ref, snap_ref, basis_ref, out_ref):
    groups = basis_ref.shape[0]
    stack = jnp.concatenate(
        [snap_ref[...]] + [basis_ref[g] for g in range(groups)], axis=0
    )
    high = stack.astype(jnp.bfloat16).astype(jnp.float32)
    low = stack - high
    zero = jnp.zeros((8, stack.shape[1]), jnp.float32)
    joined = jnp.concatenate([high, low, high, zero], axis=0).astype(jnp.bfloat16)
    out = jnp.dot(mix_ref[...], joined, preferred_element_type=jnp.float32)
    for g in range(groups):
        out_ref[g] = out[8 * g : 8 * g + 8]


def update(mix, snap, basis, chunk=4096):
    cols = snap.shape[1]
    return pl.pallas_call(
        update_kernel,
        grid=(cols // chunk,),
        in_specs=[
            pl.BlockSpec((MODES, LANES), lambda i: (0, 0)),
            pl.BlockSpec((PAD, chunk), lambda i: (0, i)),
            pl.BlockSpec((4, PAD, chunk), lambda i: (0, 0, i)),
        ],
        out_specs=pl.BlockSpec((4, PAD, chunk), lambda i: (0, 0, i)),
        out_shape=jax.ShapeDtypeStruct((4, PAD, cols), jnp.float32),
        name="update",
    )(mix, snap, basis)


def per_device(velocity, basis, levels, profile_index, advect):
    n_space, n_mode = lax.axis_size("space"), lax.axis_size("mode")
    comps, cx, cz, ny = velocity.shape
    modes_here, cols_here = basis.shape
    cols = cols_here // n_mode

    def shifted(x, axis, by):
        size = lax.axis_size(axis)
        return lax.ppermute(x, axis, [(i, (i + by) % size) for i in range(size)])

    face_lo = jnp.moveaxis(velocity[:, :, 0:2, :], 2, 1)
    face_hi = jnp.moveaxis(velocity[:, :, cz - 2 :, :], 2, 1)
    zlo = shifted(face_hi, "mode", 1)
    zhi = shifted(face_lo, "mode", -1)
    xlo = shifted(velocity[:, cx - 2 :], "space", 1)
    xhi = shifted(velocity[:, :2], "space", -1)
    corner_lo = shifted(jnp.stack([zlo[:, 1, -1], zhi[:, 0, -1]], axis=1), "space", 1)
    corner_hi = shifted(jnp.stack([zlo[:, 1, 0], zhi[:, 0, 0]], axis=1), "space", -1)

    shared = basis.reshape(modes_here, n_mode, cols).transpose(1, 0, 2)
    shared = lax.all_to_all(shared, "mode", split_axis=0, concat_axis=0, tiled=True)

    snap = snapshots(
        velocity,
        levels,
        profile_index,
        advect,
        (zlo, zhi, face_lo, face_hi, corner_lo, corner_hi, velocity, xlo, xhi),
    )
    total = gram(snap, shared)
    total = ring_sum(total, ring_parts(total, "space", n_space, 1, 2))
    total = ring_sum(total, ring_parts(total, "space", n_space, 2, 4))
    total = ring_sum(total, ring_parts(total, "space", n_space, 8, 4))
    mix, sigma = factor([total] + ring_parts(total, "mode", n_mode, 1, n_mode))
    updated = update(mix, snap, shared)
    modes = lax.all_to_all(updated, "mode", split_axis=0, concat_axis=0, tiled=True)
    modes = modes.transpose(1, 0, 2).reshape(modes_here, cols_here)
    return (modes, sigma[0, :MODES])


def solution(mesh):
    return jax.shard_map(
        per_device,
        mesh=mesh,
        in_specs=(P(None, "space", "mode", None), P("mode", "space"), P(), P(), P()),
        out_specs=(P("mode", "space"), P()),
        check_vma=False,
    )
```

```python
import functools

import jax
import jax.numpy as jnp
import numpy as np
from jax import lax
from jax.experimental import pallas as pl
from jax.experimental.pallas import tpu as pltpu
from jax.sharding import PartitionSpec as P

STRIDE = 4
MODES = 32
SWEEPS = 2
COUNT = 34
ROWS = 40
LANES = 128
PAD = 8
VMEM_SPEC = pl.BlockSpec(memory_space=pltpu.VMEM)
HBM_SPEC = pl.BlockSpec(memory_space=pltpu.HBM)


PLACE = np.array([0, 1] + list(range(PAD, PAD + MODES)))


def near(x):
    return pltpu.with_memory_space_constraint(x, pltpu.VMEM)


def far(x):
    return pltpu.with_memory_space_constraint(x, pltpu.HBM)


def pair_tables():
    rounds = COUNT - 1
    partner = np.tile(np.arange(LANES, dtype=np.int32), (ROWS, 1))
    orient = np.ones((ROWS, LANES), np.float32)
    for turn in range(rounds):
        players = [0] + [1 + (i - 1 + turn) % rounds for i in range(1, COUNT)]
        for k in range(COUNT // 2):
            lead, trail = PLACE[players[k]], PLACE[players[COUNT - 1 - k]]
            partner[turn, lead] = trail
            partner[turn, trail] = lead
            orient[turn, lead] = -1.0
    keep = np.zeros((1, LANES), np.int32)
    keep[0, :MODES] = PLACE[:MODES]
    return partner, orient, keep


def pack_kernel(vel_hbm, zfirst_ref, zlast_ref, buf, sems):
    comps, cx, cz, _ = vel_hbm.shape
    copies = []
    for c in range(comps):
        for side, at in enumerate((0, cz - PAD)):
            copies.append(
                pltpu.make_async_copy(
                    vel_hbm.at[c, :, pl.ds(at, PAD), :], buf.at[c, side], sems.at[c, side]
                )
            )
    for copy in copies:
        copy.start()
    for copy in copies:
        copy.wait()
    for c in range(comps):
        for i in range(cx):
            for k in range(2):
                row, last = (2 * c + k) * cx + i, PAD - 2 + k
                zfirst_ref[row : row + 1, :] = buf[c, 0, i, k : k + 1, :]
                zlast_ref[row : row + 1, :] = buf[c, 1, i, last : last + 1, :]


def pack(velocity):
    comps, cx, _, ny = velocity.shape
    edge = pltpu.VMEM((comps * 2 * cx, ny), jnp.float32)
    return pl.pallas_call(
        pack_kernel,
        in_specs=[HBM_SPEC],
        out_specs=[VMEM_SPEC] * 2,
        out_shape=[edge, edge],
        scratch_shapes=[
            pltpu.VMEM((comps, 2, cx, PAD, ny), jnp.float32),
            pltpu.SemaphoreType.DMA((comps, 2)),
        ],
        compiler_params=pltpu.CompilerParams(vmem_limit_bytes=4 << 20),
        name="pack",
    )(far(velocity))


def coefficients(levels_ref, index_ref, advect_ref):
    index = index_ref[...]
    visc = jnp.zeros(index.shape, jnp.float32)
    for level in range(levels_ref.shape[0]):
        visc = jnp.where(index == level, levels_ref[level], visc)
    cells = index.shape[1]
    lane = lax.broadcasted_iota(jnp.int32, index.shape, 1)
    first, last = lane == 0, lane == cells - 1
    up = jnp.where(last, visc, 0.5 * (visc + pltpu.roll(visc, cells - 1, 1)))
    down = jnp.where(first, visc, 0.5 * (visc + pltpu.roll(visc, 1, 1)))
    half = 0.5 * advect_ref[...]
    return (
        1.0 - 4.0 * visc - up - down,
        visc,
        visc - half,
        visc + half,
        jnp.where(last, 0.0, up),
        jnp.where(first, 0.0, down),
    )


def step(coefs, center, east, west, north, south):
    mid, visc, c_east, c_west, c_up, c_down = coefs
    cells = center.shape[-1]
    upward = pltpu.roll(center, cells - 1, 1)
    downward = pltpu.roll(center, 1, 1)
    return (
        mid * center
        + visc * (north + south)
        + c_east * east
        + c_west * west
        + c_up * upward
        + c_down * downward
    )


def split3(x):
    high = x.astype(jnp.bfloat16)
    rest = x - high.astype(jnp.float32)
    middle = rest.astype(jnp.bfloat16)
    low = (rest - middle.astype(jnp.float32)).astype(jnp.bfloat16)
    return high, middle, low


def stencil_kernel(
    levels_ref,
    index_ref,
    advect_ref,
    sum_ref,
    zlo_ref,
    zhi_ref,
    face_lo_ref,
    face_hi_ref,
    corner_lo_ref,
    corner_hi_ref,
    vel_hbm,
    xlo_hbm,
    xhi_hbm,
    out_ref,
    field,
    first,
    boxed,
    sems,
):
    comp = pl.program_id(0)
    cx, cz, ny = vel_hbm.shape[1:]
    inner = pl.ds(PAD, cz)

    def copies(c):
        return (
            pltpu.make_async_copy(
                vel_hbm.at[c], field.at[c, pl.ds(2, cx), inner, :], sems.at[c, 0]
            ),
            pltpu.make_async_copy(
                xlo_hbm.at[c], field.at[c, pl.ds(0, 2), inner, :], sems.at[c, 1]
            ),
            pltpu.make_async_copy(
                xhi_hbm.at[c], field.at[c, pl.ds(cx + 2, 2), inner, :], sems.at[c, 2]
            ),
        )

    @pl.when(comp == 0)
    def _():
        for c in range(3):
            for copy in copies(c):
                copy.start()

    coefs = coefficients(levels_ref, index_ref, advect_ref)

    def edge_row(ref, k):
        return ref[pl.ds(pl.multiple_of((2 * comp + k) * cx, 8), cx), :]

    zlo2, zlo1 = edge_row(zlo_ref, 0), edge_row(zlo_ref, 1)
    zhi1, zhi2 = edge_row(zhi_ref, 0), edge_row(zhi_ref, 1)
    lo_before, lo_after = corner_lo_ref[comp, 0:1], corner_hi_ref[comp, 0:1]
    hi_before, hi_after = corner_lo_ref[comp, 1:2], corner_hi_ref[comp, 1:2]
    plane = lax.broadcasted_iota(jnp.int32, (cx, ny), 0)

    def edge(row, before, after, north, south):
        east = jnp.where(plane == cx - 1, after, pltpu.roll(row, cx - 1, 0))
        west = jnp.where(plane == 0, before, pltpu.roll(row, 1, 0))
        return step(coefs, row, east, west, north, south)

    edge_lo = edge(zlo1, lo_before, lo_after, zlo2, edge_row(face_lo_ref, 0))
    edge_hi = edge(zhi1, hi_before, hi_after, edge_row(face_hi_ref, 1), zhi2)
    for i in range(cx):
        field[comp, 2 + i, PAD - 1 : PAD, :] = zlo1[i : i + 1]
        field[comp, 2 + i, PAD + cz : PAD + cz + 1, :] = zhi1[i : i + 1]
        first[1 + i, PAD - 1 : PAD, :] = edge_lo[i : i + 1]
        first[1 + i, PAD + cz : PAD + cz + 1, :] = edge_hi[i : i + 1]
    field[comp, 1, PAD - 1 : PAD, :] = lo_before
    field[comp, 1, PAD + cz : PAD + cz + 1, :] = hi_before
    field[comp, cx + 2, PAD - 1 : PAD, :] = lo_after
    field[comp, cx + 2, PAD + cz : PAD + cz + 1, :] = hi_after

    for copy in copies(comp):
        copy.wait()

    chunk = 16

    def first_plane(p, carry):
        for k in range(cz // chunk):
            at = PAD + k * chunk
            rows = pl.ds(at, chunk)
            first[p, rows, :] = step(
                coefs,
                field[comp, p + 1, rows, :],
                field[comp, p + 2, rows, :],
                field[comp, p, rows, :],
                field[comp, p + 1, pl.ds(at - 1, chunk), :],
                field[comp, p + 1, pl.ds(at + 1, chunk), :],
            )
        return carry

    lax.fori_loop(0, cx + 2, first_plane, 0)

    sums = sum_ref[...]
    lane = lax.broadcasted_iota(jnp.int32, (cz, LANES), 1)
    row = lax.broadcasted_iota(jnp.int32, (cz, LANES), 0)
    wanted = (lane // (LANES // 2)) == ((row // STRIDE) % 2)
    out_ref[...] = jnp.zeros(out_ref.shape, jnp.float32)

    def coarse(which, box):
        total = sum(
            jnp.dot(part, sums, preferred_element_type=jnp.float32)
            for part in split3(boxed[...])
        )
        total = jnp.where(wanted, total, 0.0)
        base = box * (cz // 8 * LANES)
        for r in range(cz // 8):
            line = jnp.sum(total[8 * r : 8 * r + 8], axis=0, keepdims=True) * 0.125
            at = pl.multiple_of(base + r * LANES, LANES)
            out_ref[which : which + 1, pl.ds(at, LANES)] = line

    def box_step(box, carry):
        start = 1 + STRIDE * box
        for k in range(cz // chunk):
            rows = pl.ds(PAD + k * chunk, chunk)
            boxed[pl.ds(k * chunk, chunk), :] = (
                first[start, rows, :] + first[start + 1, rows, :]
            ) + (first[start + 2, rows, :] + first[start + 3, rows, :])
        coarse(0, box)
        for k in range(cz // chunk):
            at = PAD + k * chunk
            rows = pl.ds(at, chunk)
            total = None
            for i in range(STRIDE):
                p = start + i
                value = step(
                    coefs,
                    first[p, rows, :],
                    first[p + 1, rows, :],
                    first[p - 1, rows, :],
                    first[p, pl.ds(at - 1, chunk), :],
                    first[p, pl.ds(at + 1, chunk), :],
                )
                total = value if total is None else total + value
            boxed[pl.ds(k * chunk, chunk), :] = total
        coarse(1, box)
        return carry

    lax.fori_loop(0, cx // STRIDE, box_step, 0)


def snapshots(velocity, levels, profile_index, advect, halos):
    comps, cx, cz, ny = velocity.shape
    cols = (cx // STRIDE) * (cz // STRIDE) * (ny // STRIDE)
    half = LANES // 2
    sums = np.zeros((ny, LANES), np.float32)
    for y in range(ny):
        sums[y, y // STRIDE] = 1.0
        sums[y, half + y // STRIDE] = 1.0
    return pl.pallas_call(
        stencil_kernel,
        grid=(comps,),
        in_specs=[
            pl.BlockSpec(memory_space=pltpu.SMEM),
            pl.BlockSpec((1, ny), lambda c: (0, 0)),
            pl.BlockSpec((1, ny), lambda c: (0, 0)),
            pl.BlockSpec((ny, LANES), lambda c: (0, 0)),
            *[VMEM_SPEC] * 6,
            HBM_SPEC,
            VMEM_SPEC,
            VMEM_SPEC,
        ],
        out_specs=pl.BlockSpec((PAD, cols), lambda c: (0, c)),
        out_shape=pltpu.HBM((PAD, comps * cols), jnp.float32),
        scratch_shapes=[
            pltpu.VMEM((comps, cx + 4, cz + 2 * PAD, ny), jnp.float32),
            pltpu.VMEM((cx + 2, cz + 2 * PAD, ny), jnp.float32),
            pltpu.VMEM((cz, ny), jnp.float32),
            pltpu.SemaphoreType.DMA((comps, 3)),
        ],
        compiler_params=pltpu.CompilerParams(vmem_limit_bytes=20 << 20),
        name="stencil",
    )(
        levels,
        profile_index.reshape(1, ny),
        advect.reshape(1, ny),
        jnp.asarray(sums, jnp.bfloat16),
        *[near(x) for x in halos[:6]],
        far(halos[6]),
        *[near(x) for x in halos[7:]],
    )


def stack_rows(snap, basis_ref, at):
    groups = basis_ref.shape[0]
    return jnp.concatenate(
        [snap] + [basis_ref[g, :, at] for g in range(groups)], axis=0
    )


def gram_kernel(snap_ref, basis_ref, out_ref, acc, *, chunk):
    step_at = pl.program_id(0)
    width = snap_ref.shape[1]

    @pl.when(step_at == 0)
    def _():
        acc[...] = jnp.zeros(acc.shape, jnp.float32)

    for i in range(width // chunk):
        at = pl.ds(pl.multiple_of(step_at * width + i * chunk, chunk), chunk)
        snap = snap_ref[:, i * chunk : (i + 1) * chunk]
        parts = split3(stack_rows(snap, basis_ref, at))
        joined = jnp.concatenate([part.astype(jnp.float32) for part in parts], axis=0)
        joined = joined.astype(jnp.bfloat16)
        acc[...] += lax.dot_general(
            joined, joined, (((1,), (1,)), ((), ())), preferred_element_type=jnp.float32
        )

    @pl.when(step_at == pl.num_programs(0) - 1)
    def _():
        n = ROWS
        total = acc[0:n, 0:n]
        cross = acc[0:n, n : 2 * n] + acc[n : 2 * n, 0:n]
        fine = acc[n : 2 * n, n : 2 * n] + (
            acc[0:n, 2 * n : 3 * n] + acc[2 * n : 3 * n, 0:n]
        )
        out_ref[...] = jnp.zeros(out_ref.shape, jnp.float32)
        out_ref[:, 0:n] = total + (cross + fine)


def gram(snap, basis, width=4096, chunk=2048):
    return pl.pallas_call(
        functools.partial(gram_kernel, chunk=chunk),
        grid=(snap.shape[1] // width,),
        in_specs=[pl.BlockSpec((PAD, width), lambda i: (0, i)), VMEM_SPEC],
        out_specs=VMEM_SPEC,
        out_shape=pltpu.VMEM((ROWS, LANES), jnp.float32),
        scratch_shapes=[pltpu.VMEM((3 * ROWS, 3 * ROWS), jnp.float32)],
        compiler_params=pltpu.CompilerParams(vmem_limit_bytes=12 << 20),
        name="gram",
    )(far(snap), near(basis))


def ring_moves(size, stride, width):
    moves = []
    for shift in range(1, width):
        pairs = []
        for i in range(size):
            k = (i // stride) % width
            pairs.append((i, i + ((k + shift) % width - k) * stride))
        moves.append(pairs)
    return moves


def ring_parts(x, axis, size, stride, width):
    return [lax.ppermute(x, axis, pairs) for pairs in ring_moves(size, stride, width)]


def ring_sum(x, parts):
    if len(parts) == 1:
        return x + parts[0]
    one, two, three = parts
    return (x + two) + (one + three)


def lane_sum(x):
    total = x[0:8]
    for k in range(1, ROWS // 8):
        total = total + x[8 * k : 8 * k + 8]
    total = total + pltpu.roll(total, 4, 0)
    total = total + pltpu.roll(total, 2, 0)
    return total + pltpu.roll(total, 1, 0)


def spread(x):
    return jnp.concatenate([x] * (ROWS // 8), axis=0)


def factor_kernel(
    g0_ref, g1_ref, g2_ref, g3_ref, partner_ref, orient_ref, keep_ref, mix_ref, sigma_ref
):
    a = (g0_ref[...] + g2_ref[...]) + (g1_ref[...] + g3_ref[...])
    lane = lax.broadcasted_iota(jnp.int32, (ROWS, LANES), 1)
    row = lax.broadcasted_iota(jnp.int32, (ROWS, LANES), 0)
    upper = jnp.zeros((ROWS, LANES), jnp.float32)
    for j in (int(k) for k in PLACE):
        line = jnp.broadcast_to(a[j : j + 1, :], (ROWS, LANES))
        column = jnp.broadcast_to(a[:, j : j + 1], (ROWS, LANES))
        pivot = jnp.broadcast_to(line[:, j : j + 1], (ROWS, LANES))
        scale = lax.rsqrt(pivot)
        line = line * scale
        a = a - (column * scale) * line
        upper = jnp.where((row == j) & (lane >= j), line, upper)

    def turn_step(i, state):
        x, v = state
        turn = lax.rem(i, COUNT - 1)
        other = jnp.broadcast_to(partner_ref[pl.ds(turn, 1), :], (ROWS, LANES))
        sign = jnp.broadcast_to(orient_ref[pl.ds(turn, 1), :], (8, LANES))
        y = jnp.take_along_axis(x, other, axis=1)
        vy = jnp.take_along_axis(v, other, axis=1)
        contrast = lane_sum(y * y) - lane_sum(x * x)
        inner = lane_sum(x * y)
        toward = jnp.where(contrast > 0.0, -1.0, jnp.where(contrast < 0.0, 1.0, sign))
        d = jnp.abs(contrast) + jnp.sqrt(contrast * contrast + 4.0 * inner * inner)
        positive = d > 0.0
        tangent = jnp.where(
            positive, 2.0 * inner * toward / jnp.where(positive, d, 1.0), 0.0
        )
        cosine = 1.0 / jnp.sqrt(1.0 + tangent * tangent)
        sine = spread(cosine * tangent)
        cosine = spread(cosine)
        return cosine * x + sine * y, cosine * v + sine * vy

    eye = jnp.where(row == lane, 1.0, 0.0)
    x, v = lax.fori_loop(0, SWEEPS * (COUNT - 1), turn_step, (upper, eye))
    keep = jnp.broadcast_to(keep_ref[...], (ROWS, LANES))
    sigma_ref[...] = jnp.take_along_axis(jnp.sqrt(lane_sum(x * x)), keep[0:8], axis=1)
    v = jnp.take_along_axis(v, keep, axis=1)
    high = v.astype(jnp.bfloat16).astype(jnp.float32)
    low = v - high
    mix = jnp.concatenate([high, high, low, jnp.zeros((8, LANES), jnp.float32)], axis=0)
    mix_ref[...] = jnp.transpose(mix)[0:MODES].astype(jnp.bfloat16)


def factor(parts):
    tables = [near(jnp.asarray(table)) for table in pair_tables()]
    return pl.pallas_call(
        factor_kernel,
        in_specs=[VMEM_SPEC] * 7,
        out_specs=(VMEM_SPEC, VMEM_SPEC),
        out_shape=(
            pltpu.VMEM((MODES, LANES), jnp.bfloat16),
            pltpu.VMEM((8, LANES), jnp.float32),
        ),
        compiler_params=pltpu.CompilerParams(vmem_limit_bytes=4 << 20),
        name="factor",
    )(*[near(x) for x in parts], *tables)


def update_kernel(mix_ref, snap_ref, basis_ref, out_ref, *, chunk):
    groups, _, width = out_ref.shape
    mix = mix_ref[...]
    base = pl.program_id(0) * width
    for i in range(width // chunk):
        at = pl.ds(pl.multiple_of(base + i * chunk, chunk), chunk)
        snap = snap_ref[:, i * chunk : (i + 1) * chunk]
        stack = stack_rows(snap, basis_ref, at)
        high = stack.astype(jnp.bfloat16).astype(jnp.float32)
        zero = jnp.zeros((8, chunk), jnp.float32)
        joined = jnp.concatenate([high, stack - high, high, zero], axis=0)
        out = jnp.dot(mix, joined.astype(jnp.bfloat16), preferred_element_type=jnp.float32)
        for g in range(groups):
            out_ref[g, :, i * chunk : (i + 1) * chunk] = out[8 * g : 8 * g + 8]


def update(mix, snap, basis, width=4096, chunk=1024):
    cols = snap.shape[1]
    return pl.pallas_call(
        functools.partial(update_kernel, chunk=chunk),
        grid=(cols // width,),
        in_specs=[VMEM_SPEC, pl.BlockSpec((PAD, width), lambda i: (0, i)), VMEM_SPEC],
        out_specs=pl.BlockSpec((4, PAD, width), lambda i: (0, 0, i)),
        out_shape=pltpu.HBM((4, PAD, cols), jnp.float32),
        compiler_params=pltpu.CompilerParams(vmem_limit_bytes=8 << 20),
        name="update",
    )(near(mix), far(snap), near(basis))


def program(velocity, basis, levels, profile_index, advect):
    n_space, n_mode = lax.axis_size("space"), lax.axis_size("mode")
    comps, cx, _, ny = velocity.shape
    modes_here, cols_here = basis.shape
    cols = cols_here // n_mode

    def shifted(x, axis, by):
        size = lax.axis_size(axis)
        return lax.ppermute(x, axis, [(i, (i + by) % size) for i in range(size)])

    face_lo, face_hi = pack(velocity)
    zlo = shifted(face_hi, "mode", 1)
    zhi = shifted(face_lo, "mode", -1)
    xlo = shifted(velocity[:, cx - 2 :], "space", 1)
    xhi = shifted(velocity[:, :2], "space", -1)
    near_lo = zlo.reshape(comps, 2, cx, ny)[:, 1]
    near_hi = zhi.reshape(comps, 2, cx, ny)[:, 0]
    corner_lo = jnp.stack([near_lo[:, -1], near_hi[:, -1]], axis=1)
    corner_hi = jnp.stack([near_lo[:, 0], near_hi[:, 0]], axis=1)
    corner_lo = shifted(corner_lo, "space", 1)
    corner_hi = shifted(corner_hi, "space", -1)
    shared = basis.reshape(modes_here, n_mode, cols).transpose(1, 0, 2)
    shared = lax.all_to_all(shared, "mode", split_axis=0, concat_axis=0, tiled=True)

    snap = snapshots(
        velocity,
        levels,
        profile_index,
        advect,
        (zlo, zhi, face_lo, face_hi, corner_lo, corner_hi, velocity, xlo, xhi),
    )
    total = gram(snap, shared)
    total = ring_sum(total, ring_parts(total, "space", n_space, 1, 2))
    total = ring_sum(total, ring_parts(total, "space", n_space, 2, 4))
    total = ring_sum(total, ring_parts(total, "space", n_space, 8, 4))
    mix, sigma = factor([total] + ring_parts(total, "mode", n_mode, 1, n_mode))
    updated = update(mix, snap, shared)
    modes = lax.all_to_all(updated, "mode", split_axis=0, concat_axis=0, tiled=True)
    modes = modes.transpose(1, 0, 2).reshape(modes_here, cols_here)
    return (modes, sigma[0, :MODES])


def solution(mesh):
    return jax.shard_map(
        program,
        mesh=mesh,
        in_specs=(P(None, "space", "mode", None), P("mode", "space"), P(), P(), P()),
        out_specs=(P("mode", "space"), P()),
        check_vma=False,
    )
```

```python
import functools

import jax
import jax.numpy as jnp
import numpy as np
from jax import lax
from jax.experimental import pallas as pl
from jax.experimental.pallas import tpu as pltpu
from jax.sharding import PartitionSpec as P

STRIDE = 4
MODES = 32
SWEEPS = 2
COUNT = 34
ROWS = 40
LANES = 128
PAD = 8
VMEM_SPEC = pl.BlockSpec(memory_space=pltpu.VMEM)
HBM_SPEC = pl.BlockSpec(memory_space=pltpu.HBM)
SMEM_SPEC = pl.BlockSpec(memory_space=pltpu.SMEM)


SHARED = 8192
FOLD = SHARED // 4

PLACE = np.array([0, 1] + list(range(PAD, PAD + MODES)))


def near(x):
    return pltpu.with_memory_space_constraint(x, pltpu.VMEM)


def far(x):
    return pltpu.with_memory_space_constraint(x, pltpu.HBM)


def pair_tables():
    rounds = COUNT - 1
    partner = np.tile(np.arange(LANES, dtype=np.int32), (ROWS, 1))
    orient = np.ones((ROWS, LANES), np.float32)
    for turn in range(rounds):
        players = [0] + [1 + (i - 1 + turn) % rounds for i in range(1, COUNT)]
        for k in range(COUNT // 2):
            lead, trail = PLACE[players[k]], PLACE[players[COUNT - 1 - k]]
            partner[turn, lead] = trail
            partner[turn, trail] = lead
            orient[turn, lead] = -1.0
    keep = np.zeros((1, LANES), np.int32)
    keep[0, :MODES] = PLACE[:MODES]
    return partner, orient, keep


def pack_kernel(
    here_ref,
    vel_hbm,
    basis_hbm,
    zfirst_ref,
    zlast_ref,
    xfirst_ref,
    xlast_ref,
    mine_ref,
    next_ref,
    far_ref,
    prev_ref,
    buf,
    edge_sems,
    face_sems,
    block_sems,
):
    comps, cx, cz, _ = vel_hbm.shape
    cols = mine_ref.shape[1]
    edges, rest = [], []
    for c in range(comps):
        for side, at in enumerate((0, cz - PAD)):
            source = vel_hbm.at[c, :, pl.ds(at, PAD), :]
            edges.append(pltpu.make_async_copy(source, buf.at[c, side], edge_sems.at[c, side]))
        for side, (at, ref) in enumerate(((0, xfirst_ref), (cx - 2, xlast_ref))):
            source = vel_hbm.at[c, pl.ds(at, 2)]
            rest.append(pltpu.make_async_copy(source, ref.at[c], face_sems.at[c, side]))
    for k, ref in enumerate((mine_ref, next_ref, far_ref, prev_ref)):
        at = pl.multiple_of(lax.rem(here_ref[0] + k, 4) * cols, LANES)
        source = basis_hbm.at[:, pl.ds(at, cols)]
        rest.append(pltpu.make_async_copy(source, ref, block_sems.at[k]))
    for copy in edges + rest:
        copy.start()
    for copy in edges:
        copy.wait()
    for c in range(comps):
        for i in range(cx):
            for k in range(2):
                row, last = (2 * c + k) * cx + i, PAD - 2 + k
                zfirst_ref[row : row + 1, :] = buf[c, 0, i, k : k + 1, :]
                zlast_ref[row : row + 1, :] = buf[c, 1, i, last : last + 1, :]
    for copy in rest:
        copy.wait()


def pack(here, velocity, basis):
    comps, cx, cz, ny = velocity.shape
    edge = pltpu.VMEM((comps * 2 * cx, ny), jnp.float32)
    face = pltpu.VMEM((comps, 2, cz, ny), jnp.float32)
    block = pltpu.VMEM((PAD, basis.shape[1] // 4), jnp.float32)
    return pl.pallas_call(
        pack_kernel,
        in_specs=[SMEM_SPEC, HBM_SPEC, HBM_SPEC],
        out_specs=[VMEM_SPEC] * 8,
        out_shape=[edge, edge, face, face] + [block] * 4,
        scratch_shapes=[
            pltpu.VMEM((comps, 2, cx, PAD, ny), jnp.float32),
            pltpu.SemaphoreType.DMA((comps, 2)),
            pltpu.SemaphoreType.DMA((comps, 2)),
            pltpu.SemaphoreType.DMA((4,)),
        ],
        compiler_params=pltpu.CompilerParams(vmem_limit_bytes=4 << 20),
        name="pack",
    )(here, far(velocity), far(basis))


def coefficients(levels_ref, index_ref, advect_ref):
    index = index_ref[...]
    visc = jnp.zeros(index.shape, jnp.float32)
    for level in range(levels_ref.shape[0]):
        visc = jnp.where(index == level, levels_ref[level], visc)
    cells = index.shape[1]
    lane = lax.broadcasted_iota(jnp.int32, index.shape, 1)
    first, last = lane == 0, lane == cells - 1
    up = jnp.where(last, visc, 0.5 * (visc + pltpu.roll(visc, cells - 1, 1)))
    down = jnp.where(first, visc, 0.5 * (visc + pltpu.roll(visc, 1, 1)))
    half = 0.5 * advect_ref[...]
    return (
        1.0 - 4.0 * visc - up - down,
        visc,
        visc - half,
        visc + half,
        jnp.where(last, 0.0, up),
        jnp.where(first, 0.0, down),
    )


def step(coefs, center, east, west, north, south):
    mid, visc, c_east, c_west, c_up, c_down = coefs
    cells = center.shape[-1]
    upward = pltpu.roll(center, cells - 1, 1)
    downward = pltpu.roll(center, 1, 1)
    return (
        mid * center
        + visc * (north + south)
        + c_east * east
        + c_west * west
        + c_up * upward
        + c_down * downward
    )


def split3(x):
    high = x.astype(jnp.bfloat16)
    rest = x - high.astype(jnp.float32)
    middle = rest.astype(jnp.bfloat16)
    low = (rest - middle.astype(jnp.float32)).astype(jnp.bfloat16)
    return high, middle, low


def offer_copies(here, basis_hbm, refs, sems):
    cols = basis_hbm.shape[1] // 4
    copies = []
    for side, (ref, skip) in enumerate(zip(refs, (2, 0, 3))):
        for k in range(3):
            at = pl.multiple_of(lax.rem(here + skip + k, 4) * cols, LANES)
            source = basis_hbm.at[:, pl.ds(at, SHARED)]
            target = ref.at[:, pl.ds(k * SHARED, SHARED)]
            copies.append(pltpu.make_async_copy(source, target, sems.at[side, k]))
    return copies


def stencil_kernel(
    levels_ref,
    index_ref,
    advect_ref,
    sum_ref,
    zlo_ref,
    zhi_ref,
    face_lo_ref,
    face_hi_ref,
    corner_lo_ref,
    corner_hi_ref,
    here_ref,
    basis_hbm,
    vel_hbm,
    xlo_hbm,
    xhi_hbm,
    out_ref,
    plus_ref,
    minus_ref,
    over_ref,
    field,
    first,
    boxed,
    sems,
    offer_sems,
):
    comp = pl.program_id(0)
    offer_refs = (plus_ref, minus_ref, over_ref)
    offers = offer_copies(here_ref[0], basis_hbm, offer_refs, offer_sems)
    cx, cz, ny = vel_hbm.shape[1:]
    inner = pl.ds(PAD, cz)

    def copies(c):
        return (
            pltpu.make_async_copy(
                vel_hbm.at[c], field.at[c, pl.ds(2, cx), inner, :], sems.at[c, 0]
            ),
            pltpu.make_async_copy(
                xlo_hbm.at[c], field.at[c, pl.ds(0, 2), inner, :], sems.at[c, 1]
            ),
            pltpu.make_async_copy(
                xhi_hbm.at[c], field.at[c, pl.ds(cx + 2, 2), inner, :], sems.at[c, 2]
            ),
        )

    @pl.when(comp == 0)
    def _():
        for c in range(3):
            for copy in copies(c):
                copy.start()
        for copy in offers:
            copy.start()

    @pl.when(comp == pl.num_programs(0) - 1)
    def _():
        for copy in offers:
            copy.wait()

    coefs = coefficients(levels_ref, index_ref, advect_ref)

    def edge_row(ref, k):
        return ref[pl.ds(pl.multiple_of((2 * comp + k) * cx, 8), cx), :]

    zlo2, zlo1 = edge_row(zlo_ref, 0), edge_row(zlo_ref, 1)
    zhi1, zhi2 = edge_row(zhi_ref, 0), edge_row(zhi_ref, 1)
    lo_before, lo_after = corner_lo_ref[comp, 0:1], corner_hi_ref[comp, 0:1]
    hi_before, hi_after = corner_lo_ref[comp, 1:2], corner_hi_ref[comp, 1:2]
    plane = lax.broadcasted_iota(jnp.int32, (cx, ny), 0)

    def edge(row, before, after, north, south):
        east = jnp.where(plane == cx - 1, after, pltpu.roll(row, cx - 1, 0))
        west = jnp.where(plane == 0, before, pltpu.roll(row, 1, 0))
        return step(coefs, row, east, west, north, south)

    edge_lo = edge(zlo1, lo_before, lo_after, zlo2, edge_row(face_lo_ref, 0))
    edge_hi = edge(zhi1, hi_before, hi_after, edge_row(face_hi_ref, 1), zhi2)
    for i in range(cx):
        field[comp, 2 + i, PAD - 1 : PAD, :] = zlo1[i : i + 1]
        field[comp, 2 + i, PAD + cz : PAD + cz + 1, :] = zhi1[i : i + 1]
        first[1 + i, PAD - 1 : PAD, :] = edge_lo[i : i + 1]
        first[1 + i, PAD + cz : PAD + cz + 1, :] = edge_hi[i : i + 1]
    field[comp, 1, PAD - 1 : PAD, :] = lo_before
    field[comp, 1, PAD + cz : PAD + cz + 1, :] = hi_before
    field[comp, cx + 2, PAD - 1 : PAD, :] = lo_after
    field[comp, cx + 2, PAD + cz : PAD + cz + 1, :] = hi_after

    for copy in copies(comp):
        copy.wait()

    chunk = 16

    def first_plane(p, carry):
        for k in range(cz // chunk):
            at = PAD + k * chunk
            rows = pl.ds(at, chunk)
            first[p, rows, :] = step(
                coefs,
                field[comp, p + 1, rows, :],
                field[comp, p + 2, rows, :],
                field[comp, p, rows, :],
                field[comp, p + 1, pl.ds(at - 1, chunk), :],
                field[comp, p + 1, pl.ds(at + 1, chunk), :],
            )
        return carry

    lax.fori_loop(0, cx + 2, first_plane, 0)

    sums = sum_ref[...]
    lane = lax.broadcasted_iota(jnp.int32, (cz, LANES), 1)
    row = lax.broadcasted_iota(jnp.int32, (cz, LANES), 0)
    wanted = (lane // (LANES // 2)) == ((row // STRIDE) % 2)
    part = out_ref.shape[1] // vel_hbm.shape[0]
    offset = pl.multiple_of(comp * part, LANES)
    out_ref[:, pl.ds(offset, part)] = jnp.zeros((PAD, part), jnp.float32)

    def coarse(which, box):
        total = sum(
            jnp.dot(part, sums, preferred_element_type=jnp.float32)
            for part in split3(boxed[...])
        )
        total = jnp.where(wanted, total, 0.0)
        base = offset + box * (cz // 8 * LANES)
        for r in range(cz // 8):
            line = jnp.sum(total[8 * r : 8 * r + 8], axis=0, keepdims=True) * 0.125
            at = pl.multiple_of(base + r * LANES, LANES)
            out_ref[which : which + 1, pl.ds(at, LANES)] = line

            @pl.when(comp == 0)
            def _(line=line, r=r):
                group = which * (SHARED // LANES // 8) + box * (cz // 64) + r // 8
                spot = pl.ds(pl.multiple_of(3 * SHARED + group * LANES, LANES), LANES)
                for ref in offer_refs:
                    ref[r % 8 : r % 8 + 1, spot] = line

    def box_step(box, carry):
        start = 1 + STRIDE * box
        for k in range(cz // chunk):
            rows = pl.ds(PAD + k * chunk, chunk)
            boxed[pl.ds(k * chunk, chunk), :] = (
                first[start, rows, :] + first[start + 1, rows, :]
            ) + (first[start + 2, rows, :] + first[start + 3, rows, :])
        coarse(0, box)
        for k in range(cz // chunk):
            at = PAD + k * chunk
            rows = pl.ds(at, chunk)
            total = None
            for i in range(STRIDE):
                p = start + i
                value = step(
                    coefs,
                    first[p, rows, :],
                    first[p + 1, rows, :],
                    first[p - 1, rows, :],
                    first[p, pl.ds(at - 1, chunk), :],
                    first[p, pl.ds(at + 1, chunk), :],
                )
                total = value if total is None else total + value
            boxed[pl.ds(k * chunk, chunk), :] = total
        coarse(1, box)
        return carry

    lax.fori_loop(0, cx // STRIDE, box_step, 0)


def snapshots(velocity, levels, profile_index, advect, here, basis, halos):
    comps, cx, cz, ny = velocity.shape
    cols = (cx // STRIDE) * (cz // STRIDE) * (ny // STRIDE)
    half = LANES // 2
    sums = np.zeros((ny, LANES), np.float32)
    for y in range(ny):
        sums[y, y // STRIDE] = 1.0
        sums[y, half + y // STRIDE] = 1.0
    return pl.pallas_call(
        stencil_kernel,
        grid=(comps,),
        in_specs=[
            SMEM_SPEC,
            pl.BlockSpec((1, ny), lambda c: (0, 0)),
            pl.BlockSpec((1, ny), lambda c: (0, 0)),
            pl.BlockSpec((ny, LANES), lambda c: (0, 0)),
            *[VMEM_SPEC] * 6,
            SMEM_SPEC,
            HBM_SPEC,
            HBM_SPEC,
            VMEM_SPEC,
            VMEM_SPEC,
        ],
        out_specs=[VMEM_SPEC] * 4,
        out_shape=[pltpu.VMEM((PAD, comps * cols), jnp.float32)]
        + [pltpu.VMEM((PAD, 3 * SHARED + FOLD), jnp.float32)] * 3,
        scratch_shapes=[
            pltpu.VMEM((comps, cx + 4, cz + 2 * PAD, ny), jnp.float32),
            pltpu.VMEM((cx + 2, cz + 2 * PAD, ny), jnp.float32),
            pltpu.VMEM((cz, ny), jnp.float32),
            pltpu.SemaphoreType.DMA((comps, 3)),
            pltpu.SemaphoreType.DMA((3, 3)),
        ],
        compiler_params=pltpu.CompilerParams(vmem_limit_bytes=20 << 20),
        name="stencil",
    )(
        levels,
        profile_index.reshape(1, ny),
        advect.reshape(1, ny),
        jnp.asarray(sums, jnp.bfloat16),
        *[near(x) for x in halos[:6]],
        here,
        far(basis),
        far(halos[6]),
        *[near(x) for x in halos[7:]],
    )


def stacked(refs, at):
    return jnp.concatenate([ref[:, at] for ref in refs], axis=0)


def gram_kernel(here_ref, *refs, chunk):
    stack_refs, out_ref = refs[:-1], refs[-1]
    here = here_ref[0]
    n, acc = ROWS, None
    for start in range(0, stack_refs[0].shape[1], chunk):
        stack = stacked(stack_refs, slice(start, start + chunk))
        high = stack.astype(jnp.bfloat16).astype(jnp.float32)
        joined = jnp.concatenate([high, stack - high], axis=0).astype(jnp.bfloat16)
        part = lax.dot_general(
            joined, joined, (((1,), (1,)), ((), ())), preferred_element_type=jnp.float32
        )
        acc = part if acc is None else acc + part
    cross = acc[0:n, n : 2 * n] + acc[n : 2 * n, 0:n]
    total = acc[0:n, 0:n] + (cross + acc[n : 2 * n, n : 2 * n])
    total = jnp.concatenate([total, jnp.zeros((n, LANES - n), jnp.float32)], axis=1)
    lane = lax.broadcasted_iota(jnp.int32, (n, LANES), 1)
    turned = PAD + lax.rem(lane - PAD + MODES - PAD * here + MODES, MODES)
    inside = (lane >= PAD) & (lane < n)
    total = jnp.take_along_axis(total, jnp.where(inside, turned, lane), axis=1)
    out_ref[0:PAD, :] = total[0:PAD]
    for g in range(4):
        at = pl.multiple_of(PAD + PAD * lax.rem(here + g, 4), PAD)
        out_ref[pl.ds(at, PAD), :] = total[PAD + PAD * g : 2 * PAD + PAD * g]


def gram(here, stack, chunk=2048):
    return pl.pallas_call(
        functools.partial(gram_kernel, chunk=chunk),
        in_specs=[SMEM_SPEC] + [VMEM_SPEC] * 5,
        out_specs=VMEM_SPEC,
        out_shape=pltpu.VMEM((ROWS, LANES), jnp.float32),
        compiler_params=pltpu.CompilerParams(vmem_limit_bytes=8 << 20),
        name="gram",
    )(here, *[near(x) for x in stack])


def ring_moves(size, stride, width):
    moves = []
    for shift in range(1, width):
        pairs = []
        for i in range(size):
            k = (i // stride) % width
            pairs.append((i, i + ((k + shift) % width - k) * stride))
        moves.append(pairs)
    return moves


def ring_parts(x, axis, size, stride, width):
    return [lax.ppermute(x, axis, pairs) for pairs in ring_moves(size, stride, width)]


def ring_sum(x, parts):
    if len(parts) == 1:
        return x + parts[0]
    one, two, three = parts
    return (x + two) + (one + three)


def lane_sum(x):
    total = x[0:8]
    for k in range(1, ROWS // 8):
        total = total + x[8 * k : 8 * k + 8]
    total = total + pltpu.roll(total, 4, 0)
    total = total + pltpu.roll(total, 2, 0)
    return total + pltpu.roll(total, 1, 0)


def spread(x):
    return jnp.concatenate([x] * (ROWS // 8), axis=0)


def factor_kernel(
    g0_ref, g1_ref, g2_ref, g3_ref, partner_ref, orient_ref, keep_ref, mix_ref, sigma_ref
):
    a = (g0_ref[...] + g2_ref[...]) + (g1_ref[...] + g3_ref[...])
    lane = lax.broadcasted_iota(jnp.int32, (ROWS, LANES), 1)
    row = lax.broadcasted_iota(jnp.int32, (ROWS, LANES), 0)
    upper = jnp.zeros((ROWS, LANES), jnp.float32)
    for j in (int(k) for k in PLACE):
        line = jnp.broadcast_to(a[j : j + 1, :], (ROWS, LANES))
        column = jnp.broadcast_to(a[:, j : j + 1], (ROWS, LANES))
        pivot = jnp.broadcast_to(line[:, j : j + 1], (ROWS, LANES))
        scale = lax.rsqrt(pivot)
        line = line * scale
        a = a - (column * scale) * line
        upper = jnp.where((row == j) & (lane >= j), line, upper)

    def turn_step(i, state):
        x, v = state
        turn = lax.rem(i, COUNT - 1)
        other = jnp.broadcast_to(partner_ref[pl.ds(turn, 1), :], (ROWS, LANES))
        sign = jnp.broadcast_to(orient_ref[pl.ds(turn, 1), :], (8, LANES))
        y = jnp.take_along_axis(x, other, axis=1)
        vy = jnp.take_along_axis(v, other, axis=1)
        contrast = lane_sum(y * y) - lane_sum(x * x)
        inner = lane_sum(x * y)
        toward = jnp.where(contrast > 0.0, -1.0, jnp.where(contrast < 0.0, 1.0, sign))
        d = jnp.abs(contrast) + jnp.sqrt(contrast * contrast + 4.0 * inner * inner)
        positive = d > 0.0
        tangent = jnp.where(
            positive, 2.0 * inner * toward / jnp.where(positive, d, 1.0), 0.0
        )
        cosine = 1.0 / jnp.sqrt(1.0 + tangent * tangent)
        sine = spread(cosine * tangent)
        cosine = spread(cosine)
        return cosine * x + sine * y, cosine * v + sine * vy

    eye = jnp.where(row == lane, 1.0, 0.0)
    x, v = lax.fori_loop(0, SWEEPS * (COUNT - 1), turn_step, (upper, eye))
    keep = jnp.broadcast_to(keep_ref[...], (ROWS, LANES))
    sigma_ref[...] = jnp.take_along_axis(jnp.sqrt(lane_sum(x * x)), keep[0:8], axis=1)
    v = jnp.take_along_axis(v, keep, axis=1)
    high = v.astype(jnp.bfloat16).astype(jnp.float32)
    low = v - high
    mix = jnp.concatenate([high, high, low, jnp.zeros((8, LANES), jnp.float32)], axis=0)
    mix_ref[...] = jnp.transpose(mix)[0:MODES]


def factor(parts):
    tables = [near(jnp.asarray(table)) for table in pair_tables()]
    return pl.pallas_call(
        factor_kernel,
        in_specs=[VMEM_SPEC] * 7,
        out_specs=(VMEM_SPEC, VMEM_SPEC),
        out_shape=(
            pltpu.VMEM((MODES, LANES), jnp.float32),
            pltpu.VMEM((8, LANES), jnp.float32),
        ),
        compiler_params=pltpu.CompilerParams(vmem_limit_bytes=4 << 20),
        name="factor",
    )(*[near(x) for x in parts], *tables)


def turned_mix(mix, here):
    lane = lax.broadcasted_iota(jnp.int32, mix.shape, 1)
    inside = lax.rem(lane, ROWS)
    turned = lane - inside + PAD + lax.rem(inside + (MODES - PAD) + PAD * here, MODES)
    source = jnp.where((inside < PAD) | (lane >= 3 * ROWS), lane, turned)
    return jnp.take_along_axis(mix, source, axis=1).astype(jnp.bfloat16)


def mix_rows(mix_ref, here, g):
    at = pl.multiple_of(PAD * lax.rem(here + g, 4), PAD)
    return mix_ref[pl.ds(at, PAD), :]


def mixed(mix, stack):
    high = stack.astype(jnp.bfloat16).astype(jnp.float32)
    zero = jnp.zeros((8, stack.shape[1]), jnp.float32)
    joined = jnp.concatenate([high, stack - high, high, zero], axis=0)
    return jnp.dot(mix, joined.astype(jnp.bfloat16), preferred_element_type=jnp.float32)


def update_kernel(here_ref, mix_ref, *refs, chunk):
    stack_refs, out_refs = refs[:5], refs[5:]
    here = here_ref[0]
    mix = jnp.concatenate([mix_rows(mix_ref, here, g) for g in range(4)], axis=0)
    mix = turned_mix(mix, here)
    for start in range(0, out_refs[0].shape[1], chunk):
        first = SHARED + start
        out = mixed(mix, stacked(stack_refs, slice(first, first + chunk)))
        for g, ref in enumerate(out_refs):
            ref[:, start : start + chunk] = out[PAD * g : PAD * g + PAD]


def update(here, mix, stack, chunk=1024):
    cols = stack[0].shape[1] - SHARED
    return pl.pallas_call(
        functools.partial(update_kernel, chunk=chunk),
        in_specs=[SMEM_SPEC] + [VMEM_SPEC] * 6,
        out_specs=[VMEM_SPEC] * 4,
        out_shape=[pltpu.VMEM((PAD, cols), jnp.float32)] * 4,
        compiler_params=pltpu.CompilerParams(vmem_limit_bytes=8 << 20),
        name="update",
    )(here, near(mix), *[near(x) for x in stack])


def own_kernel(here_ref, mix_ref, *refs, cols, chunk):
    stack_refs, (hi_ref, over_ref, lo_ref) = refs[:5], refs[5:8]
    basis_hbm, out_hbm, mine, snap, buf, in_sems, out_sems = refs[8:]
    here = here_ref[0]
    tiles = SHARED // LANES
    blocks = [lax.rem(here + 1 + b, 4) for b in range(4)]
    reads = []
    for b in range(3):
        at = pl.multiple_of(blocks[b] * cols, LANES)
        source = basis_hbm.at[:, pl.ds(at, SHARED)]
        reads.append(pltpu.make_async_copy(source, mine.at[b], in_sems.at[b]))
    for copy in reads:
        copy.start()
    mix = turned_mix(mix_rows(mix_ref, here, 0), here)
    for b, ref in enumerate((hi_ref, over_ref, lo_ref)):
        snap[b] = jnp.zeros((PAD, SHARED), jnp.float32)
        for k in range(2 * tiles):
            which, tile = divmod(k, tiles)
            at = 3 * SHARED + k // 8 * LANES
            line = ref[k % 8 : k % 8 + 1, at : at + LANES]
            snap[b, which : which + 1, tile * LANES : (tile + 1) * LANES] = line
    for copy in reads:
        copy.wait()
    writes = []
    for b in range(4):
        for start in range(0, SHARED, chunk):
            at = slice(start, start + chunk)
            if b == 3:
                stack = stacked(stack_refs, at)
            else:
                wide = slice(b * SHARED + start, b * SHARED + start + chunk)
                rows = [snap[b, :, at], mine[b, :, at]]
                rows += [ref[:, wide] for ref in (hi_ref, over_ref, lo_ref)]
                stack = jnp.concatenate(rows, axis=0)
            buf[b, :, at] = mixed(mix, stack)
        target = pl.ds(pl.multiple_of(blocks[b] * cols, LANES), SHARED)
        writes.append(pltpu.make_async_copy(buf.at[b], out_hbm.at[:, target], out_sems.at[b]))
        writes[-1].start()
    for copy in writes:
        copy.wait()


def own(here, mix, stack, received, basis, chunk=1024):
    cols = basis.shape[1] // 4
    return pl.pallas_call(
        functools.partial(own_kernel, cols=cols, chunk=chunk),
        in_specs=[SMEM_SPEC] + [VMEM_SPEC] * 9 + [HBM_SPEC],
        out_specs=HBM_SPEC,
        out_shape=pltpu.HBM(basis.shape, jnp.float32),
        scratch_shapes=[
            pltpu.VMEM((3, PAD, SHARED), jnp.float32),
            pltpu.VMEM((3, PAD, SHARED), jnp.float32),
            pltpu.VMEM((4, PAD, SHARED), jnp.float32),
            pltpu.SemaphoreType.DMA((3,)),
            pltpu.SemaphoreType.DMA((4,)),
        ],
        compiler_params=pltpu.CompilerParams(vmem_limit_bytes=10 << 20),
        name="own",
    )(here, *[near(x) for x in (mix, *stack, *received)], far(basis))


def join_kernel(here_ref, *refs):
    parts, (_, out_hbm, sems) = refs[:4], refs[4:]
    cols = out_hbm.shape[1] // 4
    copies = []
    for g, part in enumerate(parts):
        at = pl.multiple_of(lax.rem(here_ref[0] + g, 4) * cols + SHARED, LANES)
        target = out_hbm.at[:, pl.ds(at, cols - SHARED)]
        copies.append(pltpu.make_async_copy(part, target, sems.at[g]))
        copies[-1].start()
    for copy in copies:
        copy.wait()


def join(here, parts, whole):
    return pl.pallas_call(
        join_kernel,
        in_specs=[SMEM_SPEC] + [VMEM_SPEC] * 4 + [HBM_SPEC],
        out_specs=HBM_SPEC,
        out_shape=pltpu.HBM(whole.shape, jnp.float32),
        scratch_shapes=[pltpu.SemaphoreType.DMA((4,))],
        input_output_aliases={5: 0},
        compiler_params=pltpu.CompilerParams(vmem_limit_bytes=2 << 20),
        name="join",
    )(here, *[near(x) for x in parts], far(whole))


def program(velocity, basis, levels, profile_index, advect):
    n_space, n_mode = lax.axis_size("space"), lax.axis_size("mode")
    comps, cx, _, ny = velocity.shape
    here = lax.axis_index("mode").astype(jnp.int32).reshape(1)

    def shifted(x, axis, by):
        size = lax.axis_size(axis)
        return lax.ppermute(x, axis, [(i, (i + by) % size) for i in range(size)])

    face_lo, face_hi, plane_lo, plane_hi, *blocks = pack(here, velocity, basis)
    zlo = shifted(face_hi, "mode", 1)
    zhi = shifted(face_lo, "mode", -1)
    lo = shifted(blocks[1], "mode", 1)
    hi = shifted(blocks[3], "mode", -1)
    over = shifted(blocks[2], "mode", 2)
    xlo = shifted(plane_hi, "space", 1)
    xhi = shifted(plane_lo, "space", -1)
    near_lo = zlo.reshape(comps, 2, cx, ny)[:, 1]
    near_hi = zhi.reshape(comps, 2, cx, ny)[:, 0]
    corner_lo = jnp.stack([near_lo[:, -1], near_hi[:, -1]], axis=1)
    corner_hi = jnp.stack([near_lo[:, 0], near_hi[:, 0]], axis=1)
    corner_lo = shifted(corner_lo, "space", 1)
    corner_hi = shifted(corner_hi, "space", -1)
    snap, plus, minus, across = snapshots(
        velocity,
        levels,
        profile_index,
        advect,
        here,
        basis,
        (zlo, zhi, face_lo, face_hi, corner_lo, corner_hi, velocity, xlo, xhi),
    )
    lo_early = shifted(plus, "mode", 1)
    hi_early = shifted(minus, "mode", -1)
    stack = (snap, blocks[0], hi, over, lo)
    total = gram(here, stack)
    total = ring_sum(total, ring_parts(total, "space", n_space, 1, 2))
    total = ring_sum(total, ring_parts(total, "space", n_space, 2, 4))
    total = ring_sum(total, ring_parts(total, "space", n_space, 8, 4))
    parts = [total] + ring_parts(total, "mode", n_mode, 1, n_mode)
    over_early = shifted(across, "mode", 2)
    mix, sigma = factor(parts)
    out_own, out_next, out_over, out_prev = update(here, mix, stack)
    back_lo = shifted(out_next, "mode", 1)
    back_hi = shifted(out_prev, "mode", -1)
    back_over = shifted(out_over, "mode", 2)
    mine = own(here, mix, stack, (hi_early, over_early, lo_early), basis)
    modes = join(here, (out_own, back_hi, back_over, back_lo), mine)
    return (modes, sigma[0, :MODES])


def solution(mesh):
    return jax.shard_map(
        program,
        mesh=mesh,
        in_specs=(P(None, "space", "mode", None), P("mode", "space"), P(), P(), P()),
        out_specs=(P("mode", "space"), P()),
        check_vma=False,
    )
```

```python
import functools

import jax
import jax.numpy as jnp
import numpy as np
from jax import lax
from jax.experimental import pallas as pl
from jax.experimental.pallas import tpu as pltpu
from jax.sharding import PartitionSpec as P

STRIDE = 4
MODES = 32
SWEEPS = 2
FACTOR_BLOCK = 8
COUNT = 34
ROWS = 40
LANES = 128
PAD = 8
VMEM_SPEC = pl.BlockSpec(memory_space=pltpu.VMEM)
HBM_SPEC = pl.BlockSpec(memory_space=pltpu.HBM)
SMEM_SPEC = pl.BlockSpec(memory_space=pltpu.SMEM)


SHARED = 6144
FOLD = SHARED // 4

PLACE = np.array([0, 1] + list(range(PAD, PAD + MODES)))


def near(x):
    return pltpu.with_memory_space_constraint(x, pltpu.VMEM)


def far(x):
    return pltpu.with_memory_space_constraint(x, pltpu.HBM)


def pair_tables():
    rounds = COUNT - 1
    partner = np.tile(np.arange(LANES, dtype=np.int32), (ROWS, 1))
    orient = np.ones((ROWS, LANES), np.float32)
    for turn in range(rounds):
        players = [0] + [1 + (i - 1 + turn) % rounds for i in range(1, COUNT)]
        for k in range(COUNT // 2):
            lead, trail = PLACE[players[k]], PLACE[players[COUNT - 1 - k]]
            partner[turn, lead] = trail
            partner[turn, trail] = lead
            orient[turn, lead] = -1.0
    keep = np.zeros((1, LANES), np.int32)
    keep[0, :MODES] = PLACE[:MODES]
    return partner, orient, keep


def pack_kernel(
    here_ref,
    vel_hbm,
    basis_hbm,
    zfirst_ref,
    zlast_ref,
    xfirst_ref,
    xlast_ref,
    mine_ref,
    next_ref,
    far_ref,
    prev_ref,
    buf,
    edge_sems,
    face_sems,
    block_sems,
):
    comps, cx, cz, _ = vel_hbm.shape
    cols = mine_ref.shape[1]
    edges, rest = [], []
    for c in range(comps):
        for side, at in enumerate((0, cz - PAD)):
            source = vel_hbm.at[c, :, pl.ds(at, PAD), :]
            edges.append(pltpu.make_async_copy(source, buf.at[c, side], edge_sems.at[c, side]))
        for side, (at, ref) in enumerate(((0, xfirst_ref), (cx - 2, xlast_ref))):
            source = vel_hbm.at[c, pl.ds(at, 2)]
            rest.append(pltpu.make_async_copy(source, ref.at[c], face_sems.at[c, side]))
    for k, ref in enumerate((mine_ref, next_ref, far_ref, prev_ref)):
        at = pl.multiple_of(lax.rem(here_ref[0] + k, 4) * cols, LANES)
        source = basis_hbm.at[:, pl.ds(at, cols)]
        rest.append(pltpu.make_async_copy(source, ref, block_sems.at[k]))
    for copy in edges + rest:
        copy.start()
    for copy in edges:
        copy.wait()
    for c in range(comps):
        for i in range(cx):
            for k in range(2):
                row, last = (2 * c + k) * cx + i, PAD - 2 + k
                zfirst_ref[row : row + 1, :] = buf[c, 0, i, k : k + 1, :]
                zlast_ref[row : row + 1, :] = buf[c, 1, i, last : last + 1, :]
    for copy in rest:
        copy.wait()


def pack(here, velocity, basis):
    comps, cx, cz, ny = velocity.shape
    edge = pltpu.VMEM((comps * 2 * cx, ny), jnp.float32)
    face = pltpu.VMEM((comps, 2, cz, ny), jnp.float32)
    block = pltpu.VMEM((PAD, basis.shape[1] // 4), jnp.float32)
    return pl.pallas_call(
        pack_kernel,
        in_specs=[SMEM_SPEC, HBM_SPEC, HBM_SPEC],
        out_specs=[VMEM_SPEC] * 8,
        out_shape=[edge, edge, face, face] + [block] * 4,
        scratch_shapes=[
            pltpu.VMEM((comps, 2, cx, PAD, ny), jnp.float32),
            pltpu.SemaphoreType.DMA((comps, 2)),
            pltpu.SemaphoreType.DMA((comps, 2)),
            pltpu.SemaphoreType.DMA((4,)),
        ],
        compiler_params=pltpu.CompilerParams(vmem_limit_bytes=4 << 20),
        name="pack",
    )(here, far(velocity), far(basis))


def coefficients(levels_ref, index_ref, advect_ref):
    index = index_ref[...]
    visc = jnp.zeros(index.shape, jnp.float32)
    for level in range(levels_ref.shape[0]):
        visc = jnp.where(index == level, levels_ref[level], visc)
    cells = index.shape[1]
    lane = lax.broadcasted_iota(jnp.int32, index.shape, 1)
    first, last = lane == 0, lane == cells - 1
    up = jnp.where(last, visc, 0.5 * (visc + pltpu.roll(visc, cells - 1, 1)))
    down = jnp.where(first, visc, 0.5 * (visc + pltpu.roll(visc, 1, 1)))
    half = 0.5 * advect_ref[...]
    return (
        1.0 - 4.0 * visc - up - down,
        visc,
        visc - half,
        visc + half,
        jnp.where(last, 0.0, up),
        jnp.where(first, 0.0, down),
    )


def step(coefs, center, east, west, north, south):
    mid, visc, c_east, c_west, c_up, c_down = coefs
    cells = center.shape[-1]
    upward = pltpu.roll(center, cells - 1, 1)
    downward = pltpu.roll(center, 1, 1)
    return (
        mid * center
        + visc * (north + south)
        + c_east * east
        + c_west * west
        + c_up * upward
        + c_down * downward
    )


def split3(x):
    high = x.astype(jnp.bfloat16)
    rest = x - high.astype(jnp.float32)
    middle = rest.astype(jnp.bfloat16)
    low = (rest - middle.astype(jnp.float32)).astype(jnp.bfloat16)
    return high, middle, low


def offer_copies(here, basis_hbm, refs, sems):
    cols = basis_hbm.shape[1] // 4
    copies = []
    for side, (ref, skip) in enumerate(zip(refs, (2, 0, 3))):
        for k in range(3):
            at = pl.multiple_of(lax.rem(here + skip + k, 4) * cols, LANES)
            source = basis_hbm.at[:, pl.ds(at, SHARED)]
            target = ref.at[:, pl.ds(k * SHARED, SHARED)]
            copies.append(pltpu.make_async_copy(source, target, sems.at[side, k]))
    return copies


def stencil_kernel(
    levels_ref,
    index_ref,
    advect_ref,
    sum_ref,
    zlo_ref,
    zhi_ref,
    face_lo_ref,
    face_hi_ref,
    corner_lo_ref,
    corner_hi_ref,
    here_ref,
    basis_hbm,
    vel_hbm,
    xlo_hbm,
    xhi_hbm,
    out_ref,
    plus_ref,
    minus_ref,
    over_ref,
    field,
    first,
    boxed,
    sems,
    offer_sems,
):
    comp = pl.program_id(0)
    offer_refs = (plus_ref, minus_ref, over_ref)
    offers = offer_copies(here_ref[0], basis_hbm, offer_refs, offer_sems)
    cx, cz, ny = vel_hbm.shape[1:]
    inner = pl.ds(PAD, cz)

    def copies(c):
        return (
            pltpu.make_async_copy(
                vel_hbm.at[c], field.at[c, pl.ds(2, cx), inner, :], sems.at[c, 0]
            ),
            pltpu.make_async_copy(
                xlo_hbm.at[c], field.at[c, pl.ds(0, 2), inner, :], sems.at[c, 1]
            ),
            pltpu.make_async_copy(
                xhi_hbm.at[c], field.at[c, pl.ds(cx + 2, 2), inner, :], sems.at[c, 2]
            ),
        )

    @pl.when(comp == 0)
    def _():
        for c in range(3):
            for copy in copies(c):
                copy.start()
        for copy in offers:
            copy.start()

    @pl.when(comp == pl.num_programs(0) - 1)
    def _():
        for copy in offers:
            copy.wait()

    coefs = coefficients(levels_ref, index_ref, advect_ref)

    def edge_row(ref, k):
        return ref[pl.ds(pl.multiple_of((2 * comp + k) * cx, 8), cx), :]

    zlo2, zlo1 = edge_row(zlo_ref, 0), edge_row(zlo_ref, 1)
    zhi1, zhi2 = edge_row(zhi_ref, 0), edge_row(zhi_ref, 1)
    lo_before, lo_after = corner_lo_ref[comp, 0:1], corner_hi_ref[comp, 0:1]
    hi_before, hi_after = corner_lo_ref[comp, 1:2], corner_hi_ref[comp, 1:2]
    plane = lax.broadcasted_iota(jnp.int32, (cx, ny), 0)

    def edge(row, before, after, north, south):
        east = jnp.where(plane == cx - 1, after, pltpu.roll(row, cx - 1, 0))
        west = jnp.where(plane == 0, before, pltpu.roll(row, 1, 0))
        return step(coefs, row, east, west, north, south)

    edge_lo = edge(zlo1, lo_before, lo_after, zlo2, edge_row(face_lo_ref, 0))
    edge_hi = edge(zhi1, hi_before, hi_after, edge_row(face_hi_ref, 1), zhi2)
    for i in range(cx):
        field[comp, 2 + i, PAD - 1 : PAD, :] = zlo1[i : i + 1]
        field[comp, 2 + i, PAD + cz : PAD + cz + 1, :] = zhi1[i : i + 1]
        first[1 + i, PAD - 1 : PAD, :] = edge_lo[i : i + 1]
        first[1 + i, PAD + cz : PAD + cz + 1, :] = edge_hi[i : i + 1]
    field[comp, 1, PAD - 1 : PAD, :] = lo_before
    field[comp, 1, PAD + cz : PAD + cz + 1, :] = hi_before
    field[comp, cx + 2, PAD - 1 : PAD, :] = lo_after
    field[comp, cx + 2, PAD + cz : PAD + cz + 1, :] = hi_after

    for copy in copies(comp):
        copy.wait()

    chunk = 16

    def first_plane(p, carry):
        for k in range(cz // chunk):
            at = PAD + k * chunk
            rows = pl.ds(at, chunk)
            first[p, rows, :] = step(
                coefs,
                field[comp, p + 1, rows, :],
                field[comp, p + 2, rows, :],
                field[comp, p, rows, :],
                field[comp, p + 1, pl.ds(at - 1, chunk), :],
                field[comp, p + 1, pl.ds(at + 1, chunk), :],
            )
        return carry

    lax.fori_loop(0, cx + 2, first_plane, 0)

    sums = sum_ref[...]
    lane = lax.broadcasted_iota(jnp.int32, (cz, LANES), 1)
    row = lax.broadcasted_iota(jnp.int32, (cz, LANES), 0)
    wanted = (lane // (LANES // 2)) == ((row // STRIDE) % 2)
    part = out_ref.shape[1] // vel_hbm.shape[0]
    offset = pl.multiple_of(comp * part, LANES)
    out_ref[:, pl.ds(offset, part)] = jnp.zeros((PAD, part), jnp.float32)

    def coarse(which, box):
        total = sum(
            jnp.dot(part, sums, preferred_element_type=jnp.float32)
            for part in split3(boxed[...])
        )
        total = jnp.where(wanted, total, 0.0)
        base = offset + box * (cz // 8 * LANES)
        for r in range(cz // 8):
            line = jnp.sum(total[8 * r : 8 * r + 8], axis=0, keepdims=True) * 0.125
            at = pl.multiple_of(base + r * LANES, LANES)
            out_ref[which : which + 1, pl.ds(at, LANES)] = line

    def box_step(box, carry):
        start = 1 + STRIDE * box
        for k in range(cz // chunk):
            rows = pl.ds(PAD + k * chunk, chunk)
            boxed[pl.ds(k * chunk, chunk), :] = (
                first[start, rows, :] + first[start + 1, rows, :]
            ) + (first[start + 2, rows, :] + first[start + 3, rows, :])
        coarse(0, box)
        for k in range(cz // chunk):
            at = PAD + k * chunk
            rows = pl.ds(at, chunk)
            total = None
            for i in range(STRIDE):
                p = start + i
                value = step(
                    coefs,
                    first[p, rows, :],
                    first[p + 1, rows, :],
                    first[p - 1, rows, :],
                    first[p, pl.ds(at - 1, chunk), :],
                    first[p, pl.ds(at + 1, chunk), :],
                )
                total = value if total is None else total + value
            boxed[pl.ds(k * chunk, chunk), :] = total
        coarse(1, box)
        return carry

    lax.fori_loop(0, cx // STRIDE, box_step, 0)

    @pl.when(comp == 0)
    def _():
        tiles = SHARED // LANES
        for k in range(2 * tiles):
            which, tile = divmod(k, tiles)
            line = out_ref[which : which + 1, tile * LANES : (tile + 1) * LANES]
            at = 3 * SHARED + k // 8 * LANES
            for ref in offer_refs:
                ref[k % 8 : k % 8 + 1, at : at + LANES] = line


def snapshots(velocity, levels, profile_index, advect, here, basis, halos):
    comps, cx, cz, ny = velocity.shape
    cols = (cx // STRIDE) * (cz // STRIDE) * (ny // STRIDE)
    half = LANES // 2
    sums = np.zeros((ny, LANES), np.float32)
    for y in range(ny):
        sums[y, y // STRIDE] = 1.0
        sums[y, half + y // STRIDE] = 1.0
    return pl.pallas_call(
        stencil_kernel,
        grid=(comps,),
        in_specs=[
            SMEM_SPEC,
            pl.BlockSpec((1, ny), lambda c: (0, 0)),
            pl.BlockSpec((1, ny), lambda c: (0, 0)),
            pl.BlockSpec((ny, LANES), lambda c: (0, 0)),
            *[VMEM_SPEC] * 6,
            SMEM_SPEC,
            HBM_SPEC,
            HBM_SPEC,
            VMEM_SPEC,
            VMEM_SPEC,
        ],
        out_specs=[VMEM_SPEC] * 4,
        out_shape=[pltpu.VMEM((PAD, comps * cols), jnp.float32)]
        + [pltpu.VMEM((PAD, 3 * SHARED + FOLD), jnp.float32)] * 3,
        scratch_shapes=[
            pltpu.VMEM((comps, cx + 4, cz + 2 * PAD, ny), jnp.float32),
            pltpu.VMEM((cx + 2, cz + 2 * PAD, ny), jnp.float32),
            pltpu.VMEM((cz, ny), jnp.float32),
            pltpu.SemaphoreType.DMA((comps, 3)),
            pltpu.SemaphoreType.DMA((3, 3)),
        ],
        compiler_params=pltpu.CompilerParams(vmem_limit_bytes=20 << 20),
        name="stencil",
    )(
        levels,
        profile_index.reshape(1, ny),
        advect.reshape(1, ny),
        jnp.asarray(sums, jnp.bfloat16),
        *[near(x) for x in halos[:6]],
        here,
        far(basis),
        far(halos[6]),
        *[near(x) for x in halos[7:]],
    )


def stacked(refs, at):
    return jnp.concatenate([ref[:, at] for ref in refs], axis=0)


def gram_kernel(here_ref, *refs, chunk):
    stack_refs, out_ref = refs[:-1], refs[-1]
    here = here_ref[0]
    n, acc = ROWS, None
    for start in range(0, stack_refs[0].shape[1], chunk):
        stack = stacked(stack_refs, slice(start, start + chunk))
        high = stack.astype(jnp.bfloat16).astype(jnp.float32)
        joined = jnp.concatenate([high, stack - high], axis=0).astype(jnp.bfloat16)
        part = lax.dot_general(
            joined, joined, (((1,), (1,)), ((), ())), preferred_element_type=jnp.float32
        )
        acc = part if acc is None else acc + part
    cross = acc[0:n, n : 2 * n] + acc[n : 2 * n, 0:n]
    total = acc[0:n, 0:n] + (cross + acc[n : 2 * n, n : 2 * n])
    total = jnp.concatenate([total, jnp.zeros((n, LANES - n), jnp.float32)], axis=1)
    lane = lax.broadcasted_iota(jnp.int32, (n, LANES), 1)
    turned = PAD + lax.rem(lane - PAD + MODES - PAD * here + MODES, MODES)
    inside = (lane >= PAD) & (lane < n)
    total = jnp.take_along_axis(total, jnp.where(inside, turned, lane), axis=1)
    out_ref[0:PAD, :] = total[0:PAD]
    for g in range(4):
        at = pl.multiple_of(PAD + PAD * lax.rem(here + g, 4), PAD)
        out_ref[pl.ds(at, PAD), :] = total[PAD + PAD * g : 2 * PAD + PAD * g]


def gram(here, stack, chunk=2048):
    return pl.pallas_call(
        functools.partial(gram_kernel, chunk=chunk),
        in_specs=[SMEM_SPEC] + [VMEM_SPEC] * 5,
        out_specs=VMEM_SPEC,
        out_shape=pltpu.VMEM((ROWS, LANES), jnp.float32),
        compiler_params=pltpu.CompilerParams(vmem_limit_bytes=8 << 20),
        name="gram",
    )(here, *[near(x) for x in stack])


def ring_moves(size, stride, width):
    moves = []
    for shift in range(1, width):
        pairs = []
        for i in range(size):
            k = (i // stride) % width
            pairs.append((i, i + ((k + shift) % width - k) * stride))
        moves.append(pairs)
    return moves


def ring_parts(x, axis, size, stride, width):
    return [lax.ppermute(x, axis, pairs) for pairs in ring_moves(size, stride, width)]


def ring_sum(x, parts):
    if len(parts) == 1:
        return x + parts[0]
    one, two, three = parts
    return (x + two) + (one + three)


def lane_sum(x):
    total = x[0:8]
    for k in range(1, ROWS // 8):
        total = total + x[8 * k : 8 * k + 8]
    total = total + pltpu.roll(total, 4, 0)
    total = total + pltpu.roll(total, 2, 0)
    return total + pltpu.roll(total, 1, 0)


def spread(x):
    return jnp.concatenate([x] * (ROWS // 8), axis=0)


def factor_kernel(
    g0_ref, g1_ref, g2_ref, g3_ref, partner_ref, orient_ref, keep_ref, mix_ref, sigma_ref
):
    a = (g0_ref[...] + g2_ref[...]) + (g1_ref[...] + g3_ref[...])
    lane = lax.broadcasted_iota(jnp.int32, (ROWS, LANES), 1)
    row = lax.broadcasted_iota(jnp.int32, (ROWS, LANES), 0)
    upper = jnp.zeros((ROWS, LANES), jnp.float32)
    places = [int(k) for k in PLACE]
    while places:
        block, places = places[:FACTOR_BLOCK], places[FACTOR_BLOCK:]
        lines = [jnp.broadcast_to(a[j : j + 1, :], (8, LANES)) for j in block]
        columns = [jnp.broadcast_to(a[:, j : j + 1], (ROWS, LANES)) for j in block]

        def entry(column, j):
            return jnp.broadcast_to(column[j : j + 1, :], (8, LANES))

        for i, j in enumerate(block):
            scale = lax.rsqrt(entry(columns[i], j))
            lines[i] = lines[i] * scale
            columns[i] = columns[i] * spread(scale)
            for k in range(i + 1, len(block)):
                cross = entry(columns[i], block[k])
                lines[k] = lines[k] - cross * lines[i]
                columns[k] = columns[k] - spread(cross) * columns[i]
        for i, j in enumerate(block):
            line = spread(lines[i])
            a = a - columns[i] * line
            upper = jnp.where((row == j) & (lane >= j), line, upper)

    def turn_step(i, state):
        x, v = state
        turn = lax.rem(i, COUNT - 1)
        other = jnp.broadcast_to(partner_ref[pl.ds(turn, 1), :], (ROWS, LANES))
        sign = jnp.broadcast_to(orient_ref[pl.ds(turn, 1), :], (8, LANES))
        y = jnp.take_along_axis(x, other, axis=1)
        vy = jnp.take_along_axis(v, other, axis=1)
        contrast = lane_sum(y * y) - lane_sum(x * x)
        inner = lane_sum(x * y)
        toward = jnp.where(contrast > 0.0, -1.0, jnp.where(contrast < 0.0, 1.0, sign))
        d = jnp.abs(contrast) + jnp.sqrt(contrast * contrast + 4.0 * inner * inner)
        positive = d > 0.0
        tangent = jnp.where(
            positive, 2.0 * inner * toward / jnp.where(positive, d, 1.0), 0.0
        )
        cosine = 1.0 / jnp.sqrt(1.0 + tangent * tangent)
        sine = spread(cosine * tangent)
        cosine = spread(cosine)
        return cosine * x + sine * y, cosine * v + sine * vy

    eye = jnp.where(row == lane, 1.0, 0.0)
    x, v = lax.fori_loop(0, SWEEPS * (COUNT - 1), turn_step, (upper, eye))
    keep = jnp.broadcast_to(keep_ref[...], (ROWS, LANES))
    sigma_ref[...] = jnp.take_along_axis(jnp.sqrt(lane_sum(x * x)), keep[0:8], axis=1)
    v = jnp.take_along_axis(v, keep, axis=1)
    high = v.astype(jnp.bfloat16).astype(jnp.float32)
    low = v - high
    mix = jnp.concatenate([high, high, low, jnp.zeros((8, LANES), jnp.float32)], axis=0)
    mix_ref[...] = jnp.transpose(mix)[0:MODES]


def factor(parts):
    tables = [near(jnp.asarray(table)) for table in pair_tables()]
    return pl.pallas_call(
        factor_kernel,
        in_specs=[VMEM_SPEC] * 7,
        out_specs=(VMEM_SPEC, VMEM_SPEC),
        out_shape=(
            pltpu.VMEM((MODES, LANES), jnp.float32),
            pltpu.VMEM((8, LANES), jnp.float32),
        ),
        compiler_params=pltpu.CompilerParams(vmem_limit_bytes=4 << 20),
        name="factor",
    )(*[near(x) for x in parts], *tables)


def turned_mix(mix, here):
    lane = lax.broadcasted_iota(jnp.int32, mix.shape, 1)
    inside = lax.rem(lane, ROWS)
    turned = lane - inside + PAD + lax.rem(inside + (MODES - PAD) + PAD * here, MODES)
    source = jnp.where((inside < PAD) | (lane >= 3 * ROWS), lane, turned)
    return jnp.take_along_axis(mix, source, axis=1).astype(jnp.bfloat16)


def mix_rows(mix_ref, here, g):
    at = pl.multiple_of(PAD * lax.rem(here + g, 4), PAD)
    return mix_ref[pl.ds(at, PAD), :]


def mixed(mix, stack):
    high = stack.astype(jnp.bfloat16).astype(jnp.float32)
    zero = jnp.zeros((8, stack.shape[1]), jnp.float32)
    joined = jnp.concatenate([high, stack - high, high, zero], axis=0)
    return jnp.dot(mix, joined.astype(jnp.bfloat16), preferred_element_type=jnp.float32)


def update_kernel(here_ref, mix_ref, *refs, chunk):
    stack_refs, out_refs = refs[:5], refs[5:]
    here = here_ref[0]
    mix = jnp.concatenate([mix_rows(mix_ref, here, g) for g in range(4)], axis=0)
    mix = turned_mix(mix, here)
    for start in range(0, out_refs[0].shape[1], chunk):
        first = SHARED + start
        out = mixed(mix, stacked(stack_refs, slice(first, first + chunk)))
        for g, ref in enumerate(out_refs):
            ref[:, start : start + chunk] = out[PAD * g : PAD * g + PAD]


def update(here, mix, stack, chunk=1024):
    cols = stack[0].shape[1] - SHARED
    return pl.pallas_call(
        functools.partial(update_kernel, chunk=chunk),
        in_specs=[SMEM_SPEC] + [VMEM_SPEC] * 6,
        out_specs=[VMEM_SPEC] * 4,
        out_shape=[pltpu.VMEM((PAD, cols), jnp.float32)] * 4,
        compiler_params=pltpu.CompilerParams(vmem_limit_bytes=8 << 20),
        name="update",
    )(here, near(mix), *[near(x) for x in stack])


def own_kernel(here_ref, mix_ref, *refs, cols, chunk):
    stack_refs, (hi_ref, over_ref, lo_ref) = refs[:5], refs[5:8]
    basis_hbm, out_hbm, mine, snap, buf, in_sems, out_sems = refs[8:]
    here = here_ref[0]
    tiles = SHARED // LANES
    blocks = [lax.rem(here + 1 + b, 4) for b in range(4)]
    reads = []
    for b in range(3):
        at = pl.multiple_of(blocks[b] * cols, LANES)
        source = basis_hbm.at[:, pl.ds(at, SHARED)]
        reads.append(pltpu.make_async_copy(source, mine.at[b], in_sems.at[b]))
    for copy in reads:
        copy.start()
    mix = turned_mix(mix_rows(mix_ref, here, 0), here)
    for b, ref in enumerate((hi_ref, over_ref, lo_ref)):
        snap[b] = jnp.zeros((PAD, SHARED), jnp.float32)
        for k in range(2 * tiles):
            which, tile = divmod(k, tiles)
            at = 3 * SHARED + k // 8 * LANES
            line = ref[k % 8 : k % 8 + 1, at : at + LANES]
            snap[b, which : which + 1, tile * LANES : (tile + 1) * LANES] = line
    for copy in reads:
        copy.wait()
    writes = []
    for b in range(4):
        for start in range(0, SHARED, chunk):
            at = slice(start, start + chunk)
            if b == 3:
                stack = stacked(stack_refs, at)
            else:
                wide = slice(b * SHARED + start, b * SHARED + start + chunk)
                rows = [snap[b, :, at], mine[b, :, at]]
                rows += [ref[:, wide] for ref in (hi_ref, over_ref, lo_ref)]
                stack = jnp.concatenate(rows, axis=0)
            buf[b, :, at] = mixed(mix, stack)
        target = pl.ds(pl.multiple_of(blocks[b] * cols, LANES), SHARED)
        writes.append(pltpu.make_async_copy(buf.at[b], out_hbm.at[:, target], out_sems.at[b]))
        writes[-1].start()
    for copy in writes:
        copy.wait()


def own(here, mix, stack, received, basis, chunk=1024):
    cols = basis.shape[1] // 4
    return pl.pallas_call(
        functools.partial(own_kernel, cols=cols, chunk=chunk),
        in_specs=[SMEM_SPEC] + [VMEM_SPEC] * 9 + [HBM_SPEC],
        out_specs=HBM_SPEC,
        out_shape=pltpu.HBM(basis.shape, jnp.float32),
        scratch_shapes=[
            pltpu.VMEM((3, PAD, SHARED), jnp.float32),
            pltpu.VMEM((3, PAD, SHARED), jnp.float32),
            pltpu.VMEM((4, PAD, SHARED), jnp.float32),
            pltpu.SemaphoreType.DMA((3,)),
            pltpu.SemaphoreType.DMA((4,)),
        ],
        compiler_params=pltpu.CompilerParams(vmem_limit_bytes=10 << 20),
        name="own",
    )(here, *[near(x) for x in (mix, *stack, *received)], far(basis))


def join_kernel(here_ref, *refs):
    parts, (_, out_hbm, sems) = refs[:4], refs[4:]
    cols = out_hbm.shape[1] // 4
    copies = []
    for g, part in enumerate(parts):
        at = pl.multiple_of(lax.rem(here_ref[0] + g, 4) * cols + SHARED, LANES)
        target = out_hbm.at[:, pl.ds(at, cols - SHARED)]
        copies.append(pltpu.make_async_copy(part, target, sems.at[g]))
        copies[-1].start()
    for copy in copies:
        copy.wait()


def join(here, parts, whole):
    return pl.pallas_call(
        join_kernel,
        in_specs=[SMEM_SPEC] + [VMEM_SPEC] * 4 + [HBM_SPEC],
        out_specs=HBM_SPEC,
        out_shape=pltpu.HBM(whole.shape, jnp.float32),
        scratch_shapes=[pltpu.SemaphoreType.DMA((4,))],
        input_output_aliases={5: 0},
        compiler_params=pltpu.CompilerParams(vmem_limit_bytes=2 << 20),
        name="join",
    )(here, *[near(x) for x in parts], far(whole))


def program(velocity, basis, levels, profile_index, advect):
    n_space, n_mode = lax.axis_size("space"), lax.axis_size("mode")
    comps, cx, _, ny = velocity.shape
    here = lax.axis_index("mode").astype(jnp.int32).reshape(1)

    def shifted(x, axis, by):
        size = lax.axis_size(axis)
        return lax.ppermute(x, axis, [(i, (i + by) % size) for i in range(size)])

    face_lo, face_hi, plane_lo, plane_hi, *blocks = pack(here, velocity, basis)
    zlo = shifted(face_hi, "mode", 1)
    zhi = shifted(face_lo, "mode", -1)
    lo = shifted(blocks[1], "mode", 1)
    hi = shifted(blocks[3], "mode", -1)
    over = shifted(blocks[2], "mode", 2)
    xlo = shifted(plane_hi, "space", 1)
    xhi = shifted(plane_lo, "space", -1)
    near_lo = zlo.reshape(comps, 2, cx, ny)[:, 1]
    near_hi = zhi.reshape(comps, 2, cx, ny)[:, 0]
    corner_lo = jnp.stack([near_lo[:, -1], near_hi[:, -1]], axis=1)
    corner_hi = jnp.stack([near_lo[:, 0], near_hi[:, 0]], axis=1)
    corner_lo = shifted(corner_lo, "space", 1)
    corner_hi = shifted(corner_hi, "space", -1)
    snap, plus, minus, across = snapshots(
        velocity,
        levels,
        profile_index,
        advect,
        here,
        basis,
        (zlo, zhi, face_lo, face_hi, corner_lo, corner_hi, velocity, xlo, xhi),
    )
    lo_early = shifted(plus, "mode", 1)
    hi_early = shifted(minus, "mode", -1)
    stack = (snap, blocks[0], hi, over, lo)
    total = gram(here, stack)
    total = ring_sum(total, ring_parts(total, "space", n_space, 1, 2))
    total = ring_sum(total, ring_parts(total, "space", n_space, 2, 4))
    total = ring_sum(total, ring_parts(total, "space", n_space, 8, 4))
    parts = [total] + ring_parts(total, "mode", n_mode, 1, n_mode)
    over_early = shifted(across, "mode", 2)
    mix, sigma = factor(parts)
    out_own, out_next, out_over, out_prev = update(here, mix, stack)
    back_lo = shifted(out_next, "mode", 1)
    back_hi = shifted(out_prev, "mode", -1)
    back_over = shifted(out_over, "mode", 2)
    mine = own(here, mix, stack, (hi_early, over_early, lo_early), basis)
    modes = join(here, (out_own, back_hi, back_over, back_lo), mine)
    return (modes, sigma[0, :MODES])


def solution(mesh):
    return jax.shard_map(
        program,
        mesh=mesh,
        in_specs=(P(None, "space", "mode", None), P("mode", "space"), P(), P(), P()),
        out_specs=(P("mode", "space"), P()),
        check_vma=False,
    )
```

```python
import functools

import jax
import jax.numpy as jnp
import numpy as np
from jax import lax
from jax.experimental import pallas as pl
from jax.experimental.pallas import tpu as pltpu
from jax.sharding import PartitionSpec as P

STRIDE = 4
MODES = 32
SWEEPS = 2
FACTOR_BLOCK = 8
COUNT = 34
ROWS = 40
LANES = 128
PAD = 8
VMEM_SPEC = pl.BlockSpec(memory_space=pltpu.VMEM)
HBM_SPEC = pl.BlockSpec(memory_space=pltpu.HBM)
SMEM_SPEC = pl.BlockSpec(memory_space=pltpu.SMEM)


SHARED = 6144
FOLD = SHARED // 4

PLACE = np.array([0, 1] + list(range(PAD, PAD + MODES)))


def near(x):
    return pltpu.with_memory_space_constraint(x, pltpu.VMEM)


def far(x):
    return pltpu.with_memory_space_constraint(x, pltpu.HBM)


def pair_tables():
    rounds = COUNT - 1
    partner = np.tile(np.arange(LANES, dtype=np.int32), (ROWS, 1))
    orient = np.ones((ROWS, LANES), np.float32)
    for turn in range(rounds):
        players = [0] + [1 + (i - 1 + turn) % rounds for i in range(1, COUNT)]
        for k in range(COUNT // 2):
            lead, trail = PLACE[players[k]], PLACE[players[COUNT - 1 - k]]
            partner[turn, lead] = trail
            partner[turn, trail] = lead
            orient[turn, lead] = -1.0
    keep = np.zeros((1, LANES), np.int32)
    keep[0, :MODES] = PLACE[:MODES]
    return partner, orient, keep


def pack_kernel(
    here_ref,
    vel_hbm,
    basis_hbm,
    zfirst_ref,
    zlast_ref,
    xfirst_ref,
    xlast_ref,
    mine_ref,
    next_ref,
    far_ref,
    prev_ref,
    buf,
    edge_sems,
    face_sems,
    block_sems,
):
    comps, cx, cz, _ = vel_hbm.shape
    cols = mine_ref.shape[1]
    edges, rest = [], []
    for c in range(comps):
        for side, at in enumerate((0, cz - PAD)):
            source = vel_hbm.at[c, :, pl.ds(at, PAD), :]
            edges.append(pltpu.make_async_copy(source, buf.at[c, side], edge_sems.at[c, side]))
        for side, (at, ref) in enumerate(((0, xfirst_ref), (cx - 2, xlast_ref))):
            for k in range(2):
                source = vel_hbm.at[c, at + k]
                target = ref.at[pl.ds((2 * c + k) * cz, cz)]
                rest.append(pltpu.make_async_copy(source, target, face_sems.at[c, side, k]))
    for k, ref in enumerate((mine_ref, next_ref, far_ref, prev_ref)):
        at = pl.multiple_of(lax.rem(here_ref[0] + k, 4) * cols, LANES)
        source = basis_hbm.at[:, pl.ds(at, cols)]
        rest.append(pltpu.make_async_copy(source, ref, block_sems.at[k]))
    for copy in edges + rest:
        copy.start()
    for copy in edges:
        copy.wait()
    for c in range(comps):
        for i in range(cx):
            for k in range(2):
                row, last = (2 * c + k) * cx + i, PAD - 2 + k
                zfirst_ref[row : row + 1, :] = buf[c, 0, i, k : k + 1, :]
                zlast_ref[row : row + 1, :] = buf[c, 1, i, last : last + 1, :]
    for copy in rest:
        copy.wait()


def pack(here, velocity, basis):
    comps, cx, cz, ny = velocity.shape
    edge = pltpu.VMEM((comps * 2 * cx, ny), jnp.float32)
    face = pltpu.VMEM((comps * 2 * cz + PAD, ny), jnp.float32)
    block = pltpu.VMEM((PAD, basis.shape[1] // 4), jnp.float32)
    return pl.pallas_call(
        pack_kernel,
        in_specs=[SMEM_SPEC, HBM_SPEC, HBM_SPEC],
        out_specs=[VMEM_SPEC] * 8,
        out_shape=[edge, edge, face, face] + [block] * 4,
        scratch_shapes=[
            pltpu.VMEM((comps, 2, cx, PAD, ny), jnp.float32),
            pltpu.SemaphoreType.DMA((comps, 2)),
            pltpu.SemaphoreType.DMA((comps, 2, 2)),
            pltpu.SemaphoreType.DMA((4,)),
        ],
        compiler_params=pltpu.CompilerParams(vmem_limit_bytes=4 << 20),
        name="pack",
    )(here, far(velocity), far(basis))


def corner_kernel(zlo_ref, zhi_ref, _, __, xfirst_ref, xlast_ref, *, cx, comps):
    base = xfirst_ref.shape[0] - PAD
    zero = jnp.zeros((PAD, xfirst_ref.shape[1]), jnp.float32)
    for ref, plane in ((xfirst_ref, 0), (xlast_ref, cx - 1)):
        ref[base:, :] = zero
        for c in range(comps):
            low, high = (2 * c + 1) * cx + plane, 2 * c * cx + plane
            at = base + 2 * c
            ref[at : at + 1, :] = zlo_ref[low : low + 1, :]
            ref[at + 1 : at + 2, :] = zhi_ref[high : high + 1, :]


def add_corners(zlo, zhi, first, last, cx, comps):
    face = pltpu.VMEM(first.shape, jnp.float32)
    return pl.pallas_call(
        functools.partial(corner_kernel, cx=cx, comps=comps),
        in_specs=[VMEM_SPEC] * 4,
        out_specs=[VMEM_SPEC] * 2,
        out_shape=[face, face],
        input_output_aliases={2: 0, 3: 1},
        compiler_params=pltpu.CompilerParams(vmem_limit_bytes=1 << 20),
        name="corners",
    )(*[near(x) for x in (zlo, zhi, first, last)])


def coefficients(levels_ref, index_ref, advect_ref):
    index = index_ref[...]
    visc = jnp.zeros(index.shape, jnp.float32)
    for level in range(levels_ref.shape[0]):
        visc = jnp.where(index == level, levels_ref[level], visc)
    cells = index.shape[1]
    lane = lax.broadcasted_iota(jnp.int32, index.shape, 1)
    first, last = lane == 0, lane == cells - 1
    up = jnp.where(last, visc, 0.5 * (visc + pltpu.roll(visc, cells - 1, 1)))
    down = jnp.where(first, visc, 0.5 * (visc + pltpu.roll(visc, 1, 1)))
    half = 0.5 * advect_ref[...]
    return (
        1.0 - 4.0 * visc - up - down,
        visc,
        visc - half,
        visc + half,
        jnp.where(last, 0.0, up),
        jnp.where(first, 0.0, down),
    )


def step(coefs, center, east, west, north, south):
    mid, visc, c_east, c_west, c_up, c_down = coefs
    cells = center.shape[-1]
    upward = pltpu.roll(center, cells - 1, 1)
    downward = pltpu.roll(center, 1, 1)
    return (
        mid * center
        + visc * (north + south)
        + c_east * east
        + c_west * west
        + c_up * upward
        + c_down * downward
    )


def split3(x):
    high = x.astype(jnp.bfloat16)
    rest = x - high.astype(jnp.float32)
    middle = rest.astype(jnp.bfloat16)
    low = (rest - middle.astype(jnp.float32)).astype(jnp.bfloat16)
    return high, middle, low


def offer_copies(here, basis_hbm, refs, sems):
    cols = basis_hbm.shape[1] // 4
    copies = []
    for side, (ref, skip) in enumerate(zip(refs, (2, 0, 3))):
        for k in range(3):
            at = pl.multiple_of(lax.rem(here + skip + k, 4) * cols, LANES)
            source = basis_hbm.at[:, pl.ds(at, SHARED)]
            target = ref.at[:, pl.ds(k * SHARED, SHARED)]
            copies.append(pltpu.make_async_copy(source, target, sems.at[side, k]))
    return copies


def stencil_kernel(
    levels_ref,
    index_ref,
    advect_ref,
    sum_ref,
    zlo_ref,
    zhi_ref,
    face_lo_ref,
    face_hi_ref,
    here_ref,
    basis_hbm,
    vel_hbm,
    xlo_ref,
    xhi_ref,
    out_ref,
    plus_ref,
    minus_ref,
    over_ref,
    field,
    first,
    boxed,
    sems,
    offer_sems,
):
    comp = pl.program_id(0)
    offer_refs = (plus_ref, minus_ref, over_ref)
    offers = offer_copies(here_ref[0], basis_hbm, offer_refs, offer_sems)
    cx, cz, ny = vel_hbm.shape[1:]
    inner = pl.ds(PAD, cz)

    def copies(c):
        return (
            pltpu.make_async_copy(
                vel_hbm.at[c], field.at[c, pl.ds(2, cx), inner, :], sems.at[c, 0, 0]
            ),
            *[
                pltpu.make_async_copy(
                    ref.at[pl.ds((2 * c + k) * cz, cz)],
                    field.at[c, at + k, inner, :],
                    sems.at[c, 1 + side, k],
                )
                for side, (at, ref) in enumerate(((0, xlo_ref), (cx + 2, xhi_ref)))
                for k in range(2)
            ],
        )

    @pl.when(comp == 0)
    def _():
        for c in range(3):
            for copy in copies(c):
                copy.start()
        for copy in offers:
            copy.start()

    @pl.when(comp == pl.num_programs(0) - 1)
    def _():
        for copy in offers:
            copy.wait()

    coefs = coefficients(levels_ref, index_ref, advect_ref)

    def edge_row(ref, k):
        return ref[pl.ds(pl.multiple_of((2 * comp + k) * cx, 8), cx), :]

    zlo2, zlo1 = edge_row(zlo_ref, 0), edge_row(zlo_ref, 1)
    zhi1, zhi2 = edge_row(zhi_ref, 0), edge_row(zhi_ref, 1)
    spot = 6 * cz + 2 * comp
    lo_before, lo_after = xlo_ref[pl.ds(spot, 1), :], xhi_ref[pl.ds(spot, 1), :]
    hi_before, hi_after = xlo_ref[pl.ds(spot + 1, 1), :], xhi_ref[pl.ds(spot + 1, 1), :]
    plane = lax.broadcasted_iota(jnp.int32, (cx, ny), 0)

    def edge(row, before, after, north, south):
        east = jnp.where(plane == cx - 1, after, pltpu.roll(row, cx - 1, 0))
        west = jnp.where(plane == 0, before, pltpu.roll(row, 1, 0))
        return step(coefs, row, east, west, north, south)

    edge_lo = edge(zlo1, lo_before, lo_after, zlo2, edge_row(face_lo_ref, 0))
    edge_hi = edge(zhi1, hi_before, hi_after, edge_row(face_hi_ref, 1), zhi2)
    for i in range(cx):
        field[comp, 2 + i, PAD - 1 : PAD, :] = zlo1[i : i + 1]
        field[comp, 2 + i, PAD + cz : PAD + cz + 1, :] = zhi1[i : i + 1]
        first[1 + i, PAD - 1 : PAD, :] = edge_lo[i : i + 1]
        first[1 + i, PAD + cz : PAD + cz + 1, :] = edge_hi[i : i + 1]
    field[comp, 1, PAD - 1 : PAD, :] = lo_before
    field[comp, 1, PAD + cz : PAD + cz + 1, :] = hi_before
    field[comp, cx + 2, PAD - 1 : PAD, :] = lo_after
    field[comp, cx + 2, PAD + cz : PAD + cz + 1, :] = hi_after

    for copy in copies(comp):
        copy.wait()

    chunk = 16

    def first_plane(p, carry):
        for k in range(cz // chunk):
            at = PAD + k * chunk
            rows = pl.ds(at, chunk)
            first[p, rows, :] = step(
                coefs,
                field[comp, p + 1, rows, :],
                field[comp, p + 2, rows, :],
                field[comp, p, rows, :],
                field[comp, p + 1, pl.ds(at - 1, chunk), :],
                field[comp, p + 1, pl.ds(at + 1, chunk), :],
            )
        return carry

    lax.fori_loop(0, cx + 2, first_plane, 0)

    sums = sum_ref[...]
    lane = lax.broadcasted_iota(jnp.int32, (cz, LANES), 1)
    row = lax.broadcasted_iota(jnp.int32, (cz, LANES), 0)
    wanted = (lane // (LANES // 2)) == ((row // STRIDE) % 2)
    part = out_ref.shape[1] // vel_hbm.shape[0]
    offset = pl.multiple_of(comp * part, LANES)
    out_ref[:, pl.ds(offset, part)] = jnp.zeros((PAD, part), jnp.float32)

    def coarse(which, box):
        total = sum(
            jnp.dot(part, sums, preferred_element_type=jnp.float32)
            for part in split3(boxed[...])
        )
        total = jnp.where(wanted, total, 0.0)
        base = offset + box * (cz // 8 * LANES)
        for r in range(cz // 8):
            line = jnp.sum(total[8 * r : 8 * r + 8], axis=0, keepdims=True) * 0.125
            at = pl.multiple_of(base + r * LANES, LANES)
            out_ref[which : which + 1, pl.ds(at, LANES)] = line

    def box_step(box, carry):
        start = 1 + STRIDE * box
        for k in range(cz // chunk):
            rows = pl.ds(PAD + k * chunk, chunk)
            boxed[pl.ds(k * chunk, chunk), :] = (
                first[start, rows, :] + first[start + 1, rows, :]
            ) + (first[start + 2, rows, :] + first[start + 3, rows, :])
        coarse(0, box)
        for k in range(cz // chunk):
            at = PAD + k * chunk
            rows = pl.ds(at, chunk)
            total = None
            for i in range(STRIDE):
                p = start + i
                value = step(
                    coefs,
                    first[p, rows, :],
                    first[p + 1, rows, :],
                    first[p - 1, rows, :],
                    first[p, pl.ds(at - 1, chunk), :],
                    first[p, pl.ds(at + 1, chunk), :],
                )
                total = value if total is None else total + value
            boxed[pl.ds(k * chunk, chunk), :] = total
        coarse(1, box)
        return carry

    lax.fori_loop(0, cx // STRIDE, box_step, 0)

    @pl.when(comp == 0)
    def _():
        tiles = SHARED // LANES
        for k in range(2 * tiles):
            which, tile = divmod(k, tiles)
            line = out_ref[which : which + 1, tile * LANES : (tile + 1) * LANES]
            at = 3 * SHARED + k // 8 * LANES
            for ref in offer_refs:
                ref[k % 8 : k % 8 + 1, at : at + LANES] = line


def snapshots(velocity, levels, profile_index, advect, here, basis, halos):
    comps, cx, cz, ny = velocity.shape
    cols = (cx // STRIDE) * (cz // STRIDE) * (ny // STRIDE)
    half = LANES // 2
    sums = np.zeros((ny, LANES), np.float32)
    for y in range(ny):
        sums[y, y // STRIDE] = 1.0
        sums[y, half + y // STRIDE] = 1.0
    return pl.pallas_call(
        stencil_kernel,
        grid=(comps,),
        in_specs=[
            SMEM_SPEC,
            pl.BlockSpec((1, ny), lambda c: (0, 0)),
            pl.BlockSpec((1, ny), lambda c: (0, 0)),
            pl.BlockSpec((ny, LANES), lambda c: (0, 0)),
            *[VMEM_SPEC] * 4,
            SMEM_SPEC,
            HBM_SPEC,
            HBM_SPEC,
            VMEM_SPEC,
            VMEM_SPEC,
        ],
        out_specs=[VMEM_SPEC] * 4,
        out_shape=[pltpu.VMEM((PAD, comps * cols), jnp.float32)]
        + [pltpu.VMEM((PAD, 3 * SHARED + FOLD), jnp.float32)] * 3,
        scratch_shapes=[
            pltpu.VMEM((comps, cx + 4, cz + 2 * PAD, ny), jnp.float32),
            pltpu.VMEM((cx + 2, cz + 2 * PAD, ny), jnp.float32),
            pltpu.VMEM((cz, ny), jnp.float32),
            pltpu.SemaphoreType.DMA((comps, 3, 2)),
            pltpu.SemaphoreType.DMA((3, 3)),
        ],
        compiler_params=pltpu.CompilerParams(vmem_limit_bytes=20 << 20),
        name="stencil",
    )(
        levels,
        profile_index.reshape(1, ny),
        advect.reshape(1, ny),
        jnp.asarray(sums, jnp.bfloat16),
        *[near(x) for x in halos[:4]],
        here,
        far(basis),
        far(halos[4]),
        *[near(x) for x in halos[5:]],
    )


def stacked(refs, at):
    return jnp.concatenate([ref[:, at] for ref in refs], axis=0)


def gram_kernel(here_ref, *refs, chunk):
    stack_refs, out_ref = refs[:-1], refs[-1]
    here = here_ref[0]
    n, acc = ROWS, None
    for start in range(0, stack_refs[0].shape[1], chunk):
        stack = stacked(stack_refs, slice(start, start + chunk))
        high = stack.astype(jnp.bfloat16).astype(jnp.float32)
        joined = jnp.concatenate([high, stack - high], axis=0).astype(jnp.bfloat16)
        part = lax.dot_general(
            joined, joined, (((1,), (1,)), ((), ())), preferred_element_type=jnp.float32
        )
        acc = part if acc is None else acc + part
    cross = acc[0:n, n : 2 * n] + acc[n : 2 * n, 0:n]
    total = acc[0:n, 0:n] + (cross + acc[n : 2 * n, n : 2 * n])
    total = jnp.concatenate([total, jnp.zeros((n, LANES - n), jnp.float32)], axis=1)
    lane = lax.broadcasted_iota(jnp.int32, (n, LANES), 1)
    turned = PAD + lax.rem(lane - PAD + MODES - PAD * here + MODES, MODES)
    inside = (lane >= PAD) & (lane < n)
    total = jnp.take_along_axis(total, jnp.where(inside, turned, lane), axis=1)
    out_ref[0:PAD, :] = total[0:PAD]
    for g in range(4):
        at = pl.multiple_of(PAD + PAD * lax.rem(here + g, 4), PAD)
        out_ref[pl.ds(at, PAD), :] = total[PAD + PAD * g : 2 * PAD + PAD * g]


def gram(here, stack, chunk=2048):
    return pl.pallas_call(
        functools.partial(gram_kernel, chunk=chunk),
        in_specs=[SMEM_SPEC] + [VMEM_SPEC] * 5,
        out_specs=VMEM_SPEC,
        out_shape=pltpu.VMEM((ROWS, LANES), jnp.float32),
        compiler_params=pltpu.CompilerParams(vmem_limit_bytes=8 << 20),
        name="gram",
    )(here, *[near(x) for x in stack])


def ring_moves(size, stride, width):
    moves = []
    for shift in range(1, width):
        pairs = []
        for i in range(size):
            k = (i // stride) % width
            pairs.append((i, i + ((k + shift) % width - k) * stride))
        moves.append(pairs)
    return moves


def ring_parts(x, axis, size, stride, width):
    return [lax.ppermute(x, axis, pairs) for pairs in ring_moves(size, stride, width)]


def ring_sum(x, parts):
    if len(parts) == 1:
        return x + parts[0]
    one, two, three = parts
    return (x + two) + (one + three)


def lane_sum(x):
    total = x[0:8]
    for k in range(1, ROWS // 8):
        total = total + x[8 * k : 8 * k + 8]
    total = total + pltpu.roll(total, 4, 0)
    total = total + pltpu.roll(total, 2, 0)
    return total + pltpu.roll(total, 1, 0)


def spread(x):
    return jnp.concatenate([x] * (ROWS // 8), axis=0)


def factor_kernel(
    g0_ref, g1_ref, g2_ref, g3_ref, partner_ref, orient_ref, keep_ref, mix_ref, sigma_ref
):
    a = (g0_ref[...] + g2_ref[...]) + (g1_ref[...] + g3_ref[...])
    lane = lax.broadcasted_iota(jnp.int32, (ROWS, LANES), 1)
    row = lax.broadcasted_iota(jnp.int32, (ROWS, LANES), 0)
    upper = jnp.zeros((ROWS, LANES), jnp.float32)
    places = [int(k) for k in PLACE]
    while places:
        block, places = places[:FACTOR_BLOCK], places[FACTOR_BLOCK:]
        lines = [jnp.broadcast_to(a[j : j + 1, :], (8, LANES)) for j in block]
        columns = [jnp.broadcast_to(a[:, j : j + 1], (ROWS, LANES)) for j in block]

        def entry(column, j):
            return jnp.broadcast_to(column[j : j + 1, :], (8, LANES))

        for i, j in enumerate(block):
            scale = lax.rsqrt(entry(columns[i], j))
            lines[i] = lines[i] * scale
            columns[i] = columns[i] * spread(scale)
            for k in range(i + 1, len(block)):
                cross = entry(columns[i], block[k])
                lines[k] = lines[k] - cross * lines[i]
                columns[k] = columns[k] - spread(cross) * columns[i]
        for i, j in enumerate(block):
            line = spread(lines[i])
            a = a - columns[i] * line
            upper = jnp.where((row == j) & (lane >= j), line, upper)

    def turn_step(i, state):
        x, v = state
        turn = lax.rem(i, COUNT - 1)
        other = jnp.broadcast_to(partner_ref[pl.ds(turn, 1), :], (ROWS, LANES))
        sign = jnp.broadcast_to(orient_ref[pl.ds(turn, 1), :], (8, LANES))
        y = jnp.take_along_axis(x, other, axis=1)
        vy = jnp.take_along_axis(v, other, axis=1)
        contrast = lane_sum(y * y) - lane_sum(x * x)
        inner = lane_sum(x * y)
        toward = jnp.where(contrast > 0.0, -1.0, jnp.where(contrast < 0.0, 1.0, sign))
        d = jnp.abs(contrast) + jnp.sqrt(contrast * contrast + 4.0 * inner * inner)
        positive = d > 0.0
        tangent = jnp.where(
            positive, 2.0 * inner * toward / jnp.where(positive, d, 1.0), 0.0
        )
        cosine = lax.rsqrt(1.0 + tangent * tangent)
        sine = spread(cosine * tangent)
        cosine = spread(cosine)
        return cosine * x + sine * y, cosine * v + sine * vy

    eye = jnp.where(row == lane, 1.0, 0.0)
    x, v = lax.fori_loop(0, SWEEPS * (COUNT - 1), turn_step, (upper, eye))
    keep = jnp.broadcast_to(keep_ref[...], (ROWS, LANES))
    sigma_ref[...] = jnp.take_along_axis(jnp.sqrt(lane_sum(x * x)), keep[0:8], axis=1)
    v = jnp.take_along_axis(v, keep, axis=1)
    high = v.astype(jnp.bfloat16).astype(jnp.float32)
    low = v - high
    mix = jnp.concatenate([high, high, low, jnp.zeros((8, LANES), jnp.float32)], axis=0)
    mix_ref[...] = jnp.transpose(mix)[0:MODES]


def factor(parts):
    tables = [near(jnp.asarray(table)) for table in pair_tables()]
    return pl.pallas_call(
        factor_kernel,
        in_specs=[VMEM_SPEC] * 7,
        out_specs=(VMEM_SPEC, VMEM_SPEC),
        out_shape=(
            pltpu.VMEM((MODES, LANES), jnp.float32),
            pltpu.VMEM((8, LANES), jnp.float32),
        ),
        compiler_params=pltpu.CompilerParams(vmem_limit_bytes=4 << 20),
        name="factor",
    )(*[near(x) for x in parts], *tables)


def turned_mix(mix, here):
    lane = lax.broadcasted_iota(jnp.int32, mix.shape, 1)
    inside = lax.rem(lane, ROWS)
    turned = lane - inside + PAD + lax.rem(inside + (MODES - PAD) + PAD * here, MODES)
    source = jnp.where((inside < PAD) | (lane >= 3 * ROWS), lane, turned)
    return jnp.take_along_axis(mix, source, axis=1).astype(jnp.bfloat16)


def mix_rows(mix_ref, here, g):
    at = pl.multiple_of(PAD * lax.rem(here + g, 4), PAD)
    return mix_ref[pl.ds(at, PAD), :]


def mixed(mix, stack):
    high = stack.astype(jnp.bfloat16).astype(jnp.float32)
    zero = jnp.zeros((8, stack.shape[1]), jnp.float32)
    joined = jnp.concatenate([high, stack - high, high, zero], axis=0)
    return jnp.dot(mix, joined.astype(jnp.bfloat16), preferred_element_type=jnp.float32)


def update_kernel(here_ref, mix_ref, *refs, chunk):
    stack_refs, out_refs = refs[:5], refs[5:]
    here = here_ref[0]
    mix = jnp.concatenate([mix_rows(mix_ref, here, g) for g in range(4)], axis=0)
    mix = turned_mix(mix, here)
    for start in range(0, out_refs[0].shape[1], chunk):
        first = SHARED + start
        out = mixed(mix, stacked(stack_refs, slice(first, first + chunk)))
        for g, ref in enumerate(out_refs):
            ref[:, start : start + chunk] = out[PAD * g : PAD * g + PAD]


def update(here, mix, stack, chunk=1024):
    cols = stack[0].shape[1] - SHARED
    return pl.pallas_call(
        functools.partial(update_kernel, chunk=chunk),
        in_specs=[SMEM_SPEC] + [VMEM_SPEC] * 6,
        out_specs=[VMEM_SPEC] * 4,
        out_shape=[pltpu.VMEM((PAD, cols), jnp.float32)] * 4,
        compiler_params=pltpu.CompilerParams(vmem_limit_bytes=8 << 20),
        name="update",
    )(here, near(mix), *[near(x) for x in stack])


def own_kernel(here_ref, mix_ref, *refs, cols, chunk):
    stack_refs, (hi_ref, over_ref, lo_ref) = refs[:5], refs[5:8]
    basis_hbm, out_hbm, mine, snap, buf, in_sems, out_sems = refs[8:]
    here = here_ref[0]
    tiles = SHARED // LANES
    blocks = [lax.rem(here + 1 + b, 4) for b in range(4)]
    reads = []
    for b in range(3):
        at = pl.multiple_of(blocks[b] * cols, LANES)
        source = basis_hbm.at[:, pl.ds(at, SHARED)]
        reads.append(pltpu.make_async_copy(source, mine.at[b], in_sems.at[b]))
    for copy in reads:
        copy.start()
    mix = turned_mix(mix_rows(mix_ref, here, 0), here)
    for b, ref in enumerate((hi_ref, over_ref, lo_ref)):
        snap[b] = jnp.zeros((PAD, SHARED), jnp.float32)
        for k in range(2 * tiles):
            which, tile = divmod(k, tiles)
            at = 3 * SHARED + k // 8 * LANES
            line = ref[k % 8 : k % 8 + 1, at : at + LANES]
            snap[b, which : which + 1, tile * LANES : (tile + 1) * LANES] = line
    for copy in reads:
        copy.wait()
    writes = []
    for b in range(4):
        for start in range(0, SHARED, chunk):
            at = slice(start, start + chunk)
            if b == 3:
                stack = stacked(stack_refs, at)
            else:
                wide = slice(b * SHARED + start, b * SHARED + start + chunk)
                rows = [snap[b, :, at], mine[b, :, at]]
                rows += [ref[:, wide] for ref in (hi_ref, over_ref, lo_ref)]
                stack = jnp.concatenate(rows, axis=0)
            buf[b, :, at] = mixed(mix, stack)
        target = pl.ds(pl.multiple_of(blocks[b] * cols, LANES), SHARED)
        writes.append(pltpu.make_async_copy(buf.at[b], out_hbm.at[:, target], out_sems.at[b]))
        writes[-1].start()
    for copy in writes:
        copy.wait()


def own(here, mix, stack, received, basis, chunk=1024):
    cols = basis.shape[1] // 4
    return pl.pallas_call(
        functools.partial(own_kernel, cols=cols, chunk=chunk),
        in_specs=[SMEM_SPEC] + [VMEM_SPEC] * 9 + [HBM_SPEC],
        out_specs=HBM_SPEC,
        out_shape=pltpu.HBM(basis.shape, jnp.float32),
        scratch_shapes=[
            pltpu.VMEM((3, PAD, SHARED), jnp.float32),
            pltpu.VMEM((3, PAD, SHARED), jnp.float32),
            pltpu.VMEM((4, PAD, SHARED), jnp.float32),
            pltpu.SemaphoreType.DMA((3,)),
            pltpu.SemaphoreType.DMA((4,)),
        ],
        compiler_params=pltpu.CompilerParams(vmem_limit_bytes=10 << 20),
        name="own",
    )(here, *[near(x) for x in (mix, *stack, *received)], far(basis))


def join_kernel(here_ref, *refs):
    parts, (_, out_hbm, sems) = refs[:4], refs[4:]
    cols = out_hbm.shape[1] // 4
    copies = []
    for g, part in enumerate(parts):
        at = pl.multiple_of(lax.rem(here_ref[0] + g, 4) * cols + SHARED, LANES)
        target = out_hbm.at[:, pl.ds(at, cols - SHARED)]
        copies.append(pltpu.make_async_copy(part, target, sems.at[g]))
        copies[-1].start()
    for copy in copies:
        copy.wait()


def join(here, parts, whole):
    return pl.pallas_call(
        join_kernel,
        in_specs=[SMEM_SPEC] + [VMEM_SPEC] * 4 + [HBM_SPEC],
        out_specs=HBM_SPEC,
        out_shape=pltpu.HBM(whole.shape, jnp.float32),
        scratch_shapes=[pltpu.SemaphoreType.DMA((4,))],
        input_output_aliases={5: 0},
        compiler_params=pltpu.CompilerParams(vmem_limit_bytes=2 << 20),
        name="join",
    )(here, *[near(x) for x in parts], far(whole))


def program(velocity, basis, levels, profile_index, advect):
    n_space, n_mode = lax.axis_size("space"), lax.axis_size("mode")
    comps, cx, _, _ = velocity.shape
    here = lax.axis_index("mode").astype(jnp.int32).reshape(1)

    def shifted(x, axis, by):
        size = lax.axis_size(axis)
        return lax.ppermute(x, axis, [(i, (i + by) % size) for i in range(size)])

    face_lo, face_hi, plane_lo, plane_hi, *blocks = pack(here, velocity, basis)
    zlo = shifted(face_hi, "mode", 1)
    zhi = shifted(face_lo, "mode", -1)
    lo = shifted(blocks[1], "mode", 1)
    hi = shifted(blocks[3], "mode", -1)
    over = shifted(blocks[2], "mode", 2)
    plane_lo, plane_hi = add_corners(zlo, zhi, plane_lo, plane_hi, cx, comps)
    xlo = shifted(plane_hi, "space", 1)
    xhi = shifted(plane_lo, "space", -1)
    snap, plus, minus, across = snapshots(
        velocity,
        levels,
        profile_index,
        advect,
        here,
        basis,
        (zlo, zhi, face_lo, face_hi, velocity, xlo, xhi),
    )
    stack = (snap, blocks[0], hi, over, lo)
    total = gram(here, stack)
    total = ring_sum(total, ring_parts(total, "space", n_space, 1, 2))
    total = ring_sum(total, ring_parts(total, "mode", n_mode, 1, n_mode))
    total = ring_sum(total, ring_parts(total, "space", n_space, 2, 4))
    lo_early = shifted(plus, "mode", 1)
    hi_early = shifted(minus, "mode", -1)
    over_early = shifted(across, "mode", 2)
    parts = [total] + ring_parts(total, "space", n_space, 8, 4)
    mix, sigma = factor(parts)
    out_own, out_next, out_over, out_prev = update(here, mix, stack)
    back_lo = shifted(out_next, "mode", 1)
    back_hi = shifted(out_prev, "mode", -1)
    back_over = shifted(out_over, "mode", 2)
    mine = own(here, mix, stack, (hi_early, over_early, lo_early), basis)
    modes = join(here, (out_own, back_hi, back_over, back_lo), mine)
    return (modes, sigma[0, :MODES])


def solution(mesh):
    return jax.shard_map(
        program,
        mesh=mesh,
        in_specs=(P(None, "space", "mode", None), P("mode", "space"), P(), P(), P()),
        out_specs=(P("mode", "space"), P()),
        check_vma=False,
    )
```

```python
import functools

import jax
import jax.numpy as jnp
import numpy as np
from jax import lax
from jax.experimental import pallas as pl
from jax.experimental.pallas import tpu as pltpu
from jax.sharding import PartitionSpec as P

STRIDE = 4
MODES = 32
SWEEPS = 2
FACTOR_BLOCK = 8
COUNT = 34
ROWS = 40
LANES = 128
PAD = 8
VMEM_SPEC = pl.BlockSpec(memory_space=pltpu.VMEM)
HBM_SPEC = pl.BlockSpec(memory_space=pltpu.HBM)
SMEM_SPEC = pl.BlockSpec(memory_space=pltpu.SMEM)


SHARED = 6144
FOLD = SHARED // 4

PLACE = np.array([0, 1] + list(range(PAD, PAD + MODES)))


def near(x):
    return pltpu.with_memory_space_constraint(x, pltpu.VMEM)


def far(x):
    return pltpu.with_memory_space_constraint(x, pltpu.HBM)


def pair_tables():
    rounds = COUNT - 1
    partner = np.tile(np.arange(LANES, dtype=np.int32), (ROWS, 1))
    orient = np.ones((ROWS, LANES), np.float32)
    for turn in range(rounds):
        players = [0] + [1 + (i - 1 + turn) % rounds for i in range(1, COUNT)]
        for k in range(COUNT // 2):
            lead, trail = PLACE[players[k]], PLACE[players[COUNT - 1 - k]]
            partner[turn, lead] = trail
            partner[turn, trail] = lead
            orient[turn, lead] = -1.0
    keep = np.zeros((1, LANES), np.int32)
    keep[0, :MODES] = PLACE[:MODES]
    return partner, orient, keep


def pack_kernel(
    here_ref,
    vel_hbm,
    basis_hbm,
    zfirst_ref,
    zlast_ref,
    xfirst_ref,
    xlast_ref,
    mine_ref,
    next_ref,
    far_ref,
    prev_ref,
    next_tail_ref,
    prev_tail_ref,
    buf,
    edge_sems,
    face_sems,
    block_sems,
):
    comps, cx, cz, _ = vel_hbm.shape
    cols = mine_ref.shape[1]
    edges, rest = [], []
    for c in range(comps):
        for side, at in enumerate((0, cz - PAD)):
            source = vel_hbm.at[c, :, pl.ds(at, PAD), :]
            edges.append(pltpu.make_async_copy(source, buf.at[c, side], edge_sems.at[c, side]))
        for side, (at, ref) in enumerate(((0, xfirst_ref), (cx - 2, xlast_ref))):
            for k in range(2):
                source = vel_hbm.at[c, at + k]
                target = ref.at[pl.ds((2 * c + k) * cz, cz)]
                rest.append(pltpu.make_async_copy(source, target, face_sems.at[c, side, k]))
    targets = (
        (0, 0, mine_ref),
        (1, 0, next_ref),
        (2, 0, far_ref),
        (3, 0, prev_ref),
        (1, SHARED, next_tail_ref),
        (3, SHARED, prev_tail_ref),
    )
    for i, (k, skip, ref) in enumerate(targets):
        at = pl.multiple_of(lax.rem(here_ref[0] + k, 4) * cols + skip, LANES)
        source = basis_hbm.at[:, pl.ds(at, ref.shape[1])]
        rest.append(pltpu.make_async_copy(source, ref, block_sems.at[i]))
    for copy in edges + rest:
        copy.start()
    for copy in edges:
        copy.wait()
    for c in range(comps):
        for i in range(cx):
            for k in range(2):
                row, last = (2 * c + k) * cx + i, PAD - 2 + k
                zfirst_ref[row : row + 1, :] = buf[c, 0, i, k : k + 1, :]
                zlast_ref[row : row + 1, :] = buf[c, 1, i, last : last + 1, :]
    for copy in rest:
        copy.wait()


def pack(here, velocity, basis):
    comps, cx, cz, ny = velocity.shape
    edge = pltpu.VMEM((comps * 2 * cx, ny), jnp.float32)
    face = pltpu.VMEM((comps * 2 * cz + PAD, ny), jnp.float32)
    cols = basis.shape[1] // 4
    block, head, tail = (
        pltpu.VMEM((PAD, size), jnp.float32) for size in (cols, SHARED, cols - SHARED)
    )
    return pl.pallas_call(
        pack_kernel,
        in_specs=[SMEM_SPEC, HBM_SPEC, HBM_SPEC],
        out_specs=[VMEM_SPEC] * 10,
        out_shape=[edge, edge, face, face, block, head, block, head, tail, tail],
        scratch_shapes=[
            pltpu.VMEM((comps, 2, cx, PAD, ny), jnp.float32),
            pltpu.SemaphoreType.DMA((comps, 2)),
            pltpu.SemaphoreType.DMA((comps, 2, 2)),
            pltpu.SemaphoreType.DMA((6,)),
        ],
        compiler_params=pltpu.CompilerParams(vmem_limit_bytes=4 << 20),
        name="pack",
    )(here, far(velocity), far(basis))


def corner_kernel(zlo_ref, zhi_ref, _, __, xfirst_ref, xlast_ref, *, cx, comps):
    base = xfirst_ref.shape[0] - PAD
    zero = jnp.zeros((PAD, xfirst_ref.shape[1]), jnp.float32)
    for ref, plane in ((xfirst_ref, 0), (xlast_ref, cx - 1)):
        ref[base:, :] = zero
        for c in range(comps):
            low, high = (2 * c + 1) * cx + plane, 2 * c * cx + plane
            at = base + 2 * c
            ref[at : at + 1, :] = zlo_ref[low : low + 1, :]
            ref[at + 1 : at + 2, :] = zhi_ref[high : high + 1, :]


def add_corners(zlo, zhi, first, last, cx, comps):
    face = pltpu.VMEM(first.shape, jnp.float32)
    return pl.pallas_call(
        functools.partial(corner_kernel, cx=cx, comps=comps),
        in_specs=[VMEM_SPEC] * 4,
        out_specs=[VMEM_SPEC] * 2,
        out_shape=[face, face],
        input_output_aliases={2: 0, 3: 1},
        compiler_params=pltpu.CompilerParams(vmem_limit_bytes=1 << 20),
        name="corners",
    )(*[near(x) for x in (zlo, zhi, first, last)])


def coefficients(levels_ref, index_ref, advect_ref):
    index = index_ref[...]
    visc = jnp.zeros(index.shape, jnp.float32)
    for level in range(levels_ref.shape[0]):
        visc = jnp.where(index == level, levels_ref[level], visc)
    cells = index.shape[1]
    lane = lax.broadcasted_iota(jnp.int32, index.shape, 1)
    first, last = lane == 0, lane == cells - 1
    up = jnp.where(last, visc, 0.5 * (visc + pltpu.roll(visc, cells - 1, 1)))
    down = jnp.where(first, visc, 0.5 * (visc + pltpu.roll(visc, 1, 1)))
    half = 0.5 * advect_ref[...]
    return (
        1.0 - 4.0 * visc - up - down,
        visc,
        visc - half,
        visc + half,
        jnp.where(last, 0.0, up),
        jnp.where(first, 0.0, down),
    )


def step(coefs, center, east, west, north, south):
    mid, visc, c_east, c_west, c_up, c_down = coefs
    cells = center.shape[-1]
    upward = pltpu.roll(center, cells - 1, 1)
    downward = pltpu.roll(center, 1, 1)
    return (
        mid * center
        + visc * (north + south)
        + c_east * east
        + c_west * west
        + c_up * upward
        + c_down * downward
    )


def split3(x):
    high = x.astype(jnp.bfloat16)
    rest = x - high.astype(jnp.float32)
    middle = rest.astype(jnp.bfloat16)
    low = (rest - middle.astype(jnp.float32)).astype(jnp.bfloat16)
    return high, middle, low


def offer_copies(here, basis_hbm, refs, sems):
    cols = basis_hbm.shape[1] // 4
    copies = []
    for side, (ref, skip, count) in enumerate(zip(refs, (2, 0, 0), (3, 3, 1))):
        for k in range(count):
            at = pl.multiple_of(lax.rem(here + skip + k, 4) * cols, LANES)
            source = basis_hbm.at[:, pl.ds(at, SHARED)]
            target = ref.at[:, pl.ds(k * SHARED, SHARED)]
            copies.append(pltpu.make_async_copy(source, target, sems.at[side, k]))
    return copies


def stencil_kernel(
    levels_ref,
    index_ref,
    advect_ref,
    sum_ref,
    zlo_ref,
    zhi_ref,
    face_lo_ref,
    face_hi_ref,
    here_ref,
    basis_hbm,
    vel_hbm,
    xlo_ref,
    xhi_ref,
    out_ref,
    plus_ref,
    minus_ref,
    over_ref,
    field,
    first,
    boxed,
    sems,
    offer_sems,
):
    comp = pl.program_id(0)
    offer_refs = (plus_ref, minus_ref, over_ref)
    offers = offer_copies(here_ref[0], basis_hbm, offer_refs, offer_sems)
    cx, cz, ny = vel_hbm.shape[1:]
    inner = pl.ds(PAD, cz)

    def copies(c):
        return (
            pltpu.make_async_copy(
                vel_hbm.at[c], field.at[c, pl.ds(2, cx), inner, :], sems.at[c, 0, 0]
            ),
            *[
                pltpu.make_async_copy(
                    ref.at[pl.ds((2 * c + k) * cz, cz)],
                    field.at[c, at + k, inner, :],
                    sems.at[c, 1 + side, k],
                )
                for side, (at, ref) in enumerate(((0, xlo_ref), (cx + 2, xhi_ref)))
                for k in range(2)
            ],
        )

    @pl.when(comp == 0)
    def _():
        for c in range(3):
            for copy in copies(c):
                copy.start()
        for copy in offers:
            copy.start()

    @pl.when(comp == pl.num_programs(0) - 1)
    def _():
        for copy in offers:
            copy.wait()

    coefs = coefficients(levels_ref, index_ref, advect_ref)

    def edge_row(ref, k):
        return ref[pl.ds(pl.multiple_of((2 * comp + k) * cx, 8), cx), :]

    zlo2, zlo1 = edge_row(zlo_ref, 0), edge_row(zlo_ref, 1)
    zhi1, zhi2 = edge_row(zhi_ref, 0), edge_row(zhi_ref, 1)
    spot = 6 * cz + 2 * comp
    lo_before, lo_after = xlo_ref[pl.ds(spot, 1), :], xhi_ref[pl.ds(spot, 1), :]
    hi_before, hi_after = xlo_ref[pl.ds(spot + 1, 1), :], xhi_ref[pl.ds(spot + 1, 1), :]
    plane = lax.broadcasted_iota(jnp.int32, (cx, ny), 0)

    def edge(row, before, after, north, south):
        east = jnp.where(plane == cx - 1, after, pltpu.roll(row, cx - 1, 0))
        west = jnp.where(plane == 0, before, pltpu.roll(row, 1, 0))
        return step(coefs, row, east, west, north, south)

    edge_lo = edge(zlo1, lo_before, lo_after, zlo2, edge_row(face_lo_ref, 0))
    edge_hi = edge(zhi1, hi_before, hi_after, edge_row(face_hi_ref, 1), zhi2)
    for i in range(cx):
        field[comp, 2 + i, PAD - 1 : PAD, :] = zlo1[i : i + 1]
        field[comp, 2 + i, PAD + cz : PAD + cz + 1, :] = zhi1[i : i + 1]
        first[1 + i, PAD - 1 : PAD, :] = edge_lo[i : i + 1]
        first[1 + i, PAD + cz : PAD + cz + 1, :] = edge_hi[i : i + 1]
    field[comp, 1, PAD - 1 : PAD, :] = lo_before
    field[comp, 1, PAD + cz : PAD + cz + 1, :] = hi_before
    field[comp, cx + 2, PAD - 1 : PAD, :] = lo_after
    field[comp, cx + 2, PAD + cz : PAD + cz + 1, :] = hi_after

    for copy in copies(comp):
        copy.wait()

    chunk = 16

    def first_plane(p, carry):
        for k in range(cz // chunk):
            at = PAD + k * chunk
            rows = pl.ds(at, chunk)
            first[p, rows, :] = step(
                coefs,
                field[comp, p + 1, rows, :],
                field[comp, p + 2, rows, :],
                field[comp, p, rows, :],
                field[comp, p + 1, pl.ds(at - 1, chunk), :],
                field[comp, p + 1, pl.ds(at + 1, chunk), :],
            )
        return carry

    lax.fori_loop(0, cx + 2, first_plane, 0)

    sums = sum_ref[...]
    lane = lax.broadcasted_iota(jnp.int32, (cz, LANES), 1)
    row = lax.broadcasted_iota(jnp.int32, (cz, LANES), 0)
    wanted = (lane // (LANES // 2)) == ((row // STRIDE) % 2)
    part = out_ref.shape[1] // vel_hbm.shape[0]
    offset = pl.multiple_of(comp * part, LANES)
    out_ref[:, pl.ds(offset, part)] = jnp.zeros((PAD, part), jnp.float32)

    def coarse(which, box):
        total = sum(
            jnp.dot(part, sums, preferred_element_type=jnp.float32)
            for part in split3(boxed[...])
        )
        total = jnp.where(wanted, total, 0.0)
        base = offset + box * (cz // 8 * LANES)
        for r in range(cz // 8):
            line = jnp.sum(total[8 * r : 8 * r + 8], axis=0, keepdims=True) * 0.125
            at = pl.multiple_of(base + r * LANES, LANES)
            out_ref[which : which + 1, pl.ds(at, LANES)] = line

    def box_step(box, carry):
        start = 1 + STRIDE * box
        for k in range(cz // chunk):
            rows = pl.ds(PAD + k * chunk, chunk)
            boxed[pl.ds(k * chunk, chunk), :] = (
                first[start, rows, :] + first[start + 1, rows, :]
            ) + (first[start + 2, rows, :] + first[start + 3, rows, :])
        coarse(0, box)
        for k in range(cz // chunk):
            at = PAD + k * chunk
            rows = pl.ds(at, chunk)
            total = None
            for i in range(STRIDE):
                p = start + i
                value = step(
                    coefs,
                    first[p, rows, :],
                    first[p + 1, rows, :],
                    first[p - 1, rows, :],
                    first[p, pl.ds(at - 1, chunk), :],
                    first[p, pl.ds(at + 1, chunk), :],
                )
                total = value if total is None else total + value
            boxed[pl.ds(k * chunk, chunk), :] = total
        coarse(1, box)
        return carry

    lax.fori_loop(0, cx // STRIDE, box_step, 0)

    @pl.when(comp == 0)
    def _():
        tiles = SHARED // LANES
        for k in range(2 * tiles):
            which, tile = divmod(k, tiles)
            line = out_ref[which : which + 1, tile * LANES : (tile + 1) * LANES]
            for ref in offer_refs:
                at = ref.shape[1] - FOLD + k // 8 * LANES
                ref[k % 8 : k % 8 + 1, at : at + LANES] = line


def snapshots(velocity, levels, profile_index, advect, here, basis, halos):
    comps, cx, cz, ny = velocity.shape
    cols = (cx // STRIDE) * (cz // STRIDE) * (ny // STRIDE)
    half = LANES // 2
    sums = np.zeros((ny, LANES), np.float32)
    for y in range(ny):
        sums[y, y // STRIDE] = 1.0
        sums[y, half + y // STRIDE] = 1.0
    return pl.pallas_call(
        stencil_kernel,
        grid=(comps,),
        in_specs=[
            SMEM_SPEC,
            pl.BlockSpec((1, ny), lambda c: (0, 0)),
            pl.BlockSpec((1, ny), lambda c: (0, 0)),
            pl.BlockSpec((ny, LANES), lambda c: (0, 0)),
            *[VMEM_SPEC] * 4,
            SMEM_SPEC,
            HBM_SPEC,
            HBM_SPEC,
            VMEM_SPEC,
            VMEM_SPEC,
        ],
        out_specs=[VMEM_SPEC] * 4,
        out_shape=[pltpu.VMEM((PAD, comps * cols), jnp.float32)]
        + [pltpu.VMEM((PAD, k * SHARED + FOLD), jnp.float32) for k in (3, 3, 1)],
        scratch_shapes=[
            pltpu.VMEM((comps, cx + 4, cz + 2 * PAD, ny), jnp.float32),
            pltpu.VMEM((cx + 2, cz + 2 * PAD, ny), jnp.float32),
            pltpu.VMEM((cz, ny), jnp.float32),
            pltpu.SemaphoreType.DMA((comps, 3, 2)),
            pltpu.SemaphoreType.DMA((3, 3)),
        ],
        compiler_params=pltpu.CompilerParams(vmem_limit_bytes=20 << 20),
        name="stencil",
    )(
        levels,
        profile_index.reshape(1, ny),
        advect.reshape(1, ny),
        jnp.asarray(sums, jnp.bfloat16),
        *[near(x) for x in halos[:4]],
        here,
        far(basis),
        far(halos[4]),
        *[near(x) for x in halos[5:]],
    )


def stacked(pieces, start, size):
    rows = []
    for piece in pieces:
        if isinstance(piece, tuple):
            ref, at = (piece[0], start) if start < SHARED else (piece[1], start - SHARED)
        else:
            ref, at = piece, start
        rows.append(ref[:, at : at + size])
    return jnp.concatenate(rows, axis=0)


def pieces_of(refs):
    snap, mine, hi, hi_tail, far_block, lo, lo_tail = refs
    return [snap, mine, (hi, hi_tail), far_block, (lo, lo_tail)]


def gram_kernel(here_ref, *refs, chunk):
    pieces, out_ref = pieces_of(refs[:-1]), refs[-1]
    here = here_ref[0]
    n, acc = ROWS, None
    for start in range(0, pieces[0].shape[1], chunk):
        stack = stacked(pieces, start, chunk)
        high = stack.astype(jnp.bfloat16).astype(jnp.float32)
        joined = jnp.concatenate([high, stack - high], axis=0).astype(jnp.bfloat16)
        part = lax.dot_general(
            joined, joined, (((1,), (1,)), ((), ())), preferred_element_type=jnp.float32
        )
        acc = part if acc is None else acc + part
    cross = acc[0:n, n : 2 * n] + acc[n : 2 * n, 0:n]
    total = acc[0:n, 0:n] + (cross + acc[n : 2 * n, n : 2 * n])
    total = jnp.concatenate([total, jnp.zeros((n, LANES - n), jnp.float32)], axis=1)
    lane = lax.broadcasted_iota(jnp.int32, (n, LANES), 1)
    turned = PAD + lax.rem(lane - PAD + MODES - PAD * here + MODES, MODES)
    inside = (lane >= PAD) & (lane < n)
    total = jnp.take_along_axis(total, jnp.where(inside, turned, lane), axis=1)
    out_ref[0:PAD, :] = total[0:PAD]
    for g in range(4):
        at = pl.multiple_of(PAD + PAD * lax.rem(here + g, 4), PAD)
        out_ref[pl.ds(at, PAD), :] = total[PAD + PAD * g : 2 * PAD + PAD * g]


def gram(here, stack, chunk=2048):
    return pl.pallas_call(
        functools.partial(gram_kernel, chunk=chunk),
        in_specs=[SMEM_SPEC] + [VMEM_SPEC] * 7,
        out_specs=VMEM_SPEC,
        out_shape=pltpu.VMEM((ROWS, LANES), jnp.float32),
        compiler_params=pltpu.CompilerParams(vmem_limit_bytes=8 << 20),
        name="gram",
    )(here, *[near(x) for x in stack])


def ring_moves(size, stride, width):
    moves = []
    for shift in range(1, width):
        pairs = []
        for i in range(size):
            k = (i // stride) % width
            pairs.append((i, i + ((k + shift) % width - k) * stride))
        moves.append(pairs)
    return moves


def ring_parts(x, axis, size, stride, width):
    return [lax.ppermute(x, axis, pairs) for pairs in ring_moves(size, stride, width)]


def ring_sum(x, parts):
    if len(parts) == 1:
        return x + parts[0]
    one, two, three = parts
    return (x + two) + (one + three)


def lane_sum(x):
    total = x[0:8]
    for k in range(1, ROWS // 8):
        total = total + x[8 * k : 8 * k + 8]
    total = total + pltpu.roll(total, 4, 0)
    total = total + pltpu.roll(total, 2, 0)
    return total + pltpu.roll(total, 1, 0)


def spread(x):
    return jnp.concatenate([x] * (ROWS // 8), axis=0)


def factor_kernel(
    g0_ref, g1_ref, g2_ref, g3_ref, partner_ref, orient_ref, keep_ref, mix_ref, sigma_ref
):
    a = (g0_ref[...] + g2_ref[...]) + (g1_ref[...] + g3_ref[...])
    lane = lax.broadcasted_iota(jnp.int32, (ROWS, LANES), 1)
    row = lax.broadcasted_iota(jnp.int32, (ROWS, LANES), 0)
    upper = jnp.zeros((ROWS, LANES), jnp.float32)
    places = [int(k) for k in PLACE]
    while places:
        block, places = places[:FACTOR_BLOCK], places[FACTOR_BLOCK:]
        lines = [jnp.broadcast_to(a[j : j + 1, :], (8, LANES)) for j in block]
        columns = [jnp.broadcast_to(a[:, j : j + 1], (ROWS, LANES)) for j in block]

        def entry(column, j):
            return jnp.broadcast_to(column[j : j + 1, :], (8, LANES))

        for i, j in enumerate(block):
            scale = lax.rsqrt(entry(columns[i], j))
            lines[i] = lines[i] * scale
            columns[i] = columns[i] * spread(scale)
            for k in range(i + 1, len(block)):
                cross = entry(columns[i], block[k])
                lines[k] = lines[k] - cross * lines[i]
                columns[k] = columns[k] - spread(cross) * columns[i]
        for i, j in enumerate(block):
            line = spread(lines[i])
            a = a - columns[i] * line
            upper = jnp.where((row == j) & (lane >= j), line, upper)

    def turn_step(i, state):
        x, v = state
        turn = lax.rem(i, COUNT - 1)
        other = jnp.broadcast_to(partner_ref[pl.ds(turn, 1), :], (ROWS, LANES))
        sign = jnp.broadcast_to(orient_ref[pl.ds(turn, 1), :], (8, LANES))
        y = jnp.take_along_axis(x, other, axis=1)
        vy = jnp.take_along_axis(v, other, axis=1)
        contrast = lane_sum(y * y) - lane_sum(x * x)
        inner = lane_sum(x * y)
        toward = jnp.where(contrast > 0.0, -1.0, jnp.where(contrast < 0.0, 1.0, sign))
        d = jnp.abs(contrast) + jnp.sqrt(contrast * contrast + 4.0 * inner * inner)
        positive = d > 0.0
        tangent = jnp.where(
            positive, 2.0 * inner * toward / jnp.where(positive, d, 1.0), 0.0
        )
        cosine = lax.rsqrt(1.0 + tangent * tangent)
        sine = spread(cosine * tangent)
        cosine = spread(cosine)
        return cosine * x + sine * y, cosine * v + sine * vy

    eye = jnp.where(row == lane, 1.0, 0.0)
    x, v = lax.fori_loop(0, SWEEPS * (COUNT - 1), turn_step, (upper, eye))
    keep = jnp.broadcast_to(keep_ref[...], (ROWS, LANES))
    sigma_ref[...] = jnp.take_along_axis(jnp.sqrt(lane_sum(x * x)), keep[0:8], axis=1)
    v = jnp.take_along_axis(v, keep, axis=1)
    high = v.astype(jnp.bfloat16).astype(jnp.float32)
    low = v - high
    mix = jnp.concatenate([high, high, low, jnp.zeros((8, LANES), jnp.float32)], axis=0)
    mix_ref[...] = jnp.transpose(mix)[0:MODES]


def factor(parts):
    tables = [near(jnp.asarray(table)) for table in pair_tables()]
    return pl.pallas_call(
        factor_kernel,
        in_specs=[VMEM_SPEC] * 7,
        out_specs=(VMEM_SPEC, VMEM_SPEC),
        out_shape=(
            pltpu.VMEM((MODES, LANES), jnp.float32),
            pltpu.VMEM((8, LANES), jnp.float32),
        ),
        compiler_params=pltpu.CompilerParams(vmem_limit_bytes=4 << 20),
        name="factor",
    )(*[near(x) for x in parts], *tables)


def turned_mix(mix, here):
    lane = lax.broadcasted_iota(jnp.int32, mix.shape, 1)
    inside = lax.rem(lane, ROWS)
    turned = lane - inside + PAD + lax.rem(inside + (MODES - PAD) + PAD * here, MODES)
    source = jnp.where((inside < PAD) | (lane >= 3 * ROWS), lane, turned)
    return jnp.take_along_axis(mix, source, axis=1).astype(jnp.bfloat16)


def mix_rows(mix_ref, here, g):
    at = pl.multiple_of(PAD * lax.rem(here + g, 4), PAD)
    return mix_ref[pl.ds(at, PAD), :]


def mixed(mix, stack):
    high = stack.astype(jnp.bfloat16).astype(jnp.float32)
    zero = jnp.zeros((8, stack.shape[1]), jnp.float32)
    joined = jnp.concatenate([high, stack - high, high, zero], axis=0)
    return jnp.dot(mix, joined.astype(jnp.bfloat16), preferred_element_type=jnp.float32)


def update_kernel(here_ref, mix_ref, *refs, chunk):
    pieces, out_refs = pieces_of(refs[:7]), refs[7:]
    here = here_ref[0]
    mix = jnp.concatenate([mix_rows(mix_ref, here, g) for g in range(4)], axis=0)
    mix = turned_mix(mix, here)
    for start in range(0, out_refs[0].shape[1], chunk):
        out = mixed(mix, stacked(pieces, SHARED + start, chunk))
        for g, ref in enumerate(out_refs):
            ref[:, start : start + chunk] = out[PAD * g : PAD * g + PAD]


def update(here, mix, stack, chunk=1024):
    cols = stack[0].shape[1] - SHARED
    return pl.pallas_call(
        functools.partial(update_kernel, chunk=chunk),
        in_specs=[SMEM_SPEC] + [VMEM_SPEC] * 8,
        out_specs=[VMEM_SPEC] * 4,
        out_shape=[pltpu.VMEM((PAD, cols), jnp.float32)] * 4,
        compiler_params=pltpu.CompilerParams(vmem_limit_bytes=8 << 20),
        name="update",
    )(here, near(mix), *[near(x) for x in stack])


def own_kernel(here_ref, mix_ref, *refs, cols, chunk):
    pieces, (hi_ref, over_ref, lo_ref, hi_far_ref, lo_far_ref) = pieces_of(refs[:7]), refs[7:12]
    basis_hbm, out_hbm, mine, snap, buf, in_sems, out_sems = refs[12:]
    here = here_ref[0]
    tiles = SHARED // LANES
    blocks = [lax.rem(here + 1 + b, 4) for b in range(4)]
    reads = []
    for b in range(3):
        at = pl.multiple_of(blocks[b] * cols, LANES)
        source = basis_hbm.at[:, pl.ds(at, SHARED)]
        reads.append(pltpu.make_async_copy(source, mine.at[b], in_sems.at[b]))
    for copy in reads:
        copy.start()
    mix = turned_mix(mix_rows(mix_ref, here, 0), here)
    for b, ref in enumerate((hi_ref, over_ref, lo_ref)):
        snap[b] = jnp.zeros((PAD, SHARED), jnp.float32)
        for k in range(2 * tiles):
            which, tile = divmod(k, tiles)
            at = ref.shape[1] - FOLD + k // 8 * LANES
            line = ref[k % 8 : k % 8 + 1, at : at + LANES]
            snap[b, which : which + 1, tile * LANES : (tile + 1) * LANES] = line
    for copy in reads:
        copy.wait()
    writes = []
    for b in range(4):
        for start in range(0, SHARED, chunk):
            at = slice(start, start + chunk)
            if b == 3:
                stack = stacked(pieces, start, chunk)
            else:
                wide = slice(b * SHARED + start, b * SHARED + start + chunk)
                opposite = (hi_far_ref, over_ref, lo_far_ref)[b]
                rows = [snap[b, :, at], mine[b, :, at]]
                rows += [hi_ref[:, wide], opposite[:, at], lo_ref[:, wide]]
                stack = jnp.concatenate(rows, axis=0)
            buf[b, :, at] = mixed(mix, stack)
        target = pl.ds(pl.multiple_of(blocks[b] * cols, LANES), SHARED)
        writes.append(pltpu.make_async_copy(buf.at[b], out_hbm.at[:, target], out_sems.at[b]))
        writes[-1].start()
    for copy in writes:
        copy.wait()


def own(here, mix, stack, received, basis, chunk=1024):
    cols = basis.shape[1] // 4
    return pl.pallas_call(
        functools.partial(own_kernel, cols=cols, chunk=chunk),
        in_specs=[SMEM_SPEC] + [VMEM_SPEC] * 13 + [HBM_SPEC],
        out_specs=HBM_SPEC,
        out_shape=pltpu.HBM(basis.shape, jnp.float32),
        scratch_shapes=[
            pltpu.VMEM((3, PAD, SHARED), jnp.float32),
            pltpu.VMEM((3, PAD, SHARED), jnp.float32),
            pltpu.VMEM((4, PAD, SHARED), jnp.float32),
            pltpu.SemaphoreType.DMA((3,)),
            pltpu.SemaphoreType.DMA((4,)),
        ],
        compiler_params=pltpu.CompilerParams(vmem_limit_bytes=10 << 20),
        name="own",
    )(here, *[near(x) for x in (mix, *stack, *received)], far(basis))


def join_kernel(here_ref, *refs):
    parts, (_, out_hbm, sems) = refs[:4], refs[4:]
    cols = out_hbm.shape[1] // 4
    copies = []
    for g, part in enumerate(parts):
        at = pl.multiple_of(lax.rem(here_ref[0] + g, 4) * cols + SHARED, LANES)
        target = out_hbm.at[:, pl.ds(at, cols - SHARED)]
        copies.append(pltpu.make_async_copy(part, target, sems.at[g]))
        copies[-1].start()
    for copy in copies:
        copy.wait()


def join(here, parts, whole):
    return pl.pallas_call(
        join_kernel,
        in_specs=[SMEM_SPEC] + [VMEM_SPEC] * 4 + [HBM_SPEC],
        out_specs=HBM_SPEC,
        out_shape=pltpu.HBM(whole.shape, jnp.float32),
        scratch_shapes=[pltpu.SemaphoreType.DMA((4,))],
        input_output_aliases={5: 0},
        compiler_params=pltpu.CompilerParams(vmem_limit_bytes=2 << 20),
        name="join",
    )(here, *[near(x) for x in parts], far(whole))


def program(velocity, basis, levels, profile_index, advect):
    n_space, n_mode = lax.axis_size("space"), lax.axis_size("mode")
    comps, cx, _, _ = velocity.shape
    here = lax.axis_index("mode").astype(jnp.int32).reshape(1)

    def shifted(x, axis, by):
        size = lax.axis_size(axis)
        return lax.ppermute(x, axis, [(i, (i + by) % size) for i in range(size)])

    face_lo, face_hi, plane_lo, plane_hi, *blocks = pack(here, velocity, basis)
    block_own, block_next, block_far, block_prev, tail_next, tail_prev = blocks
    zlo = shifted(face_hi, "mode", 1)
    zhi = shifted(face_lo, "mode", -1)
    lo = shifted(block_next, "mode", 1)
    hi = shifted(block_prev, "mode", -1)
    plane_lo, plane_hi = add_corners(zlo, zhi, plane_lo, plane_hi, cx, comps)
    xlo = shifted(plane_hi, "space", 1)
    xhi = shifted(plane_lo, "space", -1)
    lo_tail = shifted(tail_next, "mode", 1)
    hi_tail = shifted(tail_prev, "mode", -1)
    over = shifted(block_far, "mode", 2)
    lo_far = shifted(lo, "mode", 1)
    hi_far = shifted(hi, "mode", -1)
    snap, plus, minus, across = snapshots(
        velocity,
        levels,
        profile_index,
        advect,
        here,
        basis,
        (zlo, zhi, face_lo, face_hi, velocity, xlo, xhi),
    )
    stack = (snap, block_own, hi, hi_tail, over, lo, lo_tail)
    total = gram(here, stack)
    total = ring_sum(total, ring_parts(total, "space", n_space, 1, 2))
    total = ring_sum(total, ring_parts(total, "mode", n_mode, 1, n_mode))
    total = ring_sum(total, ring_parts(total, "space", n_space, 2, 4))
    lo_early = shifted(plus, "mode", 1)
    hi_early = shifted(minus, "mode", -1)
    parts = [total] + ring_parts(total, "space", n_space, 8, 4)
    over_early = shifted(across, "mode", 2)
    mix, sigma = factor(parts)
    out_own, out_next, out_over, out_prev = update(here, mix, stack)
    back_lo = shifted(out_next, "mode", 1)
    back_hi = shifted(out_prev, "mode", -1)
    back_over = shifted(out_over, "mode", 2)
    mine = own(here, mix, stack, (hi_early, over_early, lo_early, hi_far, lo_far), basis)
    modes = join(here, (out_own, back_hi, back_over, back_lo), mine)
    return (modes, sigma[0, :MODES])


def solution(mesh):
    return jax.shard_map(
        program,
        mesh=mesh,
        in_specs=(P(None, "space", "mode", None), P("mode", "space"), P(), P(), P()),
        out_specs=(P("mode", "space"), P()),
        check_vma=False,
    )
```

```python
import functools

import jax
import jax.numpy as jnp
import numpy as np
from jax import lax
from jax.experimental import pallas as pl
from jax.experimental.pallas import tpu as pltpu
from jax.sharding import PartitionSpec as P

STRIDE = 4
MODES = 32
SWEEPS = 2
FACTOR_BLOCK = 8
COUNT = 34
ROWS = 40
LANES = 128
PAD = 8
VMEM_SPEC = pl.BlockSpec(memory_space=pltpu.VMEM)
HBM_SPEC = pl.BlockSpec(memory_space=pltpu.HBM)
SMEM_SPEC = pl.BlockSpec(memory_space=pltpu.SMEM)


SHARED = 5120
FOLD = SHARED // 4

PLACE = np.array([0, 1] + list(range(PAD, PAD + MODES)))


def near(x):
    return pltpu.with_memory_space_constraint(x, pltpu.VMEM)


def far(x):
    return pltpu.with_memory_space_constraint(x, pltpu.HBM)


def pair_tables():
    rounds = COUNT - 1
    partner = np.tile(np.arange(LANES), (rounds, 1))
    orient = np.ones((rounds, LANES), np.float32)
    for turn in range(rounds):
        players = [0] + [1 + (i - 1 + turn) % rounds for i in range(1, COUNT)]
        for k in range(COUNT // 2):
            lead, trail = PLACE[players[k]], PLACE[players[COUNT - 1 - k]]
            partner[turn, lead] = trail
            partner[turn, trail] = lead
            orient[turn, lead] = -1.0
    moves = np.zeros((3, ROWS, LANES), np.int32)
    signs = np.zeros((3, ROWS, LANES), np.float32)
    for k in range(rounds):
        one, two = 2 * k % rounds, (2 * k + 1) % rounds
        after = partner[two]
        moves[0, k], moves[1, k], moves[2, k] = partner[one], after, partner[one][after]
        signs[0, k], signs[1, k], signs[2, k] = orient[one], orient[one][after], orient[two]
    keep = np.zeros((1, LANES), np.int32)
    keep[0, :MODES] = PLACE[:MODES]
    return moves, signs, keep


def pack_kernel(
    here_ref,
    vel_hbm,
    basis_hbm,
    zfirst_ref,
    zlast_ref,
    xfirst_ref,
    xlast_ref,
    mine_ref,
    next_ref,
    far_ref,
    prev_ref,
    next_tail_ref,
    prev_tail_ref,
    buf,
    edge_sems,
    face_sems,
    block_sems,
):
    comps, cx, cz, _ = vel_hbm.shape
    cols = mine_ref.shape[1]
    edges, rest = [], []
    for c in range(comps):
        for side, at in enumerate((0, cz - PAD)):
            source = vel_hbm.at[c, :, pl.ds(at, PAD), :]
            edges.append(pltpu.make_async_copy(source, buf.at[c, side], edge_sems.at[c, side]))
        for side, (at, ref) in enumerate(((0, xfirst_ref), (cx - 2, xlast_ref))):
            for k in range(2):
                source = vel_hbm.at[c, at + k]
                target = ref.at[pl.ds((2 * c + k) * cz, cz)]
                rest.append(pltpu.make_async_copy(source, target, face_sems.at[c, side, k]))
    targets = (
        (0, 0, mine_ref),
        (1, 0, next_ref),
        (2, 0, far_ref),
        (3, 0, prev_ref),
        (1, SHARED, next_tail_ref),
        (3, SHARED, prev_tail_ref),
    )
    for i, (k, skip, ref) in enumerate(targets):
        at = pl.multiple_of(lax.rem(here_ref[0] + k, 4) * cols + skip, LANES)
        source = basis_hbm.at[:, pl.ds(at, ref.shape[1])]
        rest.append(pltpu.make_async_copy(source, ref, block_sems.at[i]))
    for copy in edges + rest:
        copy.start()
    for copy in edges:
        copy.wait()
    for c in range(comps):
        for i in range(cx):
            for k in range(2):
                row, last = (2 * c + k) * cx + i, PAD - 2 + k
                zfirst_ref[row : row + 1, :] = buf[c, 0, i, k : k + 1, :]
                zlast_ref[row : row + 1, :] = buf[c, 1, i, last : last + 1, :]
    for copy in rest:
        copy.wait()


def pack(here, velocity, basis):
    comps, cx, cz, ny = velocity.shape
    edge = pltpu.VMEM((comps * 2 * cx, ny), jnp.float32)
    face = pltpu.VMEM((comps * 2 * cz + PAD, ny), jnp.float32)
    cols = basis.shape[1] // 4
    block, head, tail = (
        pltpu.VMEM((PAD, size), jnp.float32) for size in (cols, SHARED, cols - SHARED)
    )
    return pl.pallas_call(
        pack_kernel,
        in_specs=[SMEM_SPEC, HBM_SPEC, HBM_SPEC],
        out_specs=[VMEM_SPEC] * 10,
        out_shape=[edge, edge, face, face, block, head, block, head, tail, tail],
        scratch_shapes=[
            pltpu.VMEM((comps, 2, cx, PAD, ny), jnp.float32),
            pltpu.SemaphoreType.DMA((comps, 2)),
            pltpu.SemaphoreType.DMA((comps, 2, 2)),
            pltpu.SemaphoreType.DMA((6,)),
        ],
        compiler_params=pltpu.CompilerParams(vmem_limit_bytes=4 << 20),
        name="pack",
    )(here, far(velocity), far(basis))


def corner_kernel(zlo_ref, zhi_ref, _, __, xfirst_ref, xlast_ref, *, cx, comps):
    base = xfirst_ref.shape[0] - PAD
    zero = jnp.zeros((PAD, xfirst_ref.shape[1]), jnp.float32)
    for ref, plane in ((xfirst_ref, 0), (xlast_ref, cx - 1)):
        ref[base:, :] = zero
        for c in range(comps):
            low, high = (2 * c + 1) * cx + plane, 2 * c * cx + plane
            at = base + 2 * c
            ref[at : at + 1, :] = zlo_ref[low : low + 1, :]
            ref[at + 1 : at + 2, :] = zhi_ref[high : high + 1, :]


def add_corners(zlo, zhi, first, last, cx, comps):
    face = pltpu.VMEM(first.shape, jnp.float32)
    return pl.pallas_call(
        functools.partial(corner_kernel, cx=cx, comps=comps),
        in_specs=[VMEM_SPEC] * 4,
        out_specs=[VMEM_SPEC] * 2,
        out_shape=[face, face],
        input_output_aliases={2: 0, 3: 1},
        compiler_params=pltpu.CompilerParams(vmem_limit_bytes=1 << 20),
        name="corners",
    )(*[near(x) for x in (zlo, zhi, first, last)])


def coefficients(levels_ref, index_ref, advect_ref):
    index = index_ref[...]
    visc = jnp.zeros(index.shape, jnp.float32)
    for level in range(levels_ref.shape[0]):
        visc = jnp.where(index == level, levels_ref[level], visc)
    cells = index.shape[1]
    lane = lax.broadcasted_iota(jnp.int32, index.shape, 1)
    first, last = lane == 0, lane == cells - 1
    up = jnp.where(last, visc, 0.5 * (visc + pltpu.roll(visc, cells - 1, 1)))
    down = jnp.where(first, visc, 0.5 * (visc + pltpu.roll(visc, 1, 1)))
    half = 0.5 * advect_ref[...]
    return (
        1.0 - 4.0 * visc - up - down,
        visc,
        visc - half,
        visc + half,
        jnp.where(last, 0.0, up),
        jnp.where(first, 0.0, down),
    )


def step(coefs, center, east, west, north, south):
    mid, visc, c_east, c_west, c_up, c_down = coefs
    cells = center.shape[-1]
    upward = pltpu.roll(center, cells - 1, 1)
    downward = pltpu.roll(center, 1, 1)
    return (
        mid * center
        + visc * (north + south)
        + c_east * east
        + c_west * west
        + c_up * upward
        + c_down * downward
    )


def split3(x):
    high = x.astype(jnp.bfloat16)
    rest = x - high.astype(jnp.float32)
    middle = rest.astype(jnp.bfloat16)
    low = (rest - middle.astype(jnp.float32)).astype(jnp.bfloat16)
    return high, middle, low


def offer_copies(here, basis_hbm, refs, sems):
    cols = basis_hbm.shape[1] // 4
    copies = []
    for side, (ref, skip, count) in enumerate(zip(refs, (2, 0, 0), (3, 3, 1))):
        for k in range(count):
            at = pl.multiple_of(lax.rem(here + skip + k, 4) * cols, LANES)
            source = basis_hbm.at[:, pl.ds(at, SHARED)]
            target = ref.at[:, pl.ds(k * SHARED, SHARED)]
            copies.append(pltpu.make_async_copy(source, target, sems.at[side, k]))
    return copies


def stencil_kernel(
    levels_ref,
    index_ref,
    advect_ref,
    sum_ref,
    zlo_ref,
    zhi_ref,
    face_lo_ref,
    face_hi_ref,
    here_ref,
    basis_hbm,
    vel_hbm,
    xlo_ref,
    xhi_ref,
    out_ref,
    plus_ref,
    minus_ref,
    over_ref,
    field,
    first,
    boxed,
    sems,
    offer_sems,
):
    comp = pl.program_id(0)
    offer_refs = (plus_ref, minus_ref, over_ref)
    offers = offer_copies(here_ref[0], basis_hbm, offer_refs, offer_sems)
    cx, cz, ny = vel_hbm.shape[1:]
    inner = pl.ds(PAD, cz)

    def copies(c):
        return (
            pltpu.make_async_copy(
                vel_hbm.at[c], field.at[c, pl.ds(2, cx), inner, :], sems.at[c, 0, 0]
            ),
            *[
                pltpu.make_async_copy(
                    ref.at[pl.ds((2 * c + k) * cz, cz)],
                    field.at[c, at + k, inner, :],
                    sems.at[c, 1 + side, k],
                )
                for side, (at, ref) in enumerate(((0, xlo_ref), (cx + 2, xhi_ref)))
                for k in range(2)
            ],
        )

    @pl.when(comp == 0)
    def _():
        for c in range(3):
            for copy in copies(c):
                copy.start()
        for copy in offers:
            copy.start()

    @pl.when(comp == pl.num_programs(0) - 1)
    def _():
        for copy in offers:
            copy.wait()

    coefs = coefficients(levels_ref, index_ref, advect_ref)

    def edge_row(ref, k):
        return ref[pl.ds(pl.multiple_of((2 * comp + k) * cx, 8), cx), :]

    zlo2, zlo1 = edge_row(zlo_ref, 0), edge_row(zlo_ref, 1)
    zhi1, zhi2 = edge_row(zhi_ref, 0), edge_row(zhi_ref, 1)
    spot = 6 * cz + 2 * comp
    lo_before, lo_after = xlo_ref[pl.ds(spot, 1), :], xhi_ref[pl.ds(spot, 1), :]
    hi_before, hi_after = xlo_ref[pl.ds(spot + 1, 1), :], xhi_ref[pl.ds(spot + 1, 1), :]
    plane = lax.broadcasted_iota(jnp.int32, (cx, ny), 0)

    def edge(row, before, after, north, south):
        east = jnp.where(plane == cx - 1, after, pltpu.roll(row, cx - 1, 0))
        west = jnp.where(plane == 0, before, pltpu.roll(row, 1, 0))
        return step(coefs, row, east, west, north, south)

    edge_lo = edge(zlo1, lo_before, lo_after, zlo2, edge_row(face_lo_ref, 0))
    edge_hi = edge(zhi1, hi_before, hi_after, edge_row(face_hi_ref, 1), zhi2)
    for i in range(cx):
        field[comp, 2 + i, PAD - 1 : PAD, :] = zlo1[i : i + 1]
        field[comp, 2 + i, PAD + cz : PAD + cz + 1, :] = zhi1[i : i + 1]
        first[1 + i, PAD - 1 : PAD, :] = edge_lo[i : i + 1]
        first[1 + i, PAD + cz : PAD + cz + 1, :] = edge_hi[i : i + 1]
    field[comp, 1, PAD - 1 : PAD, :] = lo_before
    field[comp, 1, PAD + cz : PAD + cz + 1, :] = hi_before
    field[comp, cx + 2, PAD - 1 : PAD, :] = lo_after
    field[comp, cx + 2, PAD + cz : PAD + cz + 1, :] = hi_after

    for copy in copies(comp):
        copy.wait()

    chunk = 16

    def first_plane(p, carry):
        for k in range(cz // chunk):
            at = PAD + k * chunk
            rows = pl.ds(at, chunk)
            first[p, rows, :] = step(
                coefs,
                field[comp, p + 1, rows, :],
                field[comp, p + 2, rows, :],
                field[comp, p, rows, :],
                field[comp, p + 1, pl.ds(at - 1, chunk), :],
                field[comp, p + 1, pl.ds(at + 1, chunk), :],
            )
        return carry

    lax.fori_loop(0, cx + 2, first_plane, 0)

    sums = sum_ref[...]
    lane = lax.broadcasted_iota(jnp.int32, (cz, LANES), 1)
    row = lax.broadcasted_iota(jnp.int32, (cz, LANES), 0)
    wanted = (lane // (LANES // 2)) == ((row // STRIDE) % 2)
    part = out_ref.shape[1] // vel_hbm.shape[0]
    offset = pl.multiple_of(comp * part, LANES)
    out_ref[:, pl.ds(offset, part)] = jnp.zeros((PAD, part), jnp.float32)

    def coarse(which, box):
        total = sum(
            jnp.dot(part, sums, preferred_element_type=jnp.float32)
            for part in split3(boxed[...])
        )
        total = jnp.where(wanted, total, 0.0)
        base = offset + box * (cz // 8 * LANES)
        for r in range(cz // 8):
            line = jnp.sum(total[8 * r : 8 * r + 8], axis=0, keepdims=True) * 0.125
            at = pl.multiple_of(base + r * LANES, LANES)
            out_ref[which : which + 1, pl.ds(at, LANES)] = line

    def box_step(box, carry):
        start = 1 + STRIDE * box
        for k in range(cz // chunk):
            rows = pl.ds(PAD + k * chunk, chunk)
            boxed[pl.ds(k * chunk, chunk), :] = (
                first[start, rows, :] + first[start + 1, rows, :]
            ) + (first[start + 2, rows, :] + first[start + 3, rows, :])
        coarse(0, box)
        for k in range(cz // chunk):
            at = PAD + k * chunk
            rows = pl.ds(at, chunk)
            total = None
            for i in range(STRIDE):
                p = start + i
                value = step(
                    coefs,
                    first[p, rows, :],
                    first[p + 1, rows, :],
                    first[p - 1, rows, :],
                    first[p, pl.ds(at - 1, chunk), :],
                    first[p, pl.ds(at + 1, chunk), :],
                )
                total = value if total is None else total + value
            boxed[pl.ds(k * chunk, chunk), :] = total
        coarse(1, box)
        return carry

    lax.fori_loop(0, cx // STRIDE, box_step, 0)

    @pl.when(comp == 0)
    def _():
        tiles = SHARED // LANES
        for k in range(2 * tiles):
            which, tile = divmod(k, tiles)
            line = out_ref[which : which + 1, tile * LANES : (tile + 1) * LANES]
            for ref in offer_refs:
                at = ref.shape[1] - FOLD + k // 8 * LANES
                ref[k % 8 : k % 8 + 1, at : at + LANES] = line


def snapshots(velocity, levels, profile_index, advect, here, basis, halos):
    comps, cx, cz, ny = velocity.shape
    cols = (cx // STRIDE) * (cz // STRIDE) * (ny // STRIDE)
    half = LANES // 2
    sums = np.zeros((ny, LANES), np.float32)
    for y in range(ny):
        sums[y, y // STRIDE] = 1.0
        sums[y, half + y // STRIDE] = 1.0
    return pl.pallas_call(
        stencil_kernel,
        grid=(comps,),
        in_specs=[
            SMEM_SPEC,
            pl.BlockSpec((1, ny), lambda c: (0, 0)),
            pl.BlockSpec((1, ny), lambda c: (0, 0)),
            pl.BlockSpec((ny, LANES), lambda c: (0, 0)),
            *[VMEM_SPEC] * 4,
            SMEM_SPEC,
            HBM_SPEC,
            HBM_SPEC,
            VMEM_SPEC,
            VMEM_SPEC,
        ],
        out_specs=[VMEM_SPEC] * 4,
        out_shape=[pltpu.VMEM((PAD, comps * cols), jnp.float32)]
        + [pltpu.VMEM((PAD, k * SHARED + FOLD), jnp.float32) for k in (3, 3, 1)],
        scratch_shapes=[
            pltpu.VMEM((comps, cx + 4, cz + 2 * PAD, ny), jnp.float32),
            pltpu.VMEM((cx + 2, cz + 2 * PAD, ny), jnp.float32),
            pltpu.VMEM((cz, ny), jnp.float32),
            pltpu.SemaphoreType.DMA((comps, 3, 2)),
            pltpu.SemaphoreType.DMA((3, 3)),
        ],
        compiler_params=pltpu.CompilerParams(vmem_limit_bytes=20 << 20),
        name="stencil",
    )(
        levels,
        profile_index.reshape(1, ny),
        advect.reshape(1, ny),
        jnp.asarray(sums, jnp.bfloat16),
        *[near(x) for x in halos[:4]],
        here,
        far(basis),
        far(halos[4]),
        *[near(x) for x in halos[5:]],
    )


def stacked(pieces, start, size):
    rows = []
    for piece in pieces:
        if isinstance(piece, tuple):
            ref, at = (piece[0], start) if start < SHARED else (piece[1], start - SHARED)
        else:
            ref, at = piece, start
        rows.append(ref[:, at : at + size])
    return jnp.concatenate(rows, axis=0)


def pieces_of(refs):
    snap, mine, hi, hi_tail, far_block, lo, lo_tail = refs
    return [snap, mine, (hi, hi_tail), far_block, (lo, lo_tail)]


def gram_kernel(here_ref, *refs, chunk):
    pieces, out_ref = pieces_of(refs[:-1]), refs[-1]
    here = here_ref[0]
    n, acc = ROWS, None
    for start in range(0, pieces[0].shape[1], chunk):
        stack = stacked(pieces, start, chunk)
        high = stack.astype(jnp.bfloat16).astype(jnp.float32)
        joined = jnp.concatenate([high, stack - high], axis=0).astype(jnp.bfloat16)
        part = lax.dot_general(
            joined, joined, (((1,), (1,)), ((), ())), preferred_element_type=jnp.float32
        )
        acc = part if acc is None else acc + part
    cross = acc[0:n, n : 2 * n] + acc[n : 2 * n, 0:n]
    total = acc[0:n, 0:n] + (cross + acc[n : 2 * n, n : 2 * n])
    total = jnp.concatenate([total, jnp.zeros((n, LANES - n), jnp.float32)], axis=1)
    lane = lax.broadcasted_iota(jnp.int32, (n, LANES), 1)
    turned = PAD + lax.rem(lane - PAD + MODES - PAD * here + MODES, MODES)
    inside = (lane >= PAD) & (lane < n)
    total = jnp.take_along_axis(total, jnp.where(inside, turned, lane), axis=1)
    out_ref[0:PAD, :] = total[0:PAD]
    for g in range(4):
        at = pl.multiple_of(PAD + PAD * lax.rem(here + g, 4), PAD)
        out_ref[pl.ds(at, PAD), :] = total[PAD + PAD * g : 2 * PAD + PAD * g]


def gram(here, stack, chunk=1024):
    return pl.pallas_call(
        functools.partial(gram_kernel, chunk=chunk),
        in_specs=[SMEM_SPEC] + [VMEM_SPEC] * 7,
        out_specs=VMEM_SPEC,
        out_shape=pltpu.VMEM((ROWS, LANES), jnp.float32),
        compiler_params=pltpu.CompilerParams(vmem_limit_bytes=8 << 20),
        name="gram",
    )(here, *[near(x) for x in stack])


def ring_moves(size, stride, width):
    moves = []
    for shift in range(1, width):
        pairs = []
        for i in range(size):
            k = (i // stride) % width
            pairs.append((i, i + ((k + shift) % width - k) * stride))
        moves.append(pairs)
    return moves


def ring_parts(x, axis, size, stride, width):
    return [lax.ppermute(x, axis, pairs) for pairs in ring_moves(size, stride, width)]


def ring_sum(x, parts):
    if len(parts) == 1:
        return x + parts[0]
    one, two, three = parts
    return (x + two) + (one + three)


def lane_sum(x):
    total = x[0:8]
    for k in range(1, ROWS // 8):
        total = total + x[8 * k : 8 * k + 8]
    total = total + pltpu.roll(total, 4, 0)
    total = total + pltpu.roll(total, 2, 0)
    return total + pltpu.roll(total, 1, 0)


def spread(x):
    return jnp.concatenate([x] * (ROWS // 8), axis=0)


def factor_kernel(
    g0_ref, g1_ref, g2_ref, g3_ref, partner_ref, orient_ref, keep_ref, mix_ref, sigma_ref
):
    a = (g0_ref[...] + g2_ref[...]) + (g1_ref[...] + g3_ref[...])
    lane = lax.broadcasted_iota(jnp.int32, (ROWS, LANES), 1)
    row = lax.broadcasted_iota(jnp.int32, (ROWS, LANES), 0)
    upper = jnp.zeros((ROWS, LANES), jnp.float32)
    places = [int(k) for k in PLACE]
    while places:
        block, places = places[:FACTOR_BLOCK], places[FACTOR_BLOCK:]
        lines = [jnp.broadcast_to(a[j : j + 1, :], (8, LANES)) for j in block]
        columns = [jnp.broadcast_to(a[:, j : j + 1], (ROWS, LANES)) for j in block]

        def entry(column, j):
            return jnp.broadcast_to(column[j : j + 1, :], (8, LANES))

        for i, j in enumerate(block):
            scale = lax.rsqrt(entry(columns[i], j))
            lines[i] = lines[i] * scale
            columns[i] = columns[i] * spread(scale)
            for k in range(i + 1, len(block)):
                cross = entry(columns[i], block[k])
                lines[k] = lines[k] - cross * lines[i]
                columns[k] = columns[k] - spread(cross) * columns[i]
        for i, j in enumerate(block):
            line = spread(lines[i])
            a = a - columns[i] * line
            upper = jnp.where((row == j) & (lane >= j), line, upper)

    def angle(x, y, sign):
        contrast = lane_sum(y * y) - lane_sum(x * x)
        inner = lane_sum(x * y)
        toward = jnp.where(contrast > 0.0, -1.0, jnp.where(contrast < 0.0, 1.0, sign))
        d = jnp.abs(contrast) + jnp.sqrt(contrast * contrast + 4.0 * inner * inner)
        positive = d > 0.0
        tangent = jnp.where(
            positive, 2.0 * inner * toward / jnp.where(positive, d, 1.0), 0.0
        )
        cosine = lax.rsqrt(1.0 + tangent * tangent)
        return spread(cosine), spread(cosine * tangent)

    def two_rounds(k, state):
        x, v = state
        moves = [
            jnp.broadcast_to(partner_ref[m, pl.ds(k, 1), :], (ROWS, LANES)) for m in range(3)
        ]
        signs = [
            jnp.broadcast_to(orient_ref[m, pl.ds(k, 1), :], (8, LANES)) for m in range(3)
        ]
        pair, after, cross = (jnp.take_along_axis(x, move, axis=1) for move in moves)
        c_self, s_self = angle(x, pair, signs[0])
        c_next, s_next = angle(after, cross, signs[1])
        x = c_self * x + s_self * pair
        after = c_next * after + s_next * cross
        c_last, s_last = angle(x, after, signs[2])
        x = c_last * x + s_last * after
        pair, after, cross = (jnp.take_along_axis(v, move, axis=1) for move in moves)
        v = c_self * v + s_self * pair
        after = c_next * after + s_next * cross
        return x, c_last * v + s_last * after

    eye = jnp.where(row == lane, 1.0, 0.0)
    x, v = lax.fori_loop(0, SWEEPS * (COUNT - 1) // 2, two_rounds, (upper, eye))
    keep = jnp.broadcast_to(keep_ref[...], (ROWS, LANES))
    sigma_ref[...] = jnp.take_along_axis(jnp.sqrt(lane_sum(x * x)), keep[0:8], axis=1)
    v = jnp.take_along_axis(v, keep, axis=1)
    high = v.astype(jnp.bfloat16).astype(jnp.float32)
    low = v - high
    mix = jnp.concatenate([high, high, low, jnp.zeros((8, LANES), jnp.float32)], axis=0)
    mix_ref[...] = jnp.transpose(mix)[0:MODES]


def factor(parts):
    tables = [near(jnp.asarray(table)) for table in pair_tables()]
    return pl.pallas_call(
        factor_kernel,
        in_specs=[VMEM_SPEC] * 7,
        out_specs=(VMEM_SPEC, VMEM_SPEC),
        out_shape=(
            pltpu.VMEM((MODES, LANES), jnp.float32),
            pltpu.VMEM((8, LANES), jnp.float32),
        ),
        compiler_params=pltpu.CompilerParams(vmem_limit_bytes=4 << 20),
        name="factor",
    )(*[near(x) for x in parts], *tables)


def turned_mix(mix, here):
    lane = lax.broadcasted_iota(jnp.int32, mix.shape, 1)
    inside = lax.rem(lane, ROWS)
    turned = lane - inside + PAD + lax.rem(inside + (MODES - PAD) + PAD * here, MODES)
    source = jnp.where((inside < PAD) | (lane >= 3 * ROWS), lane, turned)
    return jnp.take_along_axis(mix, source, axis=1).astype(jnp.bfloat16)


def mix_rows(mix_ref, here, g):
    at = pl.multiple_of(PAD * lax.rem(here + g, 4), PAD)
    return mix_ref[pl.ds(at, PAD), :]


def mixed(mix, stack):
    high = stack.astype(jnp.bfloat16).astype(jnp.float32)
    zero = jnp.zeros((8, stack.shape[1]), jnp.float32)
    joined = jnp.concatenate([high, stack - high, high, zero], axis=0)
    return jnp.dot(mix, joined.astype(jnp.bfloat16), preferred_element_type=jnp.float32)


def update_kernel(here_ref, mix_ref, *refs, chunk):
    pieces, out_refs = pieces_of(refs[:7]), refs[7:]
    here = here_ref[0]
    mix = jnp.concatenate([mix_rows(mix_ref, here, g) for g in range(4)], axis=0)
    mix = turned_mix(mix, here)
    for start in range(0, out_refs[0].shape[1], chunk):
        out = mixed(mix, stacked(pieces, SHARED + start, chunk))
        for g, ref in enumerate(out_refs):
            ref[:, start : start + chunk] = out[PAD * g : PAD * g + PAD]


def update(here, mix, stack, chunk=1024):
    cols = stack[0].shape[1] - SHARED
    return pl.pallas_call(
        functools.partial(update_kernel, chunk=chunk),
        in_specs=[SMEM_SPEC] + [VMEM_SPEC] * 8,
        out_specs=[VMEM_SPEC] * 4,
        out_shape=[pltpu.VMEM((PAD, cols), jnp.float32)] * 4,
        compiler_params=pltpu.CompilerParams(vmem_limit_bytes=8 << 20),
        name="update",
    )(here, near(mix), *[near(x) for x in stack])


def own_kernel(here_ref, mix_ref, *refs, cols, chunk):
    pieces, (hi_ref, over_ref, lo_ref, hi_far_ref, lo_far_ref) = pieces_of(refs[:7]), refs[7:12]
    basis_hbm, out_hbm, mine, snap, buf, in_sems, out_sems = refs[12:]
    here = here_ref[0]
    tiles = SHARED // LANES
    blocks = [lax.rem(here + 1 + b, 4) for b in range(4)]
    reads = []
    for b in range(3):
        at = pl.multiple_of(blocks[b] * cols, LANES)
        source = basis_hbm.at[:, pl.ds(at, SHARED)]
        reads.append(pltpu.make_async_copy(source, mine.at[b], in_sems.at[b]))
    for copy in reads:
        copy.start()
    mix = turned_mix(mix_rows(mix_ref, here, 0), here)
    for b, ref in enumerate((hi_ref, over_ref, lo_ref)):
        snap[b] = jnp.zeros((PAD, SHARED), jnp.float32)
        for k in range(2 * tiles):
            which, tile = divmod(k, tiles)
            at = ref.shape[1] - FOLD + k // 8 * LANES
            line = ref[k % 8 : k % 8 + 1, at : at + LANES]
            snap[b, which : which + 1, tile * LANES : (tile + 1) * LANES] = line
    for copy in reads:
        copy.wait()
    writes = []
    for b in range(4):
        for start in range(0, SHARED, chunk):
            at = slice(start, start + chunk)
            if b == 3:
                stack = stacked(pieces, start, chunk)
            else:
                wide = slice(b * SHARED + start, b * SHARED + start + chunk)
                opposite = (hi_far_ref, over_ref, lo_far_ref)[b]
                rows = [snap[b, :, at], mine[b, :, at]]
                rows += [hi_ref[:, wide], opposite[:, at], lo_ref[:, wide]]
                stack = jnp.concatenate(rows, axis=0)
            buf[b, :, at] = mixed(mix, stack)
        target = pl.ds(pl.multiple_of(blocks[b] * cols, LANES), SHARED)
        writes.append(pltpu.make_async_copy(buf.at[b], out_hbm.at[:, target], out_sems.at[b]))
        writes[-1].start()
    for copy in writes:
        copy.wait()


def own(here, mix, stack, received, basis, chunk=1024):
    cols = basis.shape[1] // 4
    return pl.pallas_call(
        functools.partial(own_kernel, cols=cols, chunk=chunk),
        in_specs=[SMEM_SPEC] + [VMEM_SPEC] * 13 + [HBM_SPEC],
        out_specs=HBM_SPEC,
        out_shape=pltpu.HBM(basis.shape, jnp.float32),
        scratch_shapes=[
            pltpu.VMEM((3, PAD, SHARED), jnp.float32),
            pltpu.VMEM((3, PAD, SHARED), jnp.float32),
            pltpu.VMEM((4, PAD, SHARED), jnp.float32),
            pltpu.SemaphoreType.DMA((3,)),
            pltpu.SemaphoreType.DMA((4,)),
        ],
        compiler_params=pltpu.CompilerParams(vmem_limit_bytes=10 << 20),
        name="own",
    )(here, *[near(x) for x in (mix, *stack, *received)], far(basis))


def join_kernel(here_ref, *refs, sources):
    parts, (_, out_hbm, sems) = refs[: len(sources)], refs[len(sources) :]
    cols = out_hbm.shape[1] // 4
    copies = []
    for g, part in zip(sources, parts):
        at = pl.multiple_of(lax.rem(here_ref[0] + g, 4) * cols + SHARED, LANES)
        target = out_hbm.at[:, pl.ds(at, cols - SHARED)]
        copies.append(pltpu.make_async_copy(part, target, sems.at[g]))
        copies[-1].start()
    for copy in copies:
        copy.wait()


def join(here, parts, whole):
    count = len(parts)
    return pl.pallas_call(
        functools.partial(join_kernel, sources=tuple(parts)),
        in_specs=[SMEM_SPEC] + [VMEM_SPEC] * count + [HBM_SPEC],
        out_specs=HBM_SPEC,
        out_shape=pltpu.HBM(whole.shape, jnp.float32),
        scratch_shapes=[pltpu.SemaphoreType.DMA((4,))],
        input_output_aliases={1 + count: 0},
        compiler_params=pltpu.CompilerParams(vmem_limit_bytes=2 << 20),
        name="join",
    )(here, *[near(x) for x in parts.values()], far(whole))


def program(velocity, basis, levels, profile_index, advect):
    n_space, n_mode = lax.axis_size("space"), lax.axis_size("mode")
    comps, cx, _, _ = velocity.shape
    here = lax.axis_index("mode").astype(jnp.int32).reshape(1)

    def shifted(x, axis, by):
        size = lax.axis_size(axis)
        return lax.ppermute(x, axis, [(i, (i + by) % size) for i in range(size)])

    face_lo, face_hi, plane_lo, plane_hi, *blocks = pack(here, velocity, basis)
    block_own, block_next, block_far, block_prev, tail_next, tail_prev = blocks
    zlo = shifted(face_hi, "mode", 1)
    zhi = shifted(face_lo, "mode", -1)
    lo = shifted(block_next, "mode", 1)
    hi = shifted(block_prev, "mode", -1)
    over = shifted(block_far, "mode", 2)
    plane_lo, plane_hi = add_corners(zlo, zhi, plane_lo, plane_hi, cx, comps)
    xlo = shifted(plane_hi, "space", 1)
    xhi = shifted(plane_lo, "space", -1)
    lo_tail = shifted(tail_next, "mode", 1)
    hi_tail = shifted(tail_prev, "mode", -1)
    lo_far = shifted(lo, "mode", 1)
    hi_far = shifted(hi, "mode", -1)
    snap, plus, minus, across = snapshots(
        velocity,
        levels,
        profile_index,
        advect,
        here,
        basis,
        (zlo, zhi, face_lo, face_hi, velocity, xlo, xhi),
    )
    stack = (snap, block_own, hi, hi_tail, over, lo, lo_tail)
    total = gram(here, stack)
    total = ring_sum(total, ring_parts(total, "space", n_space, 1, 2))
    total = ring_sum(total, ring_parts(total, "mode", n_mode, 1, n_mode))
    total = ring_sum(total, ring_parts(total, "space", n_space, 2, 4))
    lo_early = shifted(plus, "mode", 1)
    hi_early = shifted(minus, "mode", -1)
    parts = [total] + ring_parts(total, "space", n_space, 8, 4)
    over_early = shifted(across, "mode", 2)
    mix, sigma = factor(parts)
    out_own, out_next, out_over, out_prev = update(here, mix, stack)
    back_lo = shifted(out_next, "mode", 1)
    back_hi = shifted(out_prev, "mode", -1)
    back_over = shifted(out_over, "mode", 2)
    mine = own(here, mix, stack, (hi_early, over_early, lo_early, hi_far, lo_far), basis)
    modes = join(here, {0: out_own, 1: back_hi, 3: back_lo}, mine)
    modes = join(here, {2: back_over}, modes)
    return (modes, sigma[0, :MODES])


def solution(mesh):
    return jax.shard_map(
        program,
        mesh=mesh,
        in_specs=(P(None, "space", "mode", None), P("mode", "space"), P(), P(), P()),
        out_specs=(P("mode", "space"), P()),
        check_vma=False,
    )
```

```python
import functools

import jax
import jax.numpy as jnp
import numpy as np
from jax import lax
from jax.experimental import pallas as pl
from jax.experimental.pallas import tpu as pltpu
from jax.sharding import PartitionSpec as P

STRIDE = 4
MODES = 32
SWEEPS = 2
FACTOR_BLOCK = 8
COUNT = 34
ROWS = 40
LANES = 128
PAD = 8
VMEM_SPEC = pl.BlockSpec(memory_space=pltpu.VMEM)
HBM_SPEC = pl.BlockSpec(memory_space=pltpu.HBM)
SMEM_SPEC = pl.BlockSpec(memory_space=pltpu.SMEM)


SHARED = 5120
FOLD = SHARED // 4

PLACE = np.array([0, 1] + list(range(PAD, PAD + MODES)))


def near(x):
    return pltpu.with_memory_space_constraint(x, pltpu.VMEM)


def far(x):
    return pltpu.with_memory_space_constraint(x, pltpu.HBM)


def pair_tables():
    rounds = COUNT - 1
    partner = np.tile(np.arange(LANES), (rounds, 1))
    orient = np.ones((rounds, LANES), np.float32)
    for turn in range(rounds):
        players = [0] + [1 + (i - 1 + turn) % rounds for i in range(1, COUNT)]
        for k in range(COUNT // 2):
            lead, trail = PLACE[players[k]], PLACE[players[COUNT - 1 - k]]
            partner[turn, lead] = trail
            partner[turn, trail] = lead
            orient[turn, lead] = -1.0
    moves = np.zeros((3, ROWS, LANES), np.int32)
    signs = np.zeros((3, ROWS, LANES), np.float32)
    for k in range(rounds):
        one, two = 2 * k % rounds, (2 * k + 1) % rounds
        after = partner[two]
        moves[0, k], moves[1, k], moves[2, k] = partner[one], after, partner[one][after]
        signs[0, k], signs[1, k], signs[2, k] = orient[one], orient[one][after], orient[two]
    keep = np.zeros((1, LANES), np.int32)
    keep[0, :MODES] = PLACE[:MODES]
    return moves, signs, keep


def face_plane(here_ref, side, first, last):
    return jnp.where(here_ref[1] == side, first, last)


def pack_kernel(
    here_ref,
    vel_hbm,
    basis_hbm,
    zfirst_ref,
    zlast_ref,
    outer_ref,
    inner_ref,
    mine_ref,
    next_ref,
    far_ref,
    prev_ref,
    next_tail_ref,
    prev_tail_ref,
    buf,
    edge_sems,
    face_sems,
    block_sems,
):
    comps, cx, cz, _ = vel_hbm.shape
    cols = mine_ref.shape[1]
    edges, rest = [], []
    for c in range(comps):
        for side, at in enumerate((0, cz - PAD)):
            source = vel_hbm.at[c, :, pl.ds(at, PAD), :]
            edges.append(pltpu.make_async_copy(source, buf.at[c, side], edge_sems.at[c, side]))
        for side, ref in enumerate((outer_ref, inner_ref)):
            at = face_plane(here_ref, side, 0, cx - 2)
            for k in range(2):
                source = vel_hbm.at[c, at + k]
                target = ref.at[pl.ds((2 * c + k) * cz, cz)]
                rest.append(pltpu.make_async_copy(source, target, face_sems.at[c, side, k]))
    targets = (
        (0, 0, mine_ref),
        (1, 0, next_ref),
        (2, 0, far_ref),
        (3, 0, prev_ref),
        (1, SHARED, next_tail_ref),
        (3, SHARED, prev_tail_ref),
    )
    for i, (k, skip, ref) in enumerate(targets):
        at = pl.multiple_of(lax.rem(here_ref[0] + k, 4) * cols + skip, LANES)
        source = basis_hbm.at[:, pl.ds(at, ref.shape[1])]
        rest.append(pltpu.make_async_copy(source, ref, block_sems.at[i]))
    for copy in edges + rest:
        copy.start()
    for copy in edges:
        copy.wait()
    for c in range(comps):
        for i in range(cx):
            for k in range(2):
                row, last = (2 * c + k) * cx + i, PAD - 2 + k
                zfirst_ref[row : row + 1, :] = buf[c, 0, i, k : k + 1, :]
                zlast_ref[row : row + 1, :] = buf[c, 1, i, last : last + 1, :]
    for copy in rest:
        copy.wait()


def pack(here, velocity, basis):
    comps, cx, cz, ny = velocity.shape
    edge = pltpu.VMEM((comps * 2 * cx, ny), jnp.float32)
    face = pltpu.VMEM((comps * 2 * cz + PAD, ny), jnp.float32)
    cols = basis.shape[1] // 4
    block, head, tail = (
        pltpu.VMEM((PAD, size), jnp.float32) for size in (cols, SHARED, cols - SHARED)
    )
    return pl.pallas_call(
        pack_kernel,
        in_specs=[SMEM_SPEC, HBM_SPEC, HBM_SPEC],
        out_specs=[VMEM_SPEC] * 10,
        out_shape=[edge, edge, face, face, block, head, block, head, tail, tail],
        scratch_shapes=[
            pltpu.VMEM((comps, 2, cx, PAD, ny), jnp.float32),
            pltpu.SemaphoreType.DMA((comps, 2)),
            pltpu.SemaphoreType.DMA((comps, 2, 2)),
            pltpu.SemaphoreType.DMA((6,)),
        ],
        compiler_params=pltpu.CompilerParams(vmem_limit_bytes=4 << 20),
        name="pack",
    )(here, far(velocity), far(basis))


def corner_kernel(here_ref, zlo_ref, zhi_ref, _, __, outer_ref, inner_ref, *, cx, comps):
    base = outer_ref.shape[0] - PAD
    zero = jnp.zeros((PAD, outer_ref.shape[1]), jnp.float32)
    for side, ref in enumerate((outer_ref, inner_ref)):
        plane = face_plane(here_ref, side, 0, cx - 1)
        ref[base:, :] = zero
        for c in range(comps):
            at = base + 2 * c
            ref[at : at + 1, :] = zlo_ref[pl.ds((2 * c + 1) * cx + plane, 1), :]
            ref[at + 1 : at + 2, :] = zhi_ref[pl.ds(2 * c * cx + plane, 1), :]


def add_corners(here, zlo, zhi, outer, inner, cx, comps):
    face = pltpu.VMEM(outer.shape, jnp.float32)
    return pl.pallas_call(
        functools.partial(corner_kernel, cx=cx, comps=comps),
        in_specs=[SMEM_SPEC] + [VMEM_SPEC] * 4,
        out_specs=[VMEM_SPEC] * 2,
        out_shape=[face, face],
        input_output_aliases={3: 0, 4: 1},
        compiler_params=pltpu.CompilerParams(vmem_limit_bytes=1 << 20),
        name="corners",
    )(here, *[near(x) for x in (zlo, zhi, outer, inner)])


def coefficients(levels_ref, index_ref, advect_ref):
    index = index_ref[...]
    visc = jnp.zeros(index.shape, jnp.float32)
    for level in range(levels_ref.shape[0]):
        visc = jnp.where(index == level, levels_ref[level], visc)
    cells = index.shape[1]
    lane = lax.broadcasted_iota(jnp.int32, index.shape, 1)
    first, last = lane == 0, lane == cells - 1
    up = jnp.where(last, visc, 0.5 * (visc + pltpu.roll(visc, cells - 1, 1)))
    down = jnp.where(first, visc, 0.5 * (visc + pltpu.roll(visc, 1, 1)))
    half = 0.5 * advect_ref[...]
    return (
        1.0 - 4.0 * visc - up - down,
        visc,
        visc - half,
        visc + half,
        jnp.where(last, 0.0, up),
        jnp.where(first, 0.0, down),
    )


def step(coefs, center, east, west, north, south):
    mid, visc, c_east, c_west, c_up, c_down = coefs
    cells = center.shape[-1]
    upward = pltpu.roll(center, cells - 1, 1)
    downward = pltpu.roll(center, 1, 1)
    return (
        mid * center
        + visc * (north + south)
        + c_east * east
        + c_west * west
        + c_up * upward
        + c_down * downward
    )


def split3(x):
    high = x.astype(jnp.bfloat16)
    rest = x - high.astype(jnp.float32)
    middle = rest.astype(jnp.bfloat16)
    low = (rest - middle.astype(jnp.float32)).astype(jnp.bfloat16)
    return high, middle, low


def offer_copies(here, basis_hbm, refs, sems):
    cols = basis_hbm.shape[1] // 4
    copies = []
    for side, (ref, skip, count) in enumerate(zip(refs, (2, 0, 0), (3, 3, 1))):
        for k in range(count):
            at = pl.multiple_of(lax.rem(here + skip + k, 4) * cols, LANES)
            source = basis_hbm.at[:, pl.ds(at, SHARED)]
            target = ref.at[:, pl.ds(k * SHARED, SHARED)]
            copies.append(pltpu.make_async_copy(source, target, sems.at[side, k]))
    return copies


def stencil_kernel(
    levels_ref,
    index_ref,
    advect_ref,
    sum_ref,
    zlo_ref,
    zhi_ref,
    face_lo_ref,
    face_hi_ref,
    here_ref,
    basis_hbm,
    vel_hbm,
    outer_ref,
    inner_ref,
    out_ref,
    plus_ref,
    minus_ref,
    over_ref,
    field,
    first,
    boxed,
    sems,
    offer_sems,
):
    comp = pl.program_id(0)
    offer_refs = (plus_ref, minus_ref, over_ref)
    offers = offer_copies(here_ref[0], basis_hbm, offer_refs, offer_sems)
    cx, cz, ny = vel_hbm.shape[1:]
    inner = pl.ds(PAD, cz)

    def copies(c):
        return (
            pltpu.make_async_copy(
                vel_hbm.at[c], field.at[c, pl.ds(2, cx), inner, :], sems.at[c, 0, 0]
            ),
            *[
                pltpu.make_async_copy(
                    ref.at[pl.ds((2 * c + k) * cz, cz)],
                    field.at[c, face_plane(here_ref, side, 0, cx + 2) + k, inner, :],
                    sems.at[c, 1 + side, k],
                )
                for side, ref in enumerate((outer_ref, inner_ref))
                for k in range(2)
            ],
        )

    @pl.when(comp == 0)
    def _():
        for c in range(3):
            for copy in copies(c):
                copy.start()
        for copy in offers:
            copy.start()

    @pl.when(comp == pl.num_programs(0) - 1)
    def _():
        for copy in offers:
            copy.wait()

    coefs = coefficients(levels_ref, index_ref, advect_ref)

    def edge_row(ref, k):
        return ref[pl.ds(pl.multiple_of((2 * comp + k) * cx, 8), cx), :]

    zlo2, zlo1 = edge_row(zlo_ref, 0), edge_row(zlo_ref, 1)
    zhi1, zhi2 = edge_row(zhi_ref, 0), edge_row(zhi_ref, 1)
    spot = 6 * cz + 2 * comp
    first_core = here_ref[1] == 0

    def before_after(at):
        outer, other = outer_ref[pl.ds(at, 1), :], inner_ref[pl.ds(at, 1), :]
        return jnp.where(first_core, outer, other), jnp.where(first_core, other, outer)

    lo_before, lo_after = before_after(spot)
    hi_before, hi_after = before_after(spot + 1)
    plane = lax.broadcasted_iota(jnp.int32, (cx, ny), 0)

    def edge(row, before, after, north, south):
        east = jnp.where(plane == cx - 1, after, pltpu.roll(row, cx - 1, 0))
        west = jnp.where(plane == 0, before, pltpu.roll(row, 1, 0))
        return step(coefs, row, east, west, north, south)

    edge_lo = edge(zlo1, lo_before, lo_after, zlo2, edge_row(face_lo_ref, 0))
    edge_hi = edge(zhi1, hi_before, hi_after, edge_row(face_hi_ref, 1), zhi2)
    for i in range(cx):
        field[comp, 2 + i, PAD - 1 : PAD, :] = zlo1[i : i + 1]
        field[comp, 2 + i, PAD + cz : PAD + cz + 1, :] = zhi1[i : i + 1]
        first[1 + i, PAD - 1 : PAD, :] = edge_lo[i : i + 1]
        first[1 + i, PAD + cz : PAD + cz + 1, :] = edge_hi[i : i + 1]
    field[comp, 1, PAD - 1 : PAD, :] = lo_before
    field[comp, 1, PAD + cz : PAD + cz + 1, :] = hi_before
    field[comp, cx + 2, PAD - 1 : PAD, :] = lo_after
    field[comp, cx + 2, PAD + cz : PAD + cz + 1, :] = hi_after

    for copy in copies(comp):
        copy.wait()

    chunk = 16

    def first_plane(p, carry):
        for k in range(cz // chunk):
            at = PAD + k * chunk
            rows = pl.ds(at, chunk)
            first[p, rows, :] = step(
                coefs,
                field[comp, p + 1, rows, :],
                field[comp, p + 2, rows, :],
                field[comp, p, rows, :],
                field[comp, p + 1, pl.ds(at - 1, chunk), :],
                field[comp, p + 1, pl.ds(at + 1, chunk), :],
            )
        return carry

    lax.fori_loop(0, cx + 2, first_plane, 0)

    sums = sum_ref[...]
    lane = lax.broadcasted_iota(jnp.int32, (cz, LANES), 1)
    row = lax.broadcasted_iota(jnp.int32, (cz, LANES), 0)
    wanted = (lane // (LANES // 2)) == ((row // STRIDE) % 2)
    part = out_ref.shape[1] // vel_hbm.shape[0]
    offset = pl.multiple_of(comp * part, LANES)
    out_ref[:, pl.ds(offset, part)] = jnp.zeros((PAD, part), jnp.float32)

    def coarse(which, box):
        total = sum(
            jnp.dot(part, sums, preferred_element_type=jnp.float32)
            for part in split3(boxed[...])
        )
        total = jnp.where(wanted, total, 0.0)
        base = offset + box * (cz // 8 * LANES)
        for r in range(cz // 8):
            line = jnp.sum(total[8 * r : 8 * r + 8], axis=0, keepdims=True) * 0.125
            at = pl.multiple_of(base + r * LANES, LANES)
            out_ref[which : which + 1, pl.ds(at, LANES)] = line

    def box_step(box, carry):
        start = 1 + STRIDE * box
        for k in range(cz // chunk):
            rows = pl.ds(PAD + k * chunk, chunk)
            boxed[pl.ds(k * chunk, chunk), :] = (
                first[start, rows, :] + first[start + 1, rows, :]
            ) + (first[start + 2, rows, :] + first[start + 3, rows, :])
        coarse(0, box)
        for k in range(cz // chunk):
            at = PAD + k * chunk
            rows = pl.ds(at, chunk)
            total = None
            for i in range(STRIDE):
                p = start + i
                value = step(
                    coefs,
                    first[p, rows, :],
                    first[p + 1, rows, :],
                    first[p - 1, rows, :],
                    first[p, pl.ds(at - 1, chunk), :],
                    first[p, pl.ds(at + 1, chunk), :],
                )
                total = value if total is None else total + value
            boxed[pl.ds(k * chunk, chunk), :] = total
        coarse(1, box)
        return carry

    lax.fori_loop(0, cx // STRIDE, box_step, 0)

    @pl.when(comp == 0)
    def _():
        tiles = SHARED // LANES
        for k in range(2 * tiles):
            which, tile = divmod(k, tiles)
            line = out_ref[which : which + 1, tile * LANES : (tile + 1) * LANES]
            for ref in offer_refs:
                at = ref.shape[1] - FOLD + k // 8 * LANES
                ref[k % 8 : k % 8 + 1, at : at + LANES] = line


def snapshots(velocity, levels, profile_index, advect, here, basis, halos):
    comps, cx, cz, ny = velocity.shape
    cols = (cx // STRIDE) * (cz // STRIDE) * (ny // STRIDE)
    half = LANES // 2
    sums = np.zeros((ny, LANES), np.float32)
    for y in range(ny):
        sums[y, y // STRIDE] = 1.0
        sums[y, half + y // STRIDE] = 1.0
    return pl.pallas_call(
        stencil_kernel,
        grid=(comps,),
        in_specs=[
            SMEM_SPEC,
            pl.BlockSpec((1, ny), lambda c: (0, 0)),
            pl.BlockSpec((1, ny), lambda c: (0, 0)),
            pl.BlockSpec((ny, LANES), lambda c: (0, 0)),
            *[VMEM_SPEC] * 4,
            SMEM_SPEC,
            HBM_SPEC,
            HBM_SPEC,
            VMEM_SPEC,
            VMEM_SPEC,
        ],
        out_specs=[VMEM_SPEC] * 4,
        out_shape=[pltpu.VMEM((PAD, comps * cols), jnp.float32)]
        + [pltpu.VMEM((PAD, k * SHARED + FOLD), jnp.float32) for k in (3, 3, 1)],
        scratch_shapes=[
            pltpu.VMEM((comps, cx + 4, cz + 2 * PAD, ny), jnp.float32),
            pltpu.VMEM((cx + 2, cz + 2 * PAD, ny), jnp.float32),
            pltpu.VMEM((cz, ny), jnp.float32),
            pltpu.SemaphoreType.DMA((comps, 3, 2)),
            pltpu.SemaphoreType.DMA((3, 3)),
        ],
        compiler_params=pltpu.CompilerParams(vmem_limit_bytes=20 << 20),
        name="stencil",
    )(
        levels,
        profile_index.reshape(1, ny),
        advect.reshape(1, ny),
        jnp.asarray(sums, jnp.bfloat16),
        *[near(x) for x in halos[:4]],
        here,
        far(basis),
        far(halos[4]),
        *[near(x) for x in halos[5:]],
    )


def stacked(pieces, start, size):
    rows = []
    for piece in pieces:
        if isinstance(piece, tuple):
            ref, at = (piece[0], start) if start < SHARED else (piece[1], start - SHARED)
        else:
            ref, at = piece, start
        rows.append(ref[:, at : at + size])
    return jnp.concatenate(rows, axis=0)


def pieces_of(refs):
    snap, mine, hi, hi_tail, far_block, lo, lo_tail = refs
    return [snap, mine, (hi, hi_tail), far_block, (lo, lo_tail)]


def gram_kernel(here_ref, *refs, chunk):
    pieces, out_ref = pieces_of(refs[:-1]), refs[-1]
    here = here_ref[0]
    n, acc = ROWS, None
    for start in range(0, pieces[0].shape[1], chunk):
        stack = stacked(pieces, start, chunk)
        high = stack.astype(jnp.bfloat16).astype(jnp.float32)
        joined = jnp.concatenate([high, stack - high], axis=0).astype(jnp.bfloat16)
        part = lax.dot_general(
            joined, joined, (((1,), (1,)), ((), ())), preferred_element_type=jnp.float32
        )
        acc = part if acc is None else acc + part
    cross = acc[0:n, n : 2 * n] + acc[n : 2 * n, 0:n]
    total = acc[0:n, 0:n] + (cross + acc[n : 2 * n, n : 2 * n])
    total = jnp.concatenate([total, jnp.zeros((n, LANES - n), jnp.float32)], axis=1)
    lane = lax.broadcasted_iota(jnp.int32, (n, LANES), 1)
    turned = PAD + lax.rem(lane - PAD + MODES - PAD * here + MODES, MODES)
    inside = (lane >= PAD) & (lane < n)
    total = jnp.take_along_axis(total, jnp.where(inside, turned, lane), axis=1)
    out_ref[0:PAD, :] = total[0:PAD]
    for g in range(4):
        at = pl.multiple_of(PAD + PAD * lax.rem(here + g, 4), PAD)
        out_ref[pl.ds(at, PAD), :] = total[PAD + PAD * g : 2 * PAD + PAD * g]


def gram(here, stack, chunk=1024):
    return pl.pallas_call(
        functools.partial(gram_kernel, chunk=chunk),
        in_specs=[SMEM_SPEC] + [VMEM_SPEC] * 7,
        out_specs=VMEM_SPEC,
        out_shape=pltpu.VMEM((ROWS, LANES), jnp.float32),
        compiler_params=pltpu.CompilerParams(vmem_limit_bytes=8 << 20),
        name="gram",
    )(here, *[near(x) for x in stack])


def ring_moves(size, stride, width):
    moves = []
    for shift in range(1, width):
        pairs = []
        for i in range(size):
            k = (i // stride) % width
            pairs.append((i, i + ((k + shift) % width - k) * stride))
        moves.append(pairs)
    return moves


def ring_parts(x, axis, size, stride, width):
    return [lax.ppermute(x, axis, pairs) for pairs in ring_moves(size, stride, width)]


def ring_sum(x, parts):
    if len(parts) == 1:
        return x + parts[0]
    one, two, three = parts
    return (x + two) + (one + three)


def lane_sum(x):
    total = x[0:8]
    for k in range(1, ROWS // 8):
        total = total + x[8 * k : 8 * k + 8]
    total = total + pltpu.roll(total, 4, 0)
    total = total + pltpu.roll(total, 2, 0)
    return total + pltpu.roll(total, 1, 0)


def spread(x):
    return jnp.concatenate([x] * (ROWS // 8), axis=0)


def factor_kernel(
    g0_ref, g1_ref, g2_ref, g3_ref, partner_ref, orient_ref, keep_ref, mix_ref, sigma_ref
):
    a = (g0_ref[...] + g2_ref[...]) + (g1_ref[...] + g3_ref[...])
    lane = lax.broadcasted_iota(jnp.int32, (ROWS, LANES), 1)
    row = lax.broadcasted_iota(jnp.int32, (ROWS, LANES), 0)
    upper = jnp.zeros((ROWS, LANES), jnp.float32)
    places = [int(k) for k in PLACE]
    while places:
        block, places = places[:FACTOR_BLOCK], places[FACTOR_BLOCK:]
        lines = [jnp.broadcast_to(a[j : j + 1, :], (8, LANES)) for j in block]
        columns = [jnp.broadcast_to(a[:, j : j + 1], (ROWS, LANES)) for j in block]

        def entry(column, j):
            return jnp.broadcast_to(column[j : j + 1, :], (8, LANES))

        for i, j in enumerate(block):
            scale = lax.rsqrt(entry(columns[i], j))
            lines[i] = lines[i] * scale
            columns[i] = columns[i] * spread(scale)
            for k in range(i + 1, len(block)):
                cross = entry(columns[i], block[k])
                lines[k] = lines[k] - cross * lines[i]
                columns[k] = columns[k] - spread(cross) * columns[i]
        for i, j in enumerate(block):
            line = spread(lines[i])
            a = a - columns[i] * line
            upper = jnp.where((row == j) & (lane >= j), line, upper)

    def angle(x, y, sign):
        contrast = lane_sum(y * y) - lane_sum(x * x)
        inner = lane_sum(x * y)
        toward = jnp.where(contrast > 0.0, -1.0, jnp.where(contrast < 0.0, 1.0, sign))
        d = jnp.abs(contrast) + jnp.sqrt(contrast * contrast + 4.0 * inner * inner)
        positive = d > 0.0
        tangent = jnp.where(
            positive, 2.0 * inner * toward / jnp.where(positive, d, 1.0), 0.0
        )
        cosine = lax.rsqrt(1.0 + tangent * tangent)
        return spread(cosine), spread(cosine * tangent)

    def two_rounds(k, state):
        x, v = state
        moves = [
            jnp.broadcast_to(partner_ref[m, pl.ds(k, 1), :], (ROWS, LANES)) for m in range(3)
        ]
        signs = [
            jnp.broadcast_to(orient_ref[m, pl.ds(k, 1), :], (8, LANES)) for m in range(3)
        ]
        pair, after, cross = (jnp.take_along_axis(x, move, axis=1) for move in moves)
        c_self, s_self = angle(x, pair, signs[0])
        c_next, s_next = angle(after, cross, signs[1])
        x = c_self * x + s_self * pair
        after = c_next * after + s_next * cross
        c_last, s_last = angle(x, after, signs[2])
        x = c_last * x + s_last * after
        pair, after, cross = (jnp.take_along_axis(v, move, axis=1) for move in moves)
        v = c_self * v + s_self * pair
        after = c_next * after + s_next * cross
        return x, c_last * v + s_last * after

    eye = jnp.where(row == lane, 1.0, 0.0)
    x, v = lax.fori_loop(0, SWEEPS * (COUNT - 1) // 2, two_rounds, (upper, eye))
    keep = jnp.broadcast_to(keep_ref[...], (ROWS, LANES))
    sigma_ref[...] = jnp.take_along_axis(jnp.sqrt(lane_sum(x * x)), keep[0:8], axis=1)
    v = jnp.take_along_axis(v, keep, axis=1)
    high = v.astype(jnp.bfloat16).astype(jnp.float32)
    low = v - high
    mix = jnp.concatenate([high, high, low, jnp.zeros((8, LANES), jnp.float32)], axis=0)
    mix_ref[...] = jnp.transpose(mix)[0:MODES]


def factor(parts):
    tables = [near(jnp.asarray(table)) for table in pair_tables()]
    return pl.pallas_call(
        factor_kernel,
        in_specs=[VMEM_SPEC] * 7,
        out_specs=(VMEM_SPEC, VMEM_SPEC),
        out_shape=(
            pltpu.VMEM((MODES, LANES), jnp.float32),
            pltpu.VMEM((8, LANES), jnp.float32),
        ),
        compiler_params=pltpu.CompilerParams(vmem_limit_bytes=4 << 20),
        name="factor",
    )(*[near(x) for x in parts], *tables)


def turned_mix(mix, here):
    lane = lax.broadcasted_iota(jnp.int32, mix.shape, 1)
    inside = lax.rem(lane, ROWS)
    turned = lane - inside + PAD + lax.rem(inside + (MODES - PAD) + PAD * here, MODES)
    source = jnp.where((inside < PAD) | (lane >= 3 * ROWS), lane, turned)
    return jnp.take_along_axis(mix, source, axis=1).astype(jnp.bfloat16)


def mix_rows(mix_ref, here, g):
    at = pl.multiple_of(PAD * lax.rem(here + g, 4), PAD)
    return mix_ref[pl.ds(at, PAD), :]


def mixed(mix, stack):
    high = stack.astype(jnp.bfloat16).astype(jnp.float32)
    zero = jnp.zeros((8, stack.shape[1]), jnp.float32)
    joined = jnp.concatenate([high, stack - high, high, zero], axis=0)
    return jnp.dot(mix, joined.astype(jnp.bfloat16), preferred_element_type=jnp.float32)


def update_kernel(here_ref, mix_ref, *refs, chunk):
    pieces, out_refs = pieces_of(refs[:7]), refs[7:]
    here = here_ref[0]
    mix = jnp.concatenate([mix_rows(mix_ref, here, g) for g in range(4)], axis=0)
    mix = turned_mix(mix, here)
    for start in range(0, out_refs[0].shape[1], chunk):
        out = mixed(mix, stacked(pieces, SHARED + start, chunk))
        for g, ref in enumerate(out_refs):
            ref[:, start : start + chunk] = out[PAD * g : PAD * g + PAD]


def update(here, mix, stack, chunk=1024):
    cols = stack[0].shape[1] - SHARED
    return pl.pallas_call(
        functools.partial(update_kernel, chunk=chunk),
        in_specs=[SMEM_SPEC] + [VMEM_SPEC] * 8,
        out_specs=[VMEM_SPEC] * 4,
        out_shape=[pltpu.VMEM((PAD, cols), jnp.float32)] * 4,
        compiler_params=pltpu.CompilerParams(vmem_limit_bytes=8 << 20),
        name="update",
    )(here, near(mix), *[near(x) for x in stack])


def own_kernel(here_ref, mix_ref, *refs, cols, chunk):
    pieces, (hi_ref, over_ref, lo_ref, hi_far_ref, lo_far_ref) = pieces_of(refs[:7]), refs[7:12]
    basis_hbm, out_hbm, mine, snap, buf, in_sems, out_sems = refs[12:]
    here = here_ref[0]
    tiles = SHARED // LANES
    blocks = [lax.rem(here + 1 + b, 4) for b in range(4)]
    reads = []
    for b in range(3):
        at = pl.multiple_of(blocks[b] * cols, LANES)
        source = basis_hbm.at[:, pl.ds(at, SHARED)]
        reads.append(pltpu.make_async_copy(source, mine.at[b], in_sems.at[b]))
    for copy in reads:
        copy.start()
    mix = turned_mix(mix_rows(mix_ref, here, 0), here)
    for b, ref in enumerate((hi_ref, over_ref, lo_ref)):
        snap[b] = jnp.zeros((PAD, SHARED), jnp.float32)
        for k in range(2 * tiles):
            which, tile = divmod(k, tiles)
            at = ref.shape[1] - FOLD + k // 8 * LANES
            line = ref[k % 8 : k % 8 + 1, at : at + LANES]
            snap[b, which : which + 1, tile * LANES : (tile + 1) * LANES] = line
    for copy in reads:
        copy.wait()
    writes = []
    for b in range(4):
        for start in range(0, SHARED, chunk):
            at = slice(start, start + chunk)
            if b == 3:
                stack = stacked(pieces, start, chunk)
            else:
                wide = slice(b * SHARED + start, b * SHARED + start + chunk)
                opposite = (hi_far_ref, over_ref, lo_far_ref)[b]
                rows = [snap[b, :, at], mine[b, :, at]]
                rows += [hi_ref[:, wide], opposite[:, at], lo_ref[:, wide]]
                stack = jnp.concatenate(rows, axis=0)
            buf[b, :, at] = mixed(mix, stack)
        target = pl.ds(pl.multiple_of(blocks[b] * cols, LANES), SHARED)
        writes.append(pltpu.make_async_copy(buf.at[b], out_hbm.at[:, target], out_sems.at[b]))
        writes[-1].start()
    for copy in writes:
        copy.wait()


def own(here, mix, stack, received, basis, chunk=1024):
    cols = basis.shape[1] // 4
    return pl.pallas_call(
        functools.partial(own_kernel, cols=cols, chunk=chunk),
        in_specs=[SMEM_SPEC] + [VMEM_SPEC] * 13 + [HBM_SPEC],
        out_specs=HBM_SPEC,
        out_shape=pltpu.HBM(basis.shape, jnp.float32),
        scratch_shapes=[
            pltpu.VMEM((3, PAD, SHARED), jnp.float32),
            pltpu.VMEM((3, PAD, SHARED), jnp.float32),
            pltpu.VMEM((4, PAD, SHARED), jnp.float32),
            pltpu.SemaphoreType.DMA((3,)),
            pltpu.SemaphoreType.DMA((4,)),
        ],
        compiler_params=pltpu.CompilerParams(vmem_limit_bytes=10 << 20),
        name="own",
    )(here, *[near(x) for x in (mix, *stack, *received)], far(basis))


def join_kernel(here_ref, *refs, sources):
    parts, (_, out_hbm, sems) = refs[: len(sources)], refs[len(sources) :]
    cols = out_hbm.shape[1] // 4
    copies = []
    for g, part in zip(sources, parts):
        at = pl.multiple_of(lax.rem(here_ref[0] + g, 4) * cols + SHARED, LANES)
        target = out_hbm.at[:, pl.ds(at, cols - SHARED)]
        copies.append(pltpu.make_async_copy(part, target, sems.at[g]))
        copies[-1].start()
    for copy in copies:
        copy.wait()


def join(here, parts, whole):
    count = len(parts)
    return pl.pallas_call(
        functools.partial(join_kernel, sources=tuple(parts)),
        in_specs=[SMEM_SPEC] + [VMEM_SPEC] * count + [HBM_SPEC],
        out_specs=HBM_SPEC,
        out_shape=pltpu.HBM(whole.shape, jnp.float32),
        scratch_shapes=[pltpu.SemaphoreType.DMA((4,))],
        input_output_aliases={1 + count: 0},
        compiler_params=pltpu.CompilerParams(vmem_limit_bytes=2 << 20),
        name="join",
    )(here, *[near(x) for x in parts.values()], far(whole))


def program(velocity, basis, levels, profile_index, advect):
    n_space, n_mode = lax.axis_size("space"), lax.axis_size("mode")
    comps, cx, _, _ = velocity.shape
    places = (lax.axis_index("mode"), lax.rem(lax.axis_index("space"), 2))
    here = jnp.stack([place.astype(jnp.int32) for place in places])

    def shifted(x, axis, by):
        size = lax.axis_size(axis)
        return lax.ppermute(x, axis, [(i, (i + by) % size) for i in range(size)])

    face_lo, face_hi, outer, inner, *blocks = pack(here, velocity, basis)
    block_own, block_next, block_far, block_prev, tail_next, tail_prev = blocks
    zlo = shifted(face_hi, "mode", 1)
    zhi = shifted(face_lo, "mode", -1)
    lo = shifted(block_next, "mode", 1)
    hi = shifted(block_prev, "mode", -1)
    over = shifted(block_far, "mode", 2)
    outer, inner = add_corners(here, zlo, zhi, outer, inner, cx, comps)
    pairs = [(i, (i + (1 if i % 2 else -1)) % n_space) for i in range(n_space)]
    outer = lax.ppermute(outer, "space", pairs)
    inner = lax.ppermute(inner, "space", [(i, i ^ 1) for i in range(n_space)])
    lo_tail = shifted(tail_next, "mode", 1)
    hi_tail = shifted(tail_prev, "mode", -1)
    lo_far = shifted(lo, "mode", 1)
    hi_far = shifted(hi, "mode", -1)
    snap, plus, minus, across = snapshots(
        velocity,
        levels,
        profile_index,
        advect,
        here,
        basis,
        (zlo, zhi, face_lo, face_hi, velocity, outer, inner),
    )
    stack = (snap, block_own, hi, hi_tail, over, lo, lo_tail)
    total = gram(here, stack)
    total = ring_sum(total, ring_parts(total, "space", n_space, 1, 2))
    total = ring_sum(total, ring_parts(total, "mode", n_mode, 1, n_mode))
    total = ring_sum(total, ring_parts(total, "space", n_space, 2, 4))
    lo_early = shifted(plus, "mode", 1)
    hi_early = shifted(minus, "mode", -1)
    parts = [total] + ring_parts(total, "space", n_space, 8, 4)
    over_early = shifted(across, "mode", 2)
    mix, sigma = factor(parts)
    out_own, out_next, out_over, out_prev = update(here, mix, stack)
    back_lo = shifted(out_next, "mode", 1)
    back_hi = shifted(out_prev, "mode", -1)
    back_over = shifted(out_over, "mode", 2)
    mine = own(here, mix, stack, (hi_early, over_early, lo_early, hi_far, lo_far), basis)
    modes = join(here, {0: out_own, 1: back_hi, 3: back_lo}, mine)
    modes = join(here, {2: back_over}, modes)
    return (modes, sigma[0, :MODES])


def solution(mesh):
    return jax.shard_map(
        program,
        mesh=mesh,
        in_specs=(P(None, "space", "mode", None), P("mode", "space"), P(), P(), P()),
        out_specs=(P("mode", "space"), P()),
        check_vma=False,
    )
```

```python
import functools

import jax
import jax.numpy as jnp
import numpy as np
from jax import lax
from jax.experimental import pallas as pl
from jax.experimental.pallas import tpu as pltpu
from jax.sharding import PartitionSpec as P

STRIDE = 4
MODES = 32
SWEEPS = 2
FACTOR_BLOCK = 8
COUNT = 34
ROWS = 40
LANES = 128
PAD = 8
VMEM_SPEC = pl.BlockSpec(memory_space=pltpu.VMEM)
HBM_SPEC = pl.BlockSpec(memory_space=pltpu.HBM)
SMEM_SPEC = pl.BlockSpec(memory_space=pltpu.SMEM)


SHARED = 14336
EARLY = 6144
FOLD = SHARED // 4

PLACE = np.array([0, 1] + list(range(PAD, PAD + MODES)))


def near(x):
    return pltpu.with_memory_space_constraint(x, pltpu.VMEM)


def far(x):
    return pltpu.with_memory_space_constraint(x, pltpu.HBM)


def pair_tables():
    rounds = COUNT - 1
    partner = np.tile(np.arange(LANES), (rounds, 1))
    orient = np.ones((rounds, LANES), np.float32)
    for turn in range(rounds):
        players = [0] + [1 + (i - 1 + turn) % rounds for i in range(1, COUNT)]
        for k in range(COUNT // 2):
            lead, trail = PLACE[players[k]], PLACE[players[COUNT - 1 - k]]
            partner[turn, lead] = trail
            partner[turn, trail] = lead
            orient[turn, lead] = -1.0
    moves = np.zeros((3, ROWS, LANES), np.int32)
    signs = np.zeros((3, ROWS, LANES), np.float32)
    for k in range(rounds):
        one, two = 2 * k % rounds, (2 * k + 1) % rounds
        after = partner[two]
        moves[0, k], moves[1, k], moves[2, k] = partner[one], after, partner[one][after]
        signs[0, k], signs[1, k], signs[2, k] = orient[one], orient[one][after], orient[two]
    keep = np.zeros((1, LANES), np.int32)
    keep[0, :MODES] = PLACE[:MODES]
    return moves, signs, keep


def face_plane(core_ref, side, first, last):
    return jnp.where(core_ref[0] == side, first, last)


def pack_kernel(
    here_ref,
    core_ref,
    vel_hbm,
    basis_hbm,
    zfirst_ref,
    zlast_ref,
    outer_ref,
    inner_ref,
    mine_ref,
    next_ref,
    far_ref,
    prev_ref,
    buf,
    edge_sems,
    face_sems,
    block_sems,
):
    comps, cx, cz, _ = vel_hbm.shape
    cols = mine_ref.shape[1]
    edges, rest = [], []
    for c in range(comps):
        for side, at in enumerate((0, cz - PAD)):
            source = vel_hbm.at[c, :, pl.ds(at, PAD), :]
            edges.append(pltpu.make_async_copy(source, buf.at[c, side], edge_sems.at[c, side]))
        for side, ref in enumerate((outer_ref, inner_ref)):
            at = face_plane(core_ref, side, 0, cx - 2)
            for k in range(2):
                source = vel_hbm.at[c, at + k]
                target = ref.at[pl.ds((2 * c + k) * cz, cz)]
                rest.append(pltpu.make_async_copy(source, target, face_sems.at[c, side, k]))
    for k, ref in enumerate((mine_ref, next_ref, far_ref, prev_ref)):
        at = pl.multiple_of(lax.rem(here_ref[0] + k, 4) * cols, LANES)
        source = basis_hbm.at[:, pl.ds(at, cols)]
        rest.append(pltpu.make_async_copy(source, ref, block_sems.at[k]))
    for copy in edges + rest:
        copy.start()
    for copy in edges:
        copy.wait()
    for c in range(comps):
        for i in range(cx):
            for k in range(2):
                row, last = (2 * c + k) * cx + i, PAD - 2 + k
                zfirst_ref[row : row + 1, :] = buf[c, 0, i, k : k + 1, :]
                zlast_ref[row : row + 1, :] = buf[c, 1, i, last : last + 1, :]
    for copy in rest:
        copy.wait()


def pack(here, core, velocity, basis):
    comps, cx, cz, ny = velocity.shape
    edge = pltpu.VMEM((comps * 2 * cx, ny), jnp.float32)
    face = pltpu.VMEM((comps * 2 * cz + PAD, ny), jnp.float32)
    block = pltpu.VMEM((PAD, basis.shape[1] // 4), jnp.float32)
    return pl.pallas_call(
        pack_kernel,
        in_specs=[SMEM_SPEC, SMEM_SPEC, HBM_SPEC, HBM_SPEC],
        out_specs=[VMEM_SPEC] * 8,
        out_shape=[edge, edge, face, face] + [block] * 4,
        scratch_shapes=[
            pltpu.VMEM((comps, 2, cx, PAD, ny), jnp.float32),
            pltpu.SemaphoreType.DMA((comps, 2)),
            pltpu.SemaphoreType.DMA((comps, 2, 2)),
            pltpu.SemaphoreType.DMA((4,)),
        ],
        compiler_params=pltpu.CompilerParams(vmem_limit_bytes=4 << 20),
        name="pack",
    )(here, core, far(velocity), far(basis))


def corner_kernel(core_ref, zlo_ref, zhi_ref, _, __, outer_ref, inner_ref, *, cx, comps):
    base = outer_ref.shape[0] - PAD
    zero = jnp.zeros((PAD, outer_ref.shape[1]), jnp.float32)
    for side, ref in enumerate((outer_ref, inner_ref)):
        plane = face_plane(core_ref, side, 0, cx - 1)
        ref[base:, :] = zero
        for c in range(comps):
            at = base + 2 * c
            ref[at : at + 1, :] = zlo_ref[pl.ds((2 * c + 1) * cx + plane, 1), :]
            ref[at + 1 : at + 2, :] = zhi_ref[pl.ds(2 * c * cx + plane, 1), :]


def add_corners(core, zlo, zhi, outer, inner, cx, comps):
    face = pltpu.VMEM(outer.shape, jnp.float32)
    return pl.pallas_call(
        functools.partial(corner_kernel, cx=cx, comps=comps),
        in_specs=[SMEM_SPEC] + [VMEM_SPEC] * 4,
        out_specs=[VMEM_SPEC] * 2,
        out_shape=[face, face],
        input_output_aliases={3: 0, 4: 1},
        compiler_params=pltpu.CompilerParams(vmem_limit_bytes=1 << 20),
        name="corners",
    )(core, *[near(x) for x in (zlo, zhi, outer, inner)])


def coefficients(levels_ref, index_ref, advect_ref):
    index = index_ref[...]
    visc = jnp.zeros(index.shape, jnp.float32)
    for level in range(levels_ref.shape[0]):
        visc = jnp.where(index == level, levels_ref[level], visc)
    cells = index.shape[1]
    lane = lax.broadcasted_iota(jnp.int32, index.shape, 1)
    first, last = lane == 0, lane == cells - 1
    up = jnp.where(last, visc, 0.5 * (visc + pltpu.roll(visc, cells - 1, 1)))
    down = jnp.where(first, visc, 0.5 * (visc + pltpu.roll(visc, 1, 1)))
    half = 0.5 * advect_ref[...]
    return (
        1.0 - 4.0 * visc - up - down,
        visc,
        visc - half,
        visc + half,
        jnp.where(last, 0.0, up),
        jnp.where(first, 0.0, down),
    )


def step(coefs, center, east, west, north, south):
    mid, visc, c_east, c_west, c_up, c_down = coefs
    cells = center.shape[-1]
    upward = pltpu.roll(center, cells - 1, 1)
    downward = pltpu.roll(center, 1, 1)
    return (
        mid * center
        + visc * (north + south)
        + c_east * east
        + c_west * west
        + c_up * upward
        + c_down * downward
    )


def split3(x):
    high = x.astype(jnp.bfloat16)
    rest = x - high.astype(jnp.float32)
    middle = rest.astype(jnp.bfloat16)
    low = (rest - middle.astype(jnp.float32)).astype(jnp.bfloat16)
    return high, middle, low


def offer_copies(here, basis_hbm, refs, sems):
    cols = basis_hbm.shape[1] // 4
    copies = []
    spans = ((3, 0, EARLY), (3, EARLY, SHARED), (1, 0, EARLY), (1, EARLY, SHARED), (0, 0, SHARED))
    for i, (ref, (skip, first, last)) in enumerate(zip(refs, spans)):
        at = pl.multiple_of(lax.rem(here + skip, 4) * cols + first, LANES)
        source = basis_hbm.at[:, pl.ds(at, last - first)]
        copies.append(pltpu.make_async_copy(source, ref.at[:, 0 : last - first], sems.at[i]))
    return copies


def stencil_kernel(
    levels_ref,
    index_ref,
    advect_ref,
    sum_ref,
    zlo_ref,
    zhi_ref,
    face_lo_ref,
    face_hi_ref,
    here_ref,
    core_ref,
    basis_hbm,
    vel_hbm,
    outer_ref,
    inner_ref,
    out_ref,
    plus_ref,
    plus_rest_ref,
    minus_ref,
    minus_rest_ref,
    over_ref,
    field,
    first,
    boxed,
    sems,
    offer_sems,
):
    comp = pl.program_id(0)
    offer_refs = (plus_ref, plus_rest_ref, minus_ref, minus_rest_ref, over_ref)
    offers = offer_copies(here_ref[0], basis_hbm, offer_refs, offer_sems)
    cx, cz, ny = vel_hbm.shape[1:]
    inner = pl.ds(PAD, cz)

    def copies(c):
        return (
            pltpu.make_async_copy(
                vel_hbm.at[c], field.at[c, pl.ds(2, cx), inner, :], sems.at[c, 0, 0]
            ),
            *[
                pltpu.make_async_copy(
                    ref.at[pl.ds((2 * c + k) * cz, cz)],
                    field.at[c, face_plane(core_ref, side, 0, cx + 2) + k, inner, :],
                    sems.at[c, 1 + side, k],
                )
                for side, ref in enumerate((outer_ref, inner_ref))
                for k in range(2)
            ],
        )

    @pl.when(comp == 0)
    def _():
        for c in range(3):
            for copy in copies(c):
                copy.start()
        for copy in offers:
            copy.start()

    @pl.when(comp == pl.num_programs(0) - 1)
    def _():
        for copy in offers:
            copy.wait()

    coefs = coefficients(levels_ref, index_ref, advect_ref)

    def edge_row(ref, k):
        return ref[pl.ds(pl.multiple_of((2 * comp + k) * cx, 8), cx), :]

    zlo2, zlo1 = edge_row(zlo_ref, 0), edge_row(zlo_ref, 1)
    zhi1, zhi2 = edge_row(zhi_ref, 0), edge_row(zhi_ref, 1)
    spot = 6 * cz + 2 * comp
    first_core = core_ref[0] == 0

    def before_after(at):
        outer, other = outer_ref[pl.ds(at, 1), :], inner_ref[pl.ds(at, 1), :]
        return jnp.where(first_core, outer, other), jnp.where(first_core, other, outer)

    lo_before, lo_after = before_after(spot)
    hi_before, hi_after = before_after(spot + 1)
    plane = lax.broadcasted_iota(jnp.int32, (cx, ny), 0)

    def edge(row, before, after, north, south):
        east = jnp.where(plane == cx - 1, after, pltpu.roll(row, cx - 1, 0))
        west = jnp.where(plane == 0, before, pltpu.roll(row, 1, 0))
        return step(coefs, row, east, west, north, south)

    edge_lo = edge(zlo1, lo_before, lo_after, zlo2, edge_row(face_lo_ref, 0))
    edge_hi = edge(zhi1, hi_before, hi_after, edge_row(face_hi_ref, 1), zhi2)
    for i in range(cx):
        field[comp, 2 + i, PAD - 1 : PAD, :] = zlo1[i : i + 1]
        field[comp, 2 + i, PAD + cz : PAD + cz + 1, :] = zhi1[i : i + 1]
        first[1 + i, PAD - 1 : PAD, :] = edge_lo[i : i + 1]
        first[1 + i, PAD + cz : PAD + cz + 1, :] = edge_hi[i : i + 1]
    field[comp, 1, PAD - 1 : PAD, :] = lo_before
    field[comp, 1, PAD + cz : PAD + cz + 1, :] = hi_before
    field[comp, cx + 2, PAD - 1 : PAD, :] = lo_after
    field[comp, cx + 2, PAD + cz : PAD + cz + 1, :] = hi_after

    for copy in copies(comp):
        copy.wait()

    chunk = 16

    def first_plane(p, carry):
        for k in range(cz // chunk):
            at = PAD + k * chunk
            rows = pl.ds(at, chunk)
            first[p, rows, :] = step(
                coefs,
                field[comp, p + 1, rows, :],
                field[comp, p + 2, rows, :],
                field[comp, p, rows, :],
                field[comp, p + 1, pl.ds(at - 1, chunk), :],
                field[comp, p + 1, pl.ds(at + 1, chunk), :],
            )
        return carry

    lax.fori_loop(0, cx + 2, first_plane, 0)

    sums = sum_ref[...]
    lane = lax.broadcasted_iota(jnp.int32, (cz, LANES), 1)
    row = lax.broadcasted_iota(jnp.int32, (cz, LANES), 0)
    wanted = (lane // (LANES // 2)) == ((row // STRIDE) % 2)
    part = out_ref.shape[1] // vel_hbm.shape[0]
    offset = pl.multiple_of(comp * part, LANES)
    out_ref[:, pl.ds(offset, part)] = jnp.zeros((PAD, part), jnp.float32)

    def coarse(which, box):
        total = sum(
            jnp.dot(part, sums, preferred_element_type=jnp.float32)
            for part in split3(boxed[...])
        )
        total = jnp.where(wanted, total, 0.0)
        base = offset + box * (cz // 8 * LANES)
        for r in range(cz // 8):
            line = jnp.sum(total[8 * r : 8 * r + 8], axis=0, keepdims=True) * 0.125
            at = pl.multiple_of(base + r * LANES, LANES)
            out_ref[which : which + 1, pl.ds(at, LANES)] = line

    def box_step(box, carry):
        start = 1 + STRIDE * box
        for k in range(cz // chunk):
            rows = pl.ds(PAD + k * chunk, chunk)
            boxed[pl.ds(k * chunk, chunk), :] = (
                first[start, rows, :] + first[start + 1, rows, :]
            ) + (first[start + 2, rows, :] + first[start + 3, rows, :])
        coarse(0, box)
        for k in range(cz // chunk):
            at = PAD + k * chunk
            rows = pl.ds(at, chunk)
            total = None
            for i in range(STRIDE):
                p = start + i
                value = step(
                    coefs,
                    first[p, rows, :],
                    first[p + 1, rows, :],
                    first[p - 1, rows, :],
                    first[p, pl.ds(at - 1, chunk), :],
                    first[p, pl.ds(at + 1, chunk), :],
                )
                total = value if total is None else total + value
            boxed[pl.ds(k * chunk, chunk), :] = total
        coarse(1, box)
        return carry

    lax.fori_loop(0, cx // STRIDE, box_step, 0)

    @pl.when(comp == pl.num_programs(0) - 1)
    def _():
        tiles = SHARED // LANES
        for k in range(2 * tiles):
            which, tile = divmod(k, tiles)
            line = out_ref[which : which + 1, tile * LANES : (tile + 1) * LANES]
            at = SHARED + k // 8 * LANES
            over_ref[k % 8 : k % 8 + 1, at : at + LANES] = line


def snapshots(velocity, levels, profile_index, advect, here, core, basis, halos):
    comps, cx, cz, ny = velocity.shape
    cols = (cx // STRIDE) * (cz // STRIDE) * (ny // STRIDE)
    half = LANES // 2
    sums = np.zeros((ny, LANES), np.float32)
    for y in range(ny):
        sums[y, y // STRIDE] = 1.0
        sums[y, half + y // STRIDE] = 1.0
    return pl.pallas_call(
        stencil_kernel,
        grid=(comps,),
        in_specs=[
            SMEM_SPEC,
            pl.BlockSpec((1, ny), lambda c: (0, 0)),
            pl.BlockSpec((1, ny), lambda c: (0, 0)),
            pl.BlockSpec((ny, LANES), lambda c: (0, 0)),
            *[VMEM_SPEC] * 4,
            SMEM_SPEC,
            SMEM_SPEC,
            HBM_SPEC,
            HBM_SPEC,
            VMEM_SPEC,
            VMEM_SPEC,
        ],
        out_specs=[VMEM_SPEC] * 6,
        out_shape=[pltpu.VMEM((PAD, comps * cols), jnp.float32)]
        + [pltpu.VMEM((PAD, size), jnp.float32) for size in (EARLY, SHARED - EARLY) * 2]
        + [pltpu.VMEM((PAD, SHARED + FOLD), jnp.float32)],
        scratch_shapes=[
            pltpu.VMEM((comps, cx + 4, cz + 2 * PAD, ny), jnp.float32),
            pltpu.VMEM((cx + 2, cz + 2 * PAD, ny), jnp.float32),
            pltpu.VMEM((cz, ny), jnp.float32),
            pltpu.SemaphoreType.DMA((comps, 3, 2)),
            pltpu.SemaphoreType.DMA((5,)),
        ],
        compiler_params=pltpu.CompilerParams(vmem_limit_bytes=20 << 20),
        name="stencil",
    )(
        levels,
        profile_index.reshape(1, ny),
        advect.reshape(1, ny),
        jnp.asarray(sums, jnp.bfloat16),
        *[near(x) for x in halos[:4]],
        here,
        core,
        far(basis),
        far(halos[4]),
        *[near(x) for x in halos[5:]],
    )


def stacked(refs, start, size):
    return jnp.concatenate([ref[:, start : start + size] for ref in refs], axis=0)


def gram_kernel(here_ref, *refs, chunk):
    pieces, out_ref = refs[:-1], refs[-1]
    here = here_ref[0]
    n, acc = ROWS, None
    for start in range(0, pieces[0].shape[1], chunk):
        stack = stacked(pieces, start, chunk)
        high = stack.astype(jnp.bfloat16).astype(jnp.float32)
        joined = jnp.concatenate([high, stack - high], axis=0).astype(jnp.bfloat16)
        part = lax.dot_general(
            joined, joined, (((1,), (1,)), ((), ())), preferred_element_type=jnp.float32
        )
        acc = part if acc is None else acc + part
    cross = acc[0:n, n : 2 * n] + acc[n : 2 * n, 0:n]
    total = acc[0:n, 0:n] + (cross + acc[n : 2 * n, n : 2 * n])
    total = jnp.concatenate([total, jnp.zeros((n, LANES - n), jnp.float32)], axis=1)
    lane = lax.broadcasted_iota(jnp.int32, (n, LANES), 1)
    turned = PAD + lax.rem(lane - PAD + MODES - PAD * here + MODES, MODES)
    inside = (lane >= PAD) & (lane < n)
    total = jnp.take_along_axis(total, jnp.where(inside, turned, lane), axis=1)
    out_ref[0:PAD, :] = total[0:PAD]
    for g in range(4):
        at = pl.multiple_of(PAD + PAD * lax.rem(here + g, 4), PAD)
        out_ref[pl.ds(at, PAD), :] = total[PAD + PAD * g : 2 * PAD + PAD * g]


def gram(here, stack, chunk=2048):
    return pl.pallas_call(
        functools.partial(gram_kernel, chunk=chunk),
        in_specs=[SMEM_SPEC] + [VMEM_SPEC] * 5,
        out_specs=VMEM_SPEC,
        out_shape=pltpu.VMEM((ROWS, LANES), jnp.float32),
        compiler_params=pltpu.CompilerParams(vmem_limit_bytes=8 << 20),
        name="gram",
    )(here, *[near(x) for x in stack])


def ring_moves(size, stride, width):
    moves = []
    for shift in range(1, width):
        pairs = []
        for i in range(size):
            k = (i // stride) % width
            pairs.append((i, i + ((k + shift) % width - k) * stride))
        moves.append(pairs)
    return moves


def ring_parts(x, axis, size, stride, width):
    return [lax.ppermute(x, axis, pairs) for pairs in ring_moves(size, stride, width)]


def ring_sum(x, parts):
    if len(parts) == 1:
        return x + parts[0]
    one, two, three = parts
    return (x + two) + (one + three)


def lane_sum(x):
    total = x[0:8]
    for k in range(1, ROWS // 8):
        total = total + x[8 * k : 8 * k + 8]
    total = total + pltpu.roll(total, 4, 0)
    total = total + pltpu.roll(total, 2, 0)
    return total + pltpu.roll(total, 1, 0)


def spread(x):
    return jnp.concatenate([x] * (ROWS // 8), axis=0)


def factor_kernel(
    g0_ref, g1_ref, g2_ref, g3_ref, partner_ref, orient_ref, keep_ref, mix_ref, sigma_ref
):
    a = (g0_ref[...] + g2_ref[...]) + (g1_ref[...] + g3_ref[...])
    lane = lax.broadcasted_iota(jnp.int32, (ROWS, LANES), 1)
    row = lax.broadcasted_iota(jnp.int32, (ROWS, LANES), 0)
    upper = jnp.zeros((ROWS, LANES), jnp.float32)
    places = [int(k) for k in PLACE]
    while places:
        block, places = places[:FACTOR_BLOCK], places[FACTOR_BLOCK:]
        lines = [jnp.broadcast_to(a[j : j + 1, :], (8, LANES)) for j in block]
        columns = [jnp.broadcast_to(a[:, j : j + 1], (ROWS, LANES)) for j in block]

        def entry(column, j):
            return jnp.broadcast_to(column[j : j + 1, :], (8, LANES))

        for i, j in enumerate(block):
            scale = lax.rsqrt(entry(columns[i], j))
            lines[i] = lines[i] * scale
            columns[i] = columns[i] * spread(scale)
            for k in range(i + 1, len(block)):
                cross = entry(columns[i], block[k])
                lines[k] = lines[k] - cross * lines[i]
                columns[k] = columns[k] - spread(cross) * columns[i]
        for i, j in enumerate(block):
            line = spread(lines[i])
            a = a - columns[i] * line
            upper = jnp.where((row == j) & (lane >= j), line, upper)

    def angle(x, y, sign):
        contrast = lane_sum(y * y) - lane_sum(x * x)
        inner = lane_sum(x * y)
        toward = jnp.where(contrast > 0.0, -1.0, jnp.where(contrast < 0.0, 1.0, sign))
        d = jnp.abs(contrast) + jnp.sqrt(contrast * contrast + 4.0 * inner * inner)
        positive = d > 0.0
        tangent = jnp.where(
            positive, 2.0 * inner * toward / jnp.where(positive, d, 1.0), 0.0
        )
        cosine = lax.rsqrt(1.0 + tangent * tangent)
        return spread(cosine), spread(cosine * tangent)

    def two_rounds(k, state):
        x, v = state
        moves = [
            jnp.broadcast_to(partner_ref[m, pl.ds(k, 1), :], (ROWS, LANES)) for m in range(3)
        ]
        signs = [
            jnp.broadcast_to(orient_ref[m, pl.ds(k, 1), :], (8, LANES)) for m in range(3)
        ]
        pair, after, cross = (jnp.take_along_axis(x, move, axis=1) for move in moves)
        c_self, s_self = angle(x, pair, signs[0])
        c_next, s_next = angle(after, cross, signs[1])
        x = c_self * x + s_self * pair
        after = c_next * after + s_next * cross
        c_last, s_last = angle(x, after, signs[2])
        x = c_last * x + s_last * after
        pair, after, cross = (jnp.take_along_axis(v, move, axis=1) for move in moves)
        v = c_self * v + s_self * pair
        after = c_next * after + s_next * cross
        return x, c_last * v + s_last * after

    eye = jnp.where(row == lane, 1.0, 0.0)
    x, v = lax.fori_loop(0, SWEEPS * (COUNT - 1) // 2, two_rounds, (upper, eye))
    keep = jnp.broadcast_to(keep_ref[...], (ROWS, LANES))
    sigma_ref[...] = jnp.take_along_axis(jnp.sqrt(lane_sum(x * x)), keep[0:8], axis=1)
    v = jnp.take_along_axis(v, keep, axis=1)
    high = v.astype(jnp.bfloat16).astype(jnp.float32)
    low = v - high
    mix = jnp.concatenate([high, high, low, jnp.zeros((8, LANES), jnp.float32)], axis=0)
    mix_ref[...] = jnp.transpose(mix)[0:MODES]


def factor(parts):
    tables = [near(jnp.asarray(table)) for table in pair_tables()]
    return pl.pallas_call(
        factor_kernel,
        in_specs=[VMEM_SPEC] * 7,
        out_specs=(VMEM_SPEC, VMEM_SPEC),
        out_shape=(
            pltpu.VMEM((MODES, LANES), jnp.float32),
            pltpu.VMEM((8, LANES), jnp.float32),
        ),
        compiler_params=pltpu.CompilerParams(vmem_limit_bytes=4 << 20),
        name="factor",
    )(*[near(x) for x in parts], *tables)


def turned_mix(mix, here):
    lane = lax.broadcasted_iota(jnp.int32, mix.shape, 1)
    inside = lax.rem(lane, ROWS)
    turned = lane - inside + PAD + lax.rem(inside + (MODES - PAD) + PAD * here, MODES)
    source = jnp.where((inside < PAD) | (lane >= 3 * ROWS), lane, turned)
    return jnp.take_along_axis(mix, source, axis=1).astype(jnp.bfloat16)


def mix_rows(mix_ref, here, g):
    at = pl.multiple_of(PAD * lax.rem(here + g, 4), PAD)
    return mix_ref[pl.ds(at, PAD), :]


def mixed(mix, stack):
    high = stack.astype(jnp.bfloat16).astype(jnp.float32)
    zero = jnp.zeros((8, stack.shape[1]), jnp.float32)
    joined = jnp.concatenate([high, stack - high, high, zero], axis=0)
    return jnp.dot(mix, joined.astype(jnp.bfloat16), preferred_element_type=jnp.float32)


def update_kernel(here_ref, mix_ref, *refs, chunk):
    pieces, out_refs = refs[:5], refs[5:]
    here = here_ref[0]
    mix = jnp.concatenate([mix_rows(mix_ref, here, g) for g in range(4)], axis=0)
    mix = turned_mix(mix, here)
    for start in range(0, out_refs[0].shape[1], chunk):
        out = mixed(mix, stacked(pieces, start, chunk))
        for g, ref in enumerate(out_refs):
            at = start - (pieces[0].shape[1] - ref.shape[1])
            if at >= 0:
                ref[:, at : at + chunk] = out[PAD * g : PAD * g + PAD]


def update(here, mix, stack, chunk=1024):
    cols = stack[0].shape[1]
    sizes = (cols, cols, cols - SHARED, cols)
    return pl.pallas_call(
        functools.partial(update_kernel, chunk=chunk),
        in_specs=[SMEM_SPEC] + [VMEM_SPEC] * 6,
        out_specs=[VMEM_SPEC] * 4,
        out_shape=[pltpu.VMEM((PAD, size), jnp.float32) for size in sizes],
        compiler_params=pltpu.CompilerParams(vmem_limit_bytes=8 << 20),
        name="update",
    )(here, near(mix), *[near(x) for x in stack])


def own_kernel(here_ref, mix_ref, *refs, cols, chunk):
    hi_ref, hi_rest_ref, over_ref, lo_ref, lo_rest_ref = refs[:5]
    basis_hbm, out_hbm, mine, snap, buf, in_sem, out_sem = refs[5:]
    here = here_ref[0]
    tiles = SHARED // LANES
    spot = pl.ds(pl.multiple_of(lax.rem(here + 2, 4) * cols, LANES), SHARED)
    read = pltpu.make_async_copy(basis_hbm.at[:, spot], mine, in_sem)
    read.start()
    mix = turned_mix(mix_rows(mix_ref, here, 0), here)
    snap[...] = jnp.zeros((PAD, SHARED), jnp.float32)
    for k in range(2 * tiles):
        which, tile = divmod(k, tiles)
        at = SHARED + k // 8 * LANES
        line = over_ref[k % 8 : k % 8 + 1, at : at + LANES]
        snap[which : which + 1, tile * LANES : (tile + 1) * LANES] = line
    read.wait()
    for start in range(0, SHARED, chunk):
        at = slice(start, start + chunk)
        if start < EARLY:
            hi, lo = hi_ref[:, at], lo_ref[:, at]
        else:
            rest = slice(start - EARLY, start - EARLY + chunk)
            hi, lo = hi_rest_ref[:, rest], lo_rest_ref[:, rest]
        stack = jnp.concatenate([snap[:, at], mine[:, at], hi, over_ref[:, at], lo], axis=0)
        buf[:, at] = mixed(mix, stack)
    write = pltpu.make_async_copy(buf, out_hbm.at[:, spot], out_sem)
    write.start()
    write.wait()


def own(here, mix, received, basis, chunk=1024):
    cols = basis.shape[1] // 4
    return pl.pallas_call(
        functools.partial(own_kernel, cols=cols, chunk=chunk),
        in_specs=[SMEM_SPEC] + [VMEM_SPEC] * 6 + [HBM_SPEC],
        out_specs=HBM_SPEC,
        out_shape=pltpu.HBM(basis.shape, jnp.float32),
        scratch_shapes=[pltpu.VMEM((PAD, SHARED), jnp.float32)] * 3
        + [pltpu.SemaphoreType.DMA(())] * 2,
        compiler_params=pltpu.CompilerParams(vmem_limit_bytes=10 << 20),
        name="own",
    )(here, *[near(x) for x in (mix, *received)], far(basis))


def join_kernel(here_ref, *refs, sources):
    parts, (_, out_hbm, sems) = refs[: len(sources)], refs[len(sources) :]
    cols = out_hbm.shape[1] // 4
    copies = []
    for g, part in zip(sources, parts):
        size = part.shape[1]
        at = pl.multiple_of(lax.rem(here_ref[0] + g, 4) * cols + cols - size, LANES)
        target = out_hbm.at[:, pl.ds(at, size)]
        copies.append(pltpu.make_async_copy(part, target, sems.at[g]))
        copies[-1].start()
    for copy in copies:
        copy.wait()


def join(here, parts, whole):
    count = len(parts)
    return pl.pallas_call(
        functools.partial(join_kernel, sources=tuple(parts)),
        in_specs=[SMEM_SPEC] + [VMEM_SPEC] * count + [HBM_SPEC],
        out_specs=HBM_SPEC,
        out_shape=pltpu.HBM(whole.shape, jnp.float32),
        scratch_shapes=[pltpu.SemaphoreType.DMA((4,))],
        input_output_aliases={1 + count: 0},
        compiler_params=pltpu.CompilerParams(vmem_limit_bytes=2 << 20),
        name="join",
    )(here, *[near(x) for x in parts.values()], far(whole))


def program(velocity, basis, levels, profile_index, advect):
    n_space, n_mode = lax.axis_size("space"), lax.axis_size("mode")
    comps, cx, _, _ = velocity.shape
    here = lax.axis_index("mode").astype(jnp.int32).reshape(1)
    core = lax.rem(lax.axis_index("space").astype(jnp.int32), 2).reshape(1)

    def shifted(x, axis, by):
        size = lax.axis_size(axis)
        return lax.ppermute(x, axis, [(i, (i + by) % size) for i in range(size)])

    face_lo, face_hi, outer, inner, *blocks = pack(here, core, velocity, basis)
    block_own, block_next, block_far, block_prev = blocks
    zlo = shifted(face_hi, "mode", 1)
    zhi = shifted(face_lo, "mode", -1)
    lo = shifted(block_next, "mode", 1)
    hi = shifted(block_prev, "mode", -1)
    over = shifted(block_far, "mode", 2)
    outer, inner = add_corners(core, zlo, zhi, outer, inner, cx, comps)
    pairs = [(i, (i + (1 if i % 2 else -1)) % n_space) for i in range(n_space)]
    outer = lax.ppermute(outer, "space", pairs)
    inner = lax.ppermute(inner, "space", [(i, i ^ 1) for i in range(n_space)])
    snap, plus, plus_rest, minus, minus_rest, across = snapshots(
        velocity,
        levels,
        profile_index,
        advect,
        here,
        core,
        basis,
        (zlo, zhi, face_lo, face_hi, velocity, outer, inner),
    )
    lo_early = shifted(plus, "mode", 1)
    hi_early = shifted(minus, "mode", -1)
    stack = (snap, block_own, hi, over, lo)
    total = gram(here, stack)
    total = ring_sum(total, ring_parts(total, "space", n_space, 1, 2))
    total = ring_sum(total, ring_parts(total, "mode", n_mode, 1, n_mode))
    total = ring_sum(total, ring_parts(total, "space", n_space, 2, 4))
    lo_rest = shifted(plus_rest, "mode", 1)
    hi_rest = shifted(minus_rest, "mode", -1)
    parts = [total] + ring_parts(total, "space", n_space, 8, 4)
    over_early = shifted(across, "mode", 2)
    mix, sigma = factor(parts)
    out_own, out_next, out_over, out_prev = update(here, mix, stack)
    back_lo = shifted(out_next, "mode", 1)
    back_hi = shifted(out_prev, "mode", -1)
    back_over = shifted(out_over, "mode", 2)
    received = (hi_early, hi_rest, over_early, lo_early, lo_rest)
    mine = own(here, mix, received, basis)
    modes = join(here, {0: out_own, 1: back_hi, 3: back_lo}, mine)
    modes = join(here, {2: back_over}, modes)
    return (modes, sigma[0, :MODES])


def solution(mesh):
    return jax.shard_map(
        program,
        mesh=mesh,
        in_specs=(P(None, "space", "mode", None), P("mode", "space"), P(), P(), P()),
        out_specs=(P("mode", "space"), P()),
        check_vma=False,
    )
```

```python
import functools

import jax
import jax.numpy as jnp
import numpy as np
from jax import lax
from jax.experimental import pallas as pl
from jax.experimental.pallas import tpu as pltpu
from jax.sharding import PartitionSpec as P

STRIDE = 4
MODES = 32
SWEEPS = 2
FACTOR_BLOCK = 8
COUNT = 34
ROWS = 40
LANES = 128
PAD = 8
VMEM_SPEC = pl.BlockSpec(memory_space=pltpu.VMEM)
HBM_SPEC = pl.BlockSpec(memory_space=pltpu.HBM)
SMEM_SPEC = pl.BlockSpec(memory_space=pltpu.SMEM)


SHARED = 12288
FOLD = SHARED // 4

PLACE = np.array([0, 1] + list(range(PAD, PAD + MODES)))


def near(x):
    return pltpu.with_memory_space_constraint(x, pltpu.VMEM)


def far(x):
    return pltpu.with_memory_space_constraint(x, pltpu.HBM)


def pair_tables():
    rounds = COUNT - 1
    partner = np.tile(np.arange(LANES), (rounds, 1))
    orient = np.ones((rounds, LANES), np.float32)
    for turn in range(rounds):
        players = [0] + [1 + (i - 1 + turn) % rounds for i in range(1, COUNT)]
        for k in range(COUNT // 2):
            lead, trail = PLACE[players[k]], PLACE[players[COUNT - 1 - k]]
            partner[turn, lead] = trail
            partner[turn, trail] = lead
            orient[turn, lead] = -1.0
    moves = np.zeros((3, ROWS, LANES), np.int32)
    signs = np.zeros((3, ROWS, LANES), np.float32)
    for k in range(rounds):
        one, two = 2 * k % rounds, (2 * k + 1) % rounds
        after = partner[two]
        moves[0, k], moves[1, k], moves[2, k] = partner[one], after, partner[one][after]
        signs[0, k], signs[1, k], signs[2, k] = orient[one], orient[one][after], orient[two]
    keep = np.zeros((1, LANES), np.int32)
    keep[0, :MODES] = PLACE[:MODES]
    return moves, signs, keep


def face_plane(core_ref, side, first, last):
    return jnp.where(core_ref[0] == side, first, last)


def pack_kernel(
    here_ref,
    core_ref,
    vel_hbm,
    basis_hbm,
    zfirst_ref,
    zlast_ref,
    outer_ref,
    inner_ref,
    mine_ref,
    next_ref,
    far_ref,
    prev_ref,
    buf,
    edge_sems,
    face_sems,
    block_sems,
):
    comps, cx, cz, _ = vel_hbm.shape
    cols = mine_ref.shape[1]
    edges, rest = [], []
    for c in range(comps):
        for side, at in enumerate((0, cz - PAD)):
            source = vel_hbm.at[c, :, pl.ds(at, PAD), :]
            edges.append(pltpu.make_async_copy(source, buf.at[c, side], edge_sems.at[c, side]))
        for side, ref in enumerate((outer_ref, inner_ref)):
            at = face_plane(core_ref, side, 0, cx - 2)
            for k in range(2):
                source = vel_hbm.at[c, at + k]
                target = ref.at[pl.ds((2 * c + k) * cz, cz)]
                rest.append(pltpu.make_async_copy(source, target, face_sems.at[c, side, k]))
    for k, ref in enumerate((mine_ref, next_ref, far_ref, prev_ref)):
        at = pl.multiple_of(lax.rem(here_ref[0] + k, 4) * cols, LANES)
        source = basis_hbm.at[:, pl.ds(at, cols)]
        rest.append(pltpu.make_async_copy(source, ref, block_sems.at[k]))
    for copy in edges + rest:
        copy.start()
    for copy in edges:
        copy.wait()
    for c in range(comps):
        for i in range(cx):
            for k in range(2):
                row, last = (2 * c + k) * cx + i, PAD - 2 + k
                zfirst_ref[row : row + 1, :] = buf[c, 0, i, k : k + 1, :]
                zlast_ref[row : row + 1, :] = buf[c, 1, i, last : last + 1, :]
    for copy in rest:
        copy.wait()


def pack(here, core, velocity, basis):
    comps, cx, cz, ny = velocity.shape
    edge = pltpu.VMEM((comps * 2 * cx, ny), jnp.float32)
    face = pltpu.VMEM((comps * 2 * cz + PAD, ny), jnp.float32)
    block = pltpu.VMEM((PAD, basis.shape[1] // 4), jnp.float32)
    return pl.pallas_call(
        pack_kernel,
        in_specs=[SMEM_SPEC, SMEM_SPEC, HBM_SPEC, HBM_SPEC],
        out_specs=[VMEM_SPEC] * 8,
        out_shape=[edge, edge, face, face] + [block] * 4,
        scratch_shapes=[
            pltpu.VMEM((comps, 2, cx, PAD, ny), jnp.float32),
            pltpu.SemaphoreType.DMA((comps, 2)),
            pltpu.SemaphoreType.DMA((comps, 2, 2)),
            pltpu.SemaphoreType.DMA((4,)),
        ],
        compiler_params=pltpu.CompilerParams(vmem_limit_bytes=4 << 20),
        name="pack",
    )(here, core, far(velocity), far(basis))


def corner_kernel(core_ref, zlo_ref, zhi_ref, _, __, outer_ref, inner_ref, *, cx, comps):
    base = outer_ref.shape[0] - PAD
    zero = jnp.zeros((PAD, outer_ref.shape[1]), jnp.float32)
    for side, ref in enumerate((outer_ref, inner_ref)):
        plane = face_plane(core_ref, side, 0, cx - 1)
        ref[base:, :] = zero
        for c in range(comps):
            at = base + 2 * c
            ref[at : at + 1, :] = zlo_ref[pl.ds((2 * c + 1) * cx + plane, 1), :]
            ref[at + 1 : at + 2, :] = zhi_ref[pl.ds(2 * c * cx + plane, 1), :]


def add_corners(core, zlo, zhi, outer, inner, cx, comps):
    face = pltpu.VMEM(outer.shape, jnp.float32)
    return pl.pallas_call(
        functools.partial(corner_kernel, cx=cx, comps=comps),
        in_specs=[SMEM_SPEC] + [VMEM_SPEC] * 4,
        out_specs=[VMEM_SPEC] * 2,
        out_shape=[face, face],
        input_output_aliases={3: 0, 4: 1},
        compiler_params=pltpu.CompilerParams(vmem_limit_bytes=1 << 20),
        name="corners",
    )(core, *[near(x) for x in (zlo, zhi, outer, inner)])


def coefficients(levels_ref, index_ref, advect_ref):
    index = index_ref[...]
    visc = jnp.zeros(index.shape, jnp.float32)
    for level in range(levels_ref.shape[0]):
        visc = jnp.where(index == level, levels_ref[level], visc)
    cells = index.shape[1]
    lane = lax.broadcasted_iota(jnp.int32, index.shape, 1)
    first, last = lane == 0, lane == cells - 1
    up = jnp.where(last, visc, 0.5 * (visc + pltpu.roll(visc, cells - 1, 1)))
    down = jnp.where(first, visc, 0.5 * (visc + pltpu.roll(visc, 1, 1)))
    half = 0.5 * advect_ref[...]
    return (
        1.0 - 4.0 * visc - up - down,
        visc,
        visc - half,
        visc + half,
        jnp.where(last, 0.0, up),
        jnp.where(first, 0.0, down),
    )


def step(coefs, center, east, west, north, south):
    mid, visc, c_east, c_west, c_up, c_down = coefs
    cells = center.shape[-1]
    upward = pltpu.roll(center, cells - 1, 1)
    downward = pltpu.roll(center, 1, 1)
    return (
        mid * center
        + visc * (north + south)
        + c_east * east
        + c_west * west
        + c_up * upward
        + c_down * downward
    )


def split3(x):
    high = x.astype(jnp.bfloat16)
    rest = x - high.astype(jnp.float32)
    middle = rest.astype(jnp.bfloat16)
    low = (rest - middle.astype(jnp.float32)).astype(jnp.bfloat16)
    return high, middle, low


def offer_copies(here, basis_hbm, refs, sems):
    cols = basis_hbm.shape[1] // 4
    copies = []
    for i, (ref, skip) in enumerate(zip(refs, (3, 1, 0))):
        at = pl.multiple_of(lax.rem(here + skip, 4) * cols, LANES)
        source = basis_hbm.at[:, pl.ds(at, SHARED)]
        copies.append(pltpu.make_async_copy(source, ref.at[:, 0:SHARED], sems.at[i]))
    return copies


def stencil_kernel(
    levels_ref,
    index_ref,
    advect_ref,
    sum_ref,
    zlo_ref,
    zhi_ref,
    face_lo_ref,
    face_hi_ref,
    here_ref,
    core_ref,
    basis_hbm,
    vel_hbm,
    outer_ref,
    inner_ref,
    out_ref,
    plus_ref,
    minus_ref,
    over_ref,
    field,
    first,
    boxed,
    sems,
    offer_sems,
):
    comp = pl.program_id(0)
    offer_refs = (plus_ref, minus_ref, over_ref)
    offers = offer_copies(here_ref[0], basis_hbm, offer_refs, offer_sems)
    cx, cz, ny = vel_hbm.shape[1:]
    inner = pl.ds(PAD, cz)

    def copies(c):
        return (
            pltpu.make_async_copy(
                vel_hbm.at[c], field.at[c, pl.ds(2, cx), inner, :], sems.at[c, 0, 0]
            ),
            *[
                pltpu.make_async_copy(
                    ref.at[pl.ds((2 * c + k) * cz, cz)],
                    field.at[c, face_plane(core_ref, side, 0, cx + 2) + k, inner, :],
                    sems.at[c, 1 + side, k],
                )
                for side, ref in enumerate((outer_ref, inner_ref))
                for k in range(2)
            ],
        )

    @pl.when(comp == 0)
    def _():
        for c in range(3):
            for copy in copies(c):
                copy.start()
        for copy in offers:
            copy.start()

    @pl.when(comp == pl.num_programs(0) - 1)
    def _():
        for copy in offers:
            copy.wait()

    coefs = coefficients(levels_ref, index_ref, advect_ref)

    def edge_row(ref, k):
        return ref[pl.ds(pl.multiple_of((2 * comp + k) * cx, 8), cx), :]

    zlo2, zlo1 = edge_row(zlo_ref, 0), edge_row(zlo_ref, 1)
    zhi1, zhi2 = edge_row(zhi_ref, 0), edge_row(zhi_ref, 1)
    spot = 6 * cz + 2 * comp
    first_core = core_ref[0] == 0

    def before_after(at):
        outer, other = outer_ref[pl.ds(at, 1), :], inner_ref[pl.ds(at, 1), :]
        return jnp.where(first_core, outer, other), jnp.where(first_core, other, outer)

    lo_before, lo_after = before_after(spot)
    hi_before, hi_after = before_after(spot + 1)
    plane = lax.broadcasted_iota(jnp.int32, (cx, ny), 0)

    def edge(row, before, after, north, south):
        east = jnp.where(plane == cx - 1, after, pltpu.roll(row, cx - 1, 0))
        west = jnp.where(plane == 0, before, pltpu.roll(row, 1, 0))
        return step(coefs, row, east, west, north, south)

    edge_lo = edge(zlo1, lo_before, lo_after, zlo2, edge_row(face_lo_ref, 0))
    edge_hi = edge(zhi1, hi_before, hi_after, edge_row(face_hi_ref, 1), zhi2)
    for i in range(cx):
        field[comp, 2 + i, PAD - 1 : PAD, :] = zlo1[i : i + 1]
        field[comp, 2 + i, PAD + cz : PAD + cz + 1, :] = zhi1[i : i + 1]
        first[1 + i, PAD - 1 : PAD, :] = edge_lo[i : i + 1]
        first[1 + i, PAD + cz : PAD + cz + 1, :] = edge_hi[i : i + 1]
    field[comp, 1, PAD - 1 : PAD, :] = lo_before
    field[comp, 1, PAD + cz : PAD + cz + 1, :] = hi_before
    field[comp, cx + 2, PAD - 1 : PAD, :] = lo_after
    field[comp, cx + 2, PAD + cz : PAD + cz + 1, :] = hi_after

    for copy in copies(comp):
        copy.wait()

    chunk = 16

    def first_plane(p, carry):
        for k in range(cz // chunk):
            at = PAD + k * chunk
            rows = pl.ds(at, chunk)
            first[p, rows, :] = step(
                coefs,
                field[comp, p + 1, rows, :],
                field[comp, p + 2, rows, :],
                field[comp, p, rows, :],
                field[comp, p + 1, pl.ds(at - 1, chunk), :],
                field[comp, p + 1, pl.ds(at + 1, chunk), :],
            )
        return carry

    lax.fori_loop(0, cx + 2, first_plane, 0)

    sums = sum_ref[...]
    lane = lax.broadcasted_iota(jnp.int32, (cz, LANES), 1)
    row = lax.broadcasted_iota(jnp.int32, (cz, LANES), 0)
    wanted = (lane // (LANES // 2)) == ((row // STRIDE) % 2)
    part = out_ref.shape[1] // vel_hbm.shape[0]
    offset = pl.multiple_of(comp * part, LANES)
    out_ref[:, pl.ds(offset, part)] = jnp.zeros((PAD, part), jnp.float32)

    def coarse(which, box):
        total = sum(
            jnp.dot(part, sums, preferred_element_type=jnp.float32)
            for part in split3(boxed[...])
        )
        total = jnp.where(wanted, total, 0.0)
        base = offset + box * (cz // 8 * LANES)
        for r in range(cz // 8):
            line = jnp.sum(total[8 * r : 8 * r + 8], axis=0, keepdims=True) * 0.125
            at = pl.multiple_of(base + r * LANES, LANES)
            out_ref[which : which + 1, pl.ds(at, LANES)] = line

    def box_step(box, carry):
        start = 1 + STRIDE * box
        for k in range(cz // chunk):
            rows = pl.ds(PAD + k * chunk, chunk)
            boxed[pl.ds(k * chunk, chunk), :] = (
                first[start, rows, :] + first[start + 1, rows, :]
            ) + (first[start + 2, rows, :] + first[start + 3, rows, :])
        coarse(0, box)
        for k in range(cz // chunk):
            at = PAD + k * chunk
            rows = pl.ds(at, chunk)
            total = None
            for i in range(STRIDE):
                p = start + i
                value = step(
                    coefs,
                    first[p, rows, :],
                    first[p + 1, rows, :],
                    first[p - 1, rows, :],
                    first[p, pl.ds(at - 1, chunk), :],
                    first[p, pl.ds(at + 1, chunk), :],
                )
                total = value if total is None else total + value
            boxed[pl.ds(k * chunk, chunk), :] = total
        coarse(1, box)
        return carry

    lax.fori_loop(0, cx // STRIDE, box_step, 0)

    @pl.when(comp == pl.num_programs(0) - 1)
    def _():
        tiles = SHARED // LANES
        for k in range(2 * tiles):
            which, tile = divmod(k, tiles)
            line = out_ref[which : which + 1, tile * LANES : (tile + 1) * LANES]
            at = SHARED + k // 8 * LANES
            over_ref[k % 8 : k % 8 + 1, at : at + LANES] = line


def snapshots(velocity, levels, profile_index, advect, here, core, basis, halos):
    comps, cx, cz, ny = velocity.shape
    cols = (cx // STRIDE) * (cz // STRIDE) * (ny // STRIDE)
    half = LANES // 2
    sums = np.zeros((ny, LANES), np.float32)
    for y in range(ny):
        sums[y, y // STRIDE] = 1.0
        sums[y, half + y // STRIDE] = 1.0
    return pl.pallas_call(
        stencil_kernel,
        grid=(comps,),
        in_specs=[
            SMEM_SPEC,
            pl.BlockSpec((1, ny), lambda c: (0, 0)),
            pl.BlockSpec((1, ny), lambda c: (0, 0)),
            pl.BlockSpec((ny, LANES), lambda c: (0, 0)),
            *[VMEM_SPEC] * 4,
            SMEM_SPEC,
            SMEM_SPEC,
            HBM_SPEC,
            HBM_SPEC,
            VMEM_SPEC,
            VMEM_SPEC,
        ],
        out_specs=[VMEM_SPEC] * 4,
        out_shape=[pltpu.VMEM((PAD, comps * cols), jnp.float32)]
        + [pltpu.VMEM((PAD, SHARED), jnp.float32)] * 2
        + [pltpu.VMEM((PAD, SHARED + FOLD), jnp.float32)],
        scratch_shapes=[
            pltpu.VMEM((comps, cx + 4, cz + 2 * PAD, ny), jnp.float32),
            pltpu.VMEM((cx + 2, cz + 2 * PAD, ny), jnp.float32),
            pltpu.VMEM((cz, ny), jnp.float32),
            pltpu.SemaphoreType.DMA((comps, 3, 2)),
            pltpu.SemaphoreType.DMA((3,)),
        ],
        compiler_params=pltpu.CompilerParams(vmem_limit_bytes=20 << 20),
        name="stencil",
    )(
        levels,
        profile_index.reshape(1, ny),
        advect.reshape(1, ny),
        jnp.asarray(sums, jnp.bfloat16),
        *[near(x) for x in halos[:4]],
        here,
        core,
        far(basis),
        far(halos[4]),
        *[near(x) for x in halos[5:]],
    )


def stacked(refs, start, size):
    return jnp.concatenate([ref[:, start : start + size] for ref in refs], axis=0)


def gram_kernel(here_ref, *refs, chunk):
    pieces, out_ref = refs[:-1], refs[-1]
    here = here_ref[0]
    n, acc = ROWS, None
    for start in range(0, pieces[0].shape[1], chunk):
        stack = stacked(pieces, start, chunk)
        high = stack.astype(jnp.bfloat16).astype(jnp.float32)
        joined = jnp.concatenate([high, stack - high], axis=0).astype(jnp.bfloat16)
        part = lax.dot_general(
            joined, joined, (((1,), (1,)), ((), ())), preferred_element_type=jnp.float32
        )
        acc = part if acc is None else acc + part
    cross = acc[0:n, n : 2 * n] + acc[n : 2 * n, 0:n]
    total = acc[0:n, 0:n] + (cross + acc[n : 2 * n, n : 2 * n])
    total = jnp.concatenate([total, jnp.zeros((n, LANES - n), jnp.float32)], axis=1)
    lane = lax.broadcasted_iota(jnp.int32, (n, LANES), 1)
    turned = PAD + lax.rem(lane - PAD + MODES - PAD * here + MODES, MODES)
    inside = (lane >= PAD) & (lane < n)
    total = jnp.take_along_axis(total, jnp.where(inside, turned, lane), axis=1)
    out_ref[0:PAD, :] = total[0:PAD]
    for g in range(4):
        at = pl.multiple_of(PAD + PAD * lax.rem(here + g, 4), PAD)
        out_ref[pl.ds(at, PAD), :] = total[PAD + PAD * g : 2 * PAD + PAD * g]


def gram(here, stack, chunk=2048):
    return pl.pallas_call(
        functools.partial(gram_kernel, chunk=chunk),
        in_specs=[SMEM_SPEC] + [VMEM_SPEC] * 5,
        out_specs=VMEM_SPEC,
        out_shape=pltpu.VMEM((ROWS, LANES), jnp.float32),
        compiler_params=pltpu.CompilerParams(vmem_limit_bytes=8 << 20),
        name="gram",
    )(here, *[near(x) for x in stack])


def ring_moves(size, stride, width):
    moves = []
    for shift in range(1, width):
        pairs = []
        for i in range(size):
            k = (i // stride) % width
            pairs.append((i, i + ((k + shift) % width - k) * stride))
        moves.append(pairs)
    return moves


def ring_parts(x, axis, size, stride, width):
    return [lax.ppermute(x, axis, pairs) for pairs in ring_moves(size, stride, width)]


def ring_sum(x, parts):
    if len(parts) == 1:
        return x + parts[0]
    one, two, three = parts
    return (x + two) + (one + three)


def lane_sum(x):
    total = x[0:8]
    for k in range(1, ROWS // 8):
        total = total + x[8 * k : 8 * k + 8]
    total = total + pltpu.roll(total, 4, 0)
    total = total + pltpu.roll(total, 2, 0)
    return total + pltpu.roll(total, 1, 0)


def spread(x):
    return jnp.concatenate([x] * (ROWS // 8), axis=0)


def factor_kernel(
    g0_ref, g1_ref, g2_ref, g3_ref, partner_ref, orient_ref, keep_ref, mix_ref, sigma_ref
):
    a = (g0_ref[...] + g2_ref[...]) + (g1_ref[...] + g3_ref[...])
    lane = lax.broadcasted_iota(jnp.int32, (ROWS, LANES), 1)
    row = lax.broadcasted_iota(jnp.int32, (ROWS, LANES), 0)
    upper = jnp.zeros((ROWS, LANES), jnp.float32)
    places = [int(k) for k in PLACE]
    while places:
        block, places = places[:FACTOR_BLOCK], places[FACTOR_BLOCK:]
        lines = [jnp.broadcast_to(a[j : j + 1, :], (8, LANES)) for j in block]
        columns = [jnp.broadcast_to(a[:, j : j + 1], (ROWS, LANES)) for j in block]

        def entry(column, j):
            return jnp.broadcast_to(column[j : j + 1, :], (8, LANES))

        for i, j in enumerate(block):
            scale = lax.rsqrt(entry(columns[i], j))
            lines[i] = lines[i] * scale
            columns[i] = columns[i] * spread(scale)
            for k in range(i + 1, len(block)):
                cross = entry(columns[i], block[k])
                lines[k] = lines[k] - cross * lines[i]
                columns[k] = columns[k] - spread(cross) * columns[i]
        for i, j in enumerate(block):
            line = spread(lines[i])
            a = a - columns[i] * line
            upper = jnp.where((row == j) & (lane >= j), line, upper)

    def angle(x, y, sign):
        contrast = lane_sum(y * y) - lane_sum(x * x)
        inner = lane_sum(x * y)
        toward = jnp.where(contrast > 0.0, -1.0, jnp.where(contrast < 0.0, 1.0, sign))
        d = jnp.abs(contrast) + jnp.sqrt(contrast * contrast + 4.0 * inner * inner)
        positive = d > 0.0
        tangent = jnp.where(
            positive, 2.0 * inner * toward / jnp.where(positive, d, 1.0), 0.0
        )
        cosine = lax.rsqrt(1.0 + tangent * tangent)
        return spread(cosine), spread(cosine * tangent)

    def two_rounds(k, state):
        x, v = state
        moves = [
            jnp.broadcast_to(partner_ref[m, pl.ds(k, 1), :], (ROWS, LANES)) for m in range(3)
        ]
        signs = [
            jnp.broadcast_to(orient_ref[m, pl.ds(k, 1), :], (8, LANES)) for m in range(3)
        ]
        pair, after, cross = (jnp.take_along_axis(x, move, axis=1) for move in moves)
        c_self, s_self = angle(x, pair, signs[0])
        c_next, s_next = angle(after, cross, signs[1])
        x = c_self * x + s_self * pair
        after = c_next * after + s_next * cross
        c_last, s_last = angle(x, after, signs[2])
        x = c_last * x + s_last * after
        pair, after, cross = (jnp.take_along_axis(v, move, axis=1) for move in moves)
        v = c_self * v + s_self * pair
        after = c_next * after + s_next * cross
        return x, c_last * v + s_last * after

    eye = jnp.where(row == lane, 1.0, 0.0)
    x, v = lax.fori_loop(0, SWEEPS * (COUNT - 1) // 2, two_rounds, (upper, eye))
    keep = jnp.broadcast_to(keep_ref[...], (ROWS, LANES))
    sigma_ref[...] = jnp.take_along_axis(jnp.sqrt(lane_sum(x * x)), keep[0:8], axis=1)
    v = jnp.take_along_axis(v, keep, axis=1)
    high = v.astype(jnp.bfloat16).astype(jnp.float32)
    low = v - high
    mix = jnp.concatenate([high, high, low, jnp.zeros((8, LANES), jnp.float32)], axis=0)
    mix_ref[...] = jnp.transpose(mix)[0:MODES]


def factor(parts):
    tables = [near(jnp.asarray(table)) for table in pair_tables()]
    return pl.pallas_call(
        factor_kernel,
        in_specs=[VMEM_SPEC] * 7,
        out_specs=(VMEM_SPEC, VMEM_SPEC),
        out_shape=(
            pltpu.VMEM((MODES, LANES), jnp.float32),
            pltpu.VMEM((8, LANES), jnp.float32),
        ),
        compiler_params=pltpu.CompilerParams(vmem_limit_bytes=4 << 20),
        name="factor",
    )(*[near(x) for x in parts], *tables)


def turned_mix(mix, here):
    lane = lax.broadcasted_iota(jnp.int32, mix.shape, 1)
    inside = lax.rem(lane, ROWS)
    turned = lane - inside + PAD + lax.rem(inside + (MODES - PAD) + PAD * here, MODES)
    source = jnp.where((inside < PAD) | (lane >= 3 * ROWS), lane, turned)
    return jnp.take_along_axis(mix, source, axis=1).astype(jnp.bfloat16)


def mix_rows(mix_ref, here, g):
    at = pl.multiple_of(PAD * lax.rem(here + g, 4), PAD)
    return mix_ref[pl.ds(at, PAD), :]


def mixed(mix, stack):
    high = stack.astype(jnp.bfloat16).astype(jnp.float32)
    zero = jnp.zeros((8, stack.shape[1]), jnp.float32)
    joined = jnp.concatenate([high, stack - high, high, zero], axis=0)
    return jnp.dot(mix, joined.astype(jnp.bfloat16), preferred_element_type=jnp.float32)


def update_kernel(here_ref, mix_ref, *refs, chunk):
    pieces, out_refs = refs[:5], refs[5:]
    here = here_ref[0]
    mix = jnp.concatenate([mix_rows(mix_ref, here, g) for g in range(4)], axis=0)
    mix = turned_mix(mix, here)
    for start in range(0, out_refs[0].shape[1], chunk):
        out = mixed(mix, stacked(pieces, start, chunk))
        for g, ref in enumerate(out_refs):
            at = start - (pieces[0].shape[1] - ref.shape[1])
            if at >= 0:
                ref[:, at : at + chunk] = out[PAD * g : PAD * g + PAD]


def update(here, mix, stack, chunk=1024):
    cols = stack[0].shape[1]
    sizes = (cols, cols, cols - SHARED, cols)
    return pl.pallas_call(
        functools.partial(update_kernel, chunk=chunk),
        in_specs=[SMEM_SPEC] + [VMEM_SPEC] * 6,
        out_specs=[VMEM_SPEC] * 4,
        out_shape=[pltpu.VMEM((PAD, size), jnp.float32) for size in sizes],
        compiler_params=pltpu.CompilerParams(vmem_limit_bytes=8 << 20),
        name="update",
    )(here, near(mix), *[near(x) for x in stack])


def own_kernel(here_ref, mix_ref, *refs, cols, chunk):
    hi_ref, over_ref, lo_ref = refs[:3]
    basis_hbm, out_hbm, mine, snap, buf, in_sem, out_sem = refs[3:]
    here = here_ref[0]
    tiles = SHARED // LANES
    spot = pl.ds(pl.multiple_of(lax.rem(here + 2, 4) * cols, LANES), SHARED)
    read = pltpu.make_async_copy(basis_hbm.at[:, spot], mine, in_sem)
    read.start()
    mix = turned_mix(mix_rows(mix_ref, here, 0), here)
    snap[...] = jnp.zeros((PAD, SHARED), jnp.float32)
    for k in range(2 * tiles):
        which, tile = divmod(k, tiles)
        at = SHARED + k // 8 * LANES
        line = over_ref[k % 8 : k % 8 + 1, at : at + LANES]
        snap[which : which + 1, tile * LANES : (tile + 1) * LANES] = line
    read.wait()
    for start in range(0, SHARED, chunk):
        at = slice(start, start + chunk)
        rows = [snap, mine, hi_ref, over_ref, lo_ref]
        stack = jnp.concatenate([ref[:, at] for ref in rows], axis=0)
        buf[:, at] = mixed(mix, stack)
    write = pltpu.make_async_copy(buf, out_hbm.at[:, spot], out_sem)
    write.start()
    write.wait()


def own(here, mix, received, basis, chunk=1024):
    cols = basis.shape[1] // 4
    return pl.pallas_call(
        functools.partial(own_kernel, cols=cols, chunk=chunk),
        in_specs=[SMEM_SPEC] + [VMEM_SPEC] * 4 + [HBM_SPEC],
        out_specs=HBM_SPEC,
        out_shape=pltpu.HBM(basis.shape, jnp.float32),
        scratch_shapes=[pltpu.VMEM((PAD, SHARED), jnp.float32)] * 3
        + [pltpu.SemaphoreType.DMA(())] * 2,
        compiler_params=pltpu.CompilerParams(vmem_limit_bytes=10 << 20),
        name="own",
    )(here, *[near(x) for x in (mix, *received)], far(basis))


def join_kernel(here_ref, *refs, sources):
    parts, (_, out_hbm, sems) = refs[: len(sources)], refs[len(sources) :]
    cols = out_hbm.shape[1] // 4
    copies = []
    for g, part in zip(sources, parts):
        size = part.shape[1]
        at = pl.multiple_of(lax.rem(here_ref[0] + g, 4) * cols + cols - size, LANES)
        target = out_hbm.at[:, pl.ds(at, size)]
        copies.append(pltpu.make_async_copy(part, target, sems.at[g]))
        copies[-1].start()
    for copy in copies:
        copy.wait()


def join(here, parts, whole):
    count = len(parts)
    return pl.pallas_call(
        functools.partial(join_kernel, sources=tuple(parts)),
        in_specs=[SMEM_SPEC] + [VMEM_SPEC] * count + [HBM_SPEC],
        out_specs=HBM_SPEC,
        out_shape=pltpu.HBM(whole.shape, jnp.float32),
        scratch_shapes=[pltpu.SemaphoreType.DMA((4,))],
        input_output_aliases={1 + count: 0},
        compiler_params=pltpu.CompilerParams(vmem_limit_bytes=2 << 20),
        name="join",
    )(here, *[near(x) for x in parts.values()], far(whole))


def program(velocity, basis, levels, profile_index, advect):
    n_space, n_mode = lax.axis_size("space"), lax.axis_size("mode")
    comps, cx, _, _ = velocity.shape
    here = lax.axis_index("mode").astype(jnp.int32).reshape(1)
    core = lax.rem(lax.axis_index("space").astype(jnp.int32), 2).reshape(1)

    def shifted(x, axis, by):
        size = lax.axis_size(axis)
        return lax.ppermute(x, axis, [(i, (i + by) % size) for i in range(size)])

    face_lo, face_hi, outer, inner, *blocks = pack(here, core, velocity, basis)
    block_own, block_next, block_far, block_prev = blocks
    zlo = shifted(face_hi, "mode", 1)
    zhi = shifted(face_lo, "mode", -1)
    lo = shifted(block_next, "mode", 1)
    hi = shifted(block_prev, "mode", -1)
    over = shifted(block_far, "mode", 2)
    outer, inner = add_corners(core, zlo, zhi, outer, inner, cx, comps)
    pairs = [(i, (i + (1 if i % 2 else -1)) % n_space) for i in range(n_space)]
    outer = lax.ppermute(outer, "space", pairs)
    inner = lax.ppermute(inner, "space", [(i, i ^ 1) for i in range(n_space)])
    snap, plus, minus, across = snapshots(
        velocity,
        levels,
        profile_index,
        advect,
        here,
        core,
        basis,
        (zlo, zhi, face_lo, face_hi, velocity, outer, inner),
    )
    lo_early = shifted(plus, "mode", 1)
    hi_early = shifted(minus, "mode", -1)
    stack = (snap, block_own, hi, over, lo)
    total = gram(here, stack)
    total = ring_sum(total, ring_parts(total, "space", n_space, 1, 2))
    total = ring_sum(total, ring_parts(total, "space", n_space, 2, 4))
    total = ring_sum(total, ring_parts(total, "mode", n_mode, 1, n_mode))
    parts = [total] + ring_parts(total, "space", n_space, 8, 4)
    over_early = shifted(across, "mode", 2)
    mix, sigma = factor(parts)
    out_own, out_next, out_over, out_prev = update(here, mix, stack)
    back_lo = shifted(out_next, "mode", 1)
    back_hi = shifted(out_prev, "mode", -1)
    back_over = shifted(out_over, "mode", 2)
    mine = own(here, mix, (hi_early, over_early, lo_early), basis)
    modes = join(here, {0: out_own, 1: back_hi, 3: back_lo}, mine)
    modes = join(here, {2: back_over}, modes)
    return (modes, sigma[0, :MODES])


def solution(mesh):
    return jax.shard_map(
        program,
        mesh=mesh,
        in_specs=(P(None, "space", "mode", None), P("mode", "space"), P(), P(), P()),
        out_specs=(P("mode", "space"), P()),
        check_vma=False,
    )
```

```python
import functools

import jax
import jax.numpy as jnp
import numpy as np
from jax import lax
from jax.experimental import pallas as pl
from jax.experimental.pallas import tpu as pltpu
from jax.sharding import PartitionSpec as P

STRIDE = 4
MODES = 32
SWEEPS = 2
FACTOR_BLOCK = 8
COUNT = 34
ROWS = 40
LANES = 128
PAD = 8
VMEM_SPEC = pl.BlockSpec(memory_space=pltpu.VMEM)
HBM_SPEC = pl.BlockSpec(memory_space=pltpu.HBM)
SMEM_SPEC = pl.BlockSpec(memory_space=pltpu.SMEM)


SHARED = 14336
FOLD = SHARED // 4

PLACE = np.array([0, 1] + list(range(PAD, PAD + MODES)))


def near(x):
    return pltpu.with_memory_space_constraint(x, pltpu.VMEM)


def far(x):
    return pltpu.with_memory_space_constraint(x, pltpu.HBM)


def pair_tables():
    rounds = COUNT - 1
    partner = np.tile(np.arange(LANES), (rounds, 1))
    orient = np.ones((rounds, LANES), np.float32)
    for turn in range(rounds):
        players = [0] + [1 + (i - 1 + turn) % rounds for i in range(1, COUNT)]
        for k in range(COUNT // 2):
            lead, trail = PLACE[players[k]], PLACE[players[COUNT - 1 - k]]
            partner[turn, lead] = trail
            partner[turn, trail] = lead
            orient[turn, lead] = -1.0
    moves = np.zeros((3, ROWS, LANES), np.int32)
    signs = np.zeros((3, ROWS, LANES), np.float32)
    for k in range(rounds):
        one, two = 2 * k % rounds, (2 * k + 1) % rounds
        after = partner[two]
        moves[0, k], moves[1, k], moves[2, k] = partner[one], after, partner[one][after]
        signs[0, k], signs[1, k], signs[2, k] = orient[one], orient[one][after], orient[two]
    keep = np.zeros((1, LANES), np.int32)
    keep[0, :MODES] = PLACE[:MODES]
    return moves, signs, keep


def face_plane(core_ref, side, first, last):
    return jnp.where(core_ref[0] == side, first, last)


def pack_kernel(
    here_ref,
    core_ref,
    vel_hbm,
    basis_hbm,
    zfirst_ref,
    zlast_ref,
    outer_ref,
    inner_ref,
    mine_ref,
    next_ref,
    far_ref,
    prev_ref,
    buf,
    edge_sems,
    face_sems,
    block_sems,
):
    comps, cx, cz, _ = vel_hbm.shape
    cols = mine_ref.shape[1]
    edges, rest = [], []
    for c in range(comps):
        for side, at in enumerate((0, cz - PAD)):
            source = vel_hbm.at[c, :, pl.ds(at, PAD), :]
            edges.append(pltpu.make_async_copy(source, buf.at[c, side], edge_sems.at[c, side]))
        for side, ref in enumerate((outer_ref, inner_ref)):
            at = face_plane(core_ref, side, 0, cx - 2)
            for k in range(2):
                source = vel_hbm.at[c, at + k]
                target = ref.at[pl.ds((2 * c + k) * cz, cz)]
                rest.append(pltpu.make_async_copy(source, target, face_sems.at[c, side, k]))
    for k, ref in enumerate((mine_ref, next_ref, far_ref, prev_ref)):
        at = pl.multiple_of(lax.rem(here_ref[0] + k, 4) * cols, LANES)
        source = basis_hbm.at[:, pl.ds(at, cols)]
        rest.append(pltpu.make_async_copy(source, ref, block_sems.at[k]))
    for copy in edges + rest:
        copy.start()
    for copy in edges:
        copy.wait()
    for c in range(comps):
        for i in range(cx):
            for k in range(2):
                row, last = (2 * c + k) * cx + i, PAD - 2 + k
                zfirst_ref[row : row + 1, :] = buf[c, 0, i, k : k + 1, :]
                zlast_ref[row : row + 1, :] = buf[c, 1, i, last : last + 1, :]
    for copy in rest:
        copy.wait()


def pack(here, core, velocity, basis):
    comps, cx, cz, ny = velocity.shape
    edge = pltpu.VMEM((comps * 2 * cx, ny), jnp.float32)
    face = pltpu.VMEM((comps * 2 * cz + PAD, ny), jnp.float32)
    block = pltpu.VMEM((PAD, basis.shape[1] // 4), jnp.float32)
    return pl.pallas_call(
        pack_kernel,
        in_specs=[SMEM_SPEC, SMEM_SPEC, HBM_SPEC, HBM_SPEC],
        out_specs=[VMEM_SPEC] * 8,
        out_shape=[edge, edge, face, face] + [block] * 4,
        scratch_shapes=[
            pltpu.VMEM((comps, 2, cx, PAD, ny), jnp.float32),
            pltpu.SemaphoreType.DMA((comps, 2)),
            pltpu.SemaphoreType.DMA((comps, 2, 2)),
            pltpu.SemaphoreType.DMA((4,)),
        ],
        compiler_params=pltpu.CompilerParams(vmem_limit_bytes=4 << 20),
        name="pack",
    )(here, core, far(velocity), far(basis))


def corner_kernel(core_ref, zlo_ref, zhi_ref, _, __, outer_ref, inner_ref, *, cx, comps):
    base = outer_ref.shape[0] - PAD
    zero = jnp.zeros((PAD, outer_ref.shape[1]), jnp.float32)
    for side, ref in enumerate((outer_ref, inner_ref)):
        plane = face_plane(core_ref, side, 0, cx - 1)
        ref[base:, :] = zero
        for c in range(comps):
            at = base + 2 * c
            ref[at : at + 1, :] = zlo_ref[pl.ds((2 * c + 1) * cx + plane, 1), :]
            ref[at + 1 : at + 2, :] = zhi_ref[pl.ds(2 * c * cx + plane, 1), :]


def add_corners(core, zlo, zhi, outer, inner, cx, comps):
    face = pltpu.VMEM(outer.shape, jnp.float32)
    return pl.pallas_call(
        functools.partial(corner_kernel, cx=cx, comps=comps),
        in_specs=[SMEM_SPEC] + [VMEM_SPEC] * 4,
        out_specs=[VMEM_SPEC] * 2,
        out_shape=[face, face],
        input_output_aliases={3: 0, 4: 1},
        compiler_params=pltpu.CompilerParams(vmem_limit_bytes=1 << 20),
        name="corners",
    )(core, *[near(x) for x in (zlo, zhi, outer, inner)])


def coefficients(levels_ref, index_ref, advect_ref):
    index = index_ref[...]
    visc = jnp.zeros(index.shape, jnp.float32)
    for level in range(levels_ref.shape[0]):
        visc = jnp.where(index == level, levels_ref[level], visc)
    cells = index.shape[1]
    lane = lax.broadcasted_iota(jnp.int32, index.shape, 1)
    first, last = lane == 0, lane == cells - 1
    up = jnp.where(last, visc, 0.5 * (visc + pltpu.roll(visc, cells - 1, 1)))
    down = jnp.where(first, visc, 0.5 * (visc + pltpu.roll(visc, 1, 1)))
    half = 0.5 * advect_ref[...]
    return (
        1.0 - 4.0 * visc - up - down,
        visc,
        visc - half,
        visc + half,
        jnp.where(last, 0.0, up),
        jnp.where(first, 0.0, down),
    )


def step(coefs, center, east, west, north, south):
    mid, visc, c_east, c_west, c_up, c_down = coefs
    cells = center.shape[-1]
    upward = pltpu.roll(center, cells - 1, 1)
    downward = pltpu.roll(center, 1, 1)
    return (
        mid * center
        + visc * (north + south)
        + c_east * east
        + c_west * west
        + c_up * upward
        + c_down * downward
    )


def split2(x):
    high = x.astype(jnp.bfloat16)
    return high, (x - high.astype(jnp.float32)).astype(jnp.bfloat16)


def first_chunk(coefs, field, first, comp, p, at, size):
    rows = pl.ds(at, size)
    first[comp, p, rows, :] = step(
        coefs,
        field[comp, p + 1, rows, :],
        field[comp, p + 2, rows, :],
        field[comp, p, rows, :],
        field[comp, p + 1, pl.ds(at - 1, size), :],
        field[comp, p + 1, pl.ds(at + 1, size), :],
    )


CHUNK = 16


def inner_kernel(levels_ref, index_ref, advect_ref, zlo_ref, zhi_ref, vel_hbm, field, first, sems):
    comp = pl.program_id(0)
    comps, cx, cz, _ = vel_hbm.shape

    def copy(c):
        target = field.at[c, pl.ds(2, cx), pl.ds(PAD, cz), :]
        return pltpu.make_async_copy(vel_hbm.at[c], target, sems.at[c])

    @pl.when(comp == 0)
    def _():
        for c in range(comps):
            copy(c).start()

    coefs = coefficients(levels_ref, index_ref, advect_ref)
    low = zlo_ref[pl.ds(pl.multiple_of((2 * comp + 1) * cx, 8), cx), :]
    high = zhi_ref[pl.ds(pl.multiple_of(2 * comp * cx, 8), cx), :]
    for i in range(cx):
        field[comp, 2 + i, PAD - 1 : PAD, :] = low[i : i + 1]
        field[comp, 2 + i, PAD + cz : PAD + cz + 1, :] = high[i : i + 1]
    copy(comp).wait()

    def plane(p, carry):
        for k in range(cz // CHUNK):
            first_chunk(coefs, field, first, comp, p, PAD + k * CHUNK, CHUNK)
        return carry

    lax.fori_loop(2, cx, plane, 0)


def inner_planes(velocity, levels, profile_index, advect, zlo, zhi):
    comps, cx, cz, ny = velocity.shape
    return pl.pallas_call(
        inner_kernel,
        grid=(comps,),
        in_specs=[
            SMEM_SPEC,
            pl.BlockSpec((1, ny), lambda c: (0, 0)),
            pl.BlockSpec((1, ny), lambda c: (0, 0)),
            VMEM_SPEC,
            VMEM_SPEC,
            HBM_SPEC,
        ],
        out_specs=[VMEM_SPEC] * 2,
        out_shape=[
            pltpu.VMEM((comps, cx + 4, cz + 2 * PAD, ny), jnp.float32),
            pltpu.VMEM((comps, cx + 2, cz + 2 * PAD, ny), jnp.float32),
        ],
        scratch_shapes=[pltpu.SemaphoreType.DMA((comps,))],
        compiler_params=pltpu.CompilerParams(vmem_limit_bytes=3 << 20),
        name="inner",
    )(
        levels,
        profile_index.reshape(1, ny),
        advect.reshape(1, ny),
        near(zlo),
        near(zhi),
        far(velocity),
    )


def offer_copies(here, basis_hbm, refs, sems):
    cols = basis_hbm.shape[1] // 4
    copies = []
    for i, (ref, skip) in enumerate(zip(refs, (3, 1, 0))):
        at = pl.multiple_of(lax.rem(here + skip, 4) * cols, LANES)
        source = basis_hbm.at[:, pl.ds(at, SHARED)]
        copies.append(pltpu.make_async_copy(source, ref.at[:, 0:SHARED], sems.at[i]))
    return copies


def stencil_kernel(
    levels_ref,
    index_ref,
    advect_ref,
    sum_ref,
    zlo_ref,
    zhi_ref,
    face_lo_ref,
    face_hi_ref,
    here_ref,
    core_ref,
    basis_hbm,
    outer_ref,
    inner_ref,
    _,
    __,
    out_ref,
    plus_ref,
    minus_ref,
    over_ref,
    field,
    first,
    boxed,
    sems,
    offer_sems,
):
    comp = pl.program_id(0)
    offer_refs = (plus_ref, minus_ref, over_ref)
    offers = offer_copies(here_ref[0], basis_hbm, offer_refs, offer_sems)
    cx, cz, ny = field.shape[1] - 4, field.shape[2] - 2 * PAD, field.shape[3]
    inner = pl.ds(PAD, cz)

    def copies(c):
        return (
            *[
                pltpu.make_async_copy(
                    ref.at[pl.ds((2 * c + k) * cz, cz)],
                    field.at[c, face_plane(core_ref, side, 0, cx + 2) + k, inner, :],
                    sems.at[c, side, k],
                )
                for side, ref in enumerate((outer_ref, inner_ref))
                for k in range(2)
            ],
        )

    @pl.when(comp == 0)
    def _():
        for c in range(3):
            for copy in copies(c):
                copy.start()
        for copy in offers:
            copy.start()

    @pl.when(comp == pl.num_programs(0) - 1)
    def _():
        for copy in offers:
            copy.wait()

    coefs = coefficients(levels_ref, index_ref, advect_ref)

    def edge_row(ref, k):
        return ref[pl.ds(pl.multiple_of((2 * comp + k) * cx, 8), cx), :]

    zlo2, zlo1 = edge_row(zlo_ref, 0), edge_row(zlo_ref, 1)
    zhi1, zhi2 = edge_row(zhi_ref, 0), edge_row(zhi_ref, 1)
    spot = 6 * cz + 2 * comp
    first_core = core_ref[0] == 0

    def before_after(at):
        outer, other = outer_ref[pl.ds(at, 1), :], inner_ref[pl.ds(at, 1), :]
        return jnp.where(first_core, outer, other), jnp.where(first_core, other, outer)

    lo_before, lo_after = before_after(spot)
    hi_before, hi_after = before_after(spot + 1)
    plane = lax.broadcasted_iota(jnp.int32, (cx, ny), 0)

    def edge(row, before, after, north, south):
        east = jnp.where(plane == cx - 1, after, pltpu.roll(row, cx - 1, 0))
        west = jnp.where(plane == 0, before, pltpu.roll(row, 1, 0))
        return step(coefs, row, east, west, north, south)

    edge_lo = edge(zlo1, lo_before, lo_after, zlo2, edge_row(face_lo_ref, 0))
    edge_hi = edge(zhi1, hi_before, hi_after, edge_row(face_hi_ref, 1), zhi2)
    for i in range(cx):
        first[comp, 1 + i, PAD - 1 : PAD, :] = edge_lo[i : i + 1]
        first[comp, 1 + i, PAD + cz : PAD + cz + 1, :] = edge_hi[i : i + 1]
    field[comp, 1, PAD - 1 : PAD, :] = lo_before
    field[comp, 1, PAD + cz : PAD + cz + 1, :] = hi_before
    field[comp, cx + 2, PAD - 1 : PAD, :] = lo_after
    field[comp, cx + 2, PAD + cz : PAD + cz + 1, :] = hi_after

    for copy in copies(comp):
        copy.wait()

    chunk = CHUNK

    def outer_plane(k, carry):
        p = jnp.where(k < 2, k, cx - 2 + k)
        for i in range(cz // chunk):
            first_chunk(coefs, field, first, comp, p, PAD + i * chunk, chunk)
        return carry

    lax.fori_loop(0, 4, outer_plane, 0)

    sums = sum_ref[...]
    lane = lax.broadcasted_iota(jnp.int32, (cz, LANES), 1)
    row = lax.broadcasted_iota(jnp.int32, (cz, LANES), 0)
    wanted = (lane // (LANES // 2)) == ((row // STRIDE) % 2)
    part = out_ref.shape[1] // field.shape[0]
    offset = pl.multiple_of(comp * part, LANES)
    out_ref[:, pl.ds(offset, part)] = jnp.zeros((PAD, part), jnp.float32)

    def coarse(which, box):
        total = sum(
            jnp.dot(part, sums, preferred_element_type=jnp.float32)
            for part in split2(boxed[...])
        )
        total = jnp.where(wanted, total, 0.0)
        base = offset + box * (cz // 8 * LANES)
        for r in range(cz // 8):
            line = jnp.sum(total[8 * r : 8 * r + 8], axis=0, keepdims=True) * 0.125
            at = pl.multiple_of(base + r * LANES, LANES)
            out_ref[which : which + 1, pl.ds(at, LANES)] = line

    def box_step(box, carry):
        start = 1 + STRIDE * box
        for k in range(cz // chunk):
            rows = pl.ds(PAD + k * chunk, chunk)
            boxed[pl.ds(k * chunk, chunk), :] = (
                first[comp, start, rows, :] + first[comp, start + 1, rows, :]
            ) + (first[comp, start + 2, rows, :] + first[comp, start + 3, rows, :])
        coarse(0, box)
        for k in range(cz // chunk):
            at = PAD + k * chunk
            rows = pl.ds(at, chunk)
            total = None
            for i in range(STRIDE):
                p = start + i
                value = step(
                    coefs,
                    first[comp, p, rows, :],
                    first[comp, p + 1, rows, :],
                    first[comp, p - 1, rows, :],
                    first[comp, p, pl.ds(at - 1, chunk), :],
                    first[comp, p, pl.ds(at + 1, chunk), :],
                )
                total = value if total is None else total + value
            boxed[pl.ds(k * chunk, chunk), :] = total
        coarse(1, box)
        return carry

    lax.fori_loop(0, cx // STRIDE, box_step, 0)

    @pl.when(comp == pl.num_programs(0) - 1)
    def _():
        tiles = SHARED // LANES
        for k in range(2 * tiles):
            which, tile = divmod(k, tiles)
            line = out_ref[which : which + 1, tile * LANES : (tile + 1) * LANES]
            at = SHARED + k // 8 * LANES
            over_ref[k % 8 : k % 8 + 1, at : at + LANES] = line


def snapshots(levels, profile_index, advect, here, core, basis, halos, state):
    comps, cx, cz, ny = (size - grow for size, grow in zip(state[0].shape, (0, 4, 2 * PAD, 0)))
    cols = (cx // STRIDE) * (cz // STRIDE) * (ny // STRIDE)
    half = LANES // 2
    sums = np.zeros((ny, LANES), np.float32)
    for y in range(ny):
        sums[y, y // STRIDE] = 1.0
        sums[y, half + y // STRIDE] = 1.0
    return pl.pallas_call(
        stencil_kernel,
        grid=(comps,),
        in_specs=[
            SMEM_SPEC,
            pl.BlockSpec((1, ny), lambda c: (0, 0)),
            pl.BlockSpec((1, ny), lambda c: (0, 0)),
            pl.BlockSpec((ny, LANES), lambda c: (0, 0)),
            *[VMEM_SPEC] * 4,
            SMEM_SPEC,
            SMEM_SPEC,
            HBM_SPEC,
            *[VMEM_SPEC] * 4,
        ],
        out_specs=[VMEM_SPEC] * 6,
        input_output_aliases={13: 4, 14: 5},
        out_shape=[pltpu.VMEM((PAD, comps * cols), jnp.float32)]
        + [pltpu.VMEM((PAD, SHARED), jnp.float32)] * 2
        + [pltpu.VMEM((PAD, SHARED + FOLD), jnp.float32)]
        + [pltpu.VMEM(x.shape, jnp.float32) for x in state],
        scratch_shapes=[
            pltpu.VMEM((cz, ny), jnp.float32),
            pltpu.SemaphoreType.DMA((comps, 2, 2)),
            pltpu.SemaphoreType.DMA((3,)),
        ],
        compiler_params=pltpu.CompilerParams(vmem_limit_bytes=6 << 20),
        name="stencil",
    )(
        levels,
        profile_index.reshape(1, ny),
        advect.reshape(1, ny),
        jnp.asarray(sums, jnp.bfloat16),
        *[near(x) for x in halos[:4]],
        here,
        core,
        far(basis),
        *[near(x) for x in (*halos[4:], *state)],
    )[:4]


def stacked(refs, start, size):
    return jnp.concatenate([ref[:, start : start + size] for ref in refs], axis=0)


def gram_kernel(here_ref, *refs, chunk):
    pieces, out_ref = refs[:-1], refs[-1]
    here = here_ref[0]
    n, acc = ROWS, None
    for start in range(0, pieces[0].shape[1], chunk):
        stack = stacked(pieces, start, chunk)
        high = stack.astype(jnp.bfloat16).astype(jnp.float32)
        joined = jnp.concatenate([high, stack - high], axis=0).astype(jnp.bfloat16)
        part = lax.dot_general(
            joined, joined, (((1,), (1,)), ((), ())), preferred_element_type=jnp.float32
        )
        acc = part if acc is None else acc + part
    cross = acc[0:n, n : 2 * n] + acc[n : 2 * n, 0:n]
    total = acc[0:n, 0:n] + (cross + acc[n : 2 * n, n : 2 * n])
    total = jnp.concatenate([total, jnp.zeros((n, LANES - n), jnp.float32)], axis=1)
    lane = lax.broadcasted_iota(jnp.int32, (n, LANES), 1)
    turned = PAD + lax.rem(lane - PAD + MODES - PAD * here + MODES, MODES)
    inside = (lane >= PAD) & (lane < n)
    total = jnp.take_along_axis(total, jnp.where(inside, turned, lane), axis=1)
    out_ref[0:PAD, :] = total[0:PAD]
    for g in range(4):
        at = pl.multiple_of(PAD + PAD * lax.rem(here + g, 4), PAD)
        out_ref[pl.ds(at, PAD), :] = total[PAD + PAD * g : 2 * PAD + PAD * g]


def gram(here, stack, chunk=2048):
    return pl.pallas_call(
        functools.partial(gram_kernel, chunk=chunk),
        in_specs=[SMEM_SPEC] + [VMEM_SPEC] * 5,
        out_specs=VMEM_SPEC,
        out_shape=pltpu.VMEM((ROWS, LANES), jnp.float32),
        compiler_params=pltpu.CompilerParams(vmem_limit_bytes=8 << 20),
        name="gram",
    )(here, *[near(x) for x in stack])


def ring_moves(size, stride, width):
    moves = []
    for shift in range(1, width):
        pairs = []
        for i in range(size):
            k = (i // stride) % width
            pairs.append((i, i + ((k + shift) % width - k) * stride))
        moves.append(pairs)
    return moves


def ring_parts(x, axis, size, stride, width):
    return [lax.ppermute(x, axis, pairs) for pairs in ring_moves(size, stride, width)]


def ring_sum(x, parts):
    if len(parts) == 1:
        return x + parts[0]
    one, two, three = parts
    return (x + two) + (one + three)


def lane_sum(x):
    total = x[0:8]
    for k in range(1, ROWS // 8):
        total = total + x[8 * k : 8 * k + 8]
    total = total + pltpu.roll(total, 4, 0)
    total = total + pltpu.roll(total, 2, 0)
    return total + pltpu.roll(total, 1, 0)


def spread(x):
    return jnp.concatenate([x] * (ROWS // 8), axis=0)


def factor_kernel(
    g0_ref, g1_ref, g2_ref, g3_ref, partner_ref, orient_ref, keep_ref, mix_ref, sigma_ref
):
    a = (g0_ref[...] + g2_ref[...]) + (g1_ref[...] + g3_ref[...])
    lane = lax.broadcasted_iota(jnp.int32, (ROWS, LANES), 1)
    row = lax.broadcasted_iota(jnp.int32, (ROWS, LANES), 0)
    upper = jnp.zeros((ROWS, LANES), jnp.float32)
    places = [int(k) for k in PLACE]
    while places:
        block, places = places[:FACTOR_BLOCK], places[FACTOR_BLOCK:]
        lines = [jnp.broadcast_to(a[j : j + 1, :], (8, LANES)) for j in block]
        columns = [jnp.broadcast_to(a[:, j : j + 1], (ROWS, LANES)) for j in block]

        def entry(column, j):
            return jnp.broadcast_to(column[j : j + 1, :], (8, LANES))

        for i, j in enumerate(block):
            scale = lax.rsqrt(entry(columns[i], j))
            lines[i] = lines[i] * scale
            columns[i] = columns[i] * spread(scale)
            for k in range(i + 1, len(block)):
                cross = entry(columns[i], block[k])
                lines[k] = lines[k] - cross * lines[i]
                columns[k] = columns[k] - spread(cross) * columns[i]
        for i, j in enumerate(block):
            line = spread(lines[i])
            a = a - columns[i] * line
            upper = jnp.where((row == j) & (lane >= j), line, upper)

    def angle(x, y, sign):
        contrast = lane_sum(y * y) - lane_sum(x * x)
        inner = lane_sum(x * y)
        toward = jnp.where(contrast > 0.0, -1.0, jnp.where(contrast < 0.0, 1.0, sign))
        d = jnp.abs(contrast) + jnp.sqrt(contrast * contrast + 4.0 * inner * inner)
        positive = d > 0.0
        tangent = jnp.where(
            positive, 2.0 * inner * toward / jnp.where(positive, d, 1.0), 0.0
        )
        cosine = lax.rsqrt(1.0 + tangent * tangent)
        return spread(cosine), spread(cosine * tangent)

    def two_rounds(k, state):
        x, v = state
        moves = [
            jnp.broadcast_to(partner_ref[m, pl.ds(k, 1), :], (ROWS, LANES)) for m in range(3)
        ]
        signs = [
            jnp.broadcast_to(orient_ref[m, pl.ds(k, 1), :], (8, LANES)) for m in range(3)
        ]
        pair, after, cross = (jnp.take_along_axis(x, move, axis=1) for move in moves)
        c_self, s_self = angle(x, pair, signs[0])
        c_next, s_next = angle(after, cross, signs[1])
        x = c_self * x + s_self * pair
        after = c_next * after + s_next * cross
        c_last, s_last = angle(x, after, signs[2])
        x = c_last * x + s_last * after
        pair, after, cross = (jnp.take_along_axis(v, move, axis=1) for move in moves)
        v = c_self * v + s_self * pair
        after = c_next * after + s_next * cross
        return x, c_last * v + s_last * after

    eye = jnp.where(row == lane, 1.0, 0.0)
    x, v = lax.fori_loop(0, SWEEPS * (COUNT - 1) // 2, two_rounds, (upper, eye))
    keep = jnp.broadcast_to(keep_ref[...], (ROWS, LANES))
    sigma_ref[...] = jnp.take_along_axis(jnp.sqrt(lane_sum(x * x)), keep[0:8], axis=1)
    v = jnp.take_along_axis(v, keep, axis=1)
    high = v.astype(jnp.bfloat16).astype(jnp.float32)
    low = v - high
    mix = jnp.concatenate([high, high, low, jnp.zeros((8, LANES), jnp.float32)], axis=0)
    mix_ref[...] = jnp.transpose(mix)[0:MODES]


def factor(parts):
    tables = [near(jnp.asarray(table)) for table in pair_tables()]
    return pl.pallas_call(
        factor_kernel,
        in_specs=[VMEM_SPEC] * 7,
        out_specs=(VMEM_SPEC, VMEM_SPEC),
        out_shape=(
            pltpu.VMEM((MODES, LANES), jnp.float32),
            pltpu.VMEM((8, LANES), jnp.float32),
        ),
        compiler_params=pltpu.CompilerParams(vmem_limit_bytes=4 << 20),
        name="factor",
    )(*[near(x) for x in parts], *tables)


def turned_mix(mix, here):
    lane = lax.broadcasted_iota(jnp.int32, mix.shape, 1)
    inside = lax.rem(lane, ROWS)
    turned = lane - inside + PAD + lax.rem(inside + (MODES - PAD) + PAD * here, MODES)
    source = jnp.where((inside < PAD) | (lane >= 3 * ROWS), lane, turned)
    return jnp.take_along_axis(mix, source, axis=1).astype(jnp.bfloat16)


def mix_rows(mix_ref, here, g):
    at = pl.multiple_of(PAD * lax.rem(here + g, 4), PAD)
    return mix_ref[pl.ds(at, PAD), :]


def mixed(mix, stack):
    high = stack.astype(jnp.bfloat16).astype(jnp.float32)
    zero = jnp.zeros((8, stack.shape[1]), jnp.float32)
    joined = jnp.concatenate([high, stack - high, high, zero], axis=0)
    return jnp.dot(mix, joined.astype(jnp.bfloat16), preferred_element_type=jnp.float32)


def update_kernel(here_ref, mix_ref, *refs, chunk):
    pieces, out_refs = refs[:5], refs[5:]
    here = here_ref[0]
    mix = jnp.concatenate([mix_rows(mix_ref, here, g) for g in range(4)], axis=0)
    mix = turned_mix(mix, here)
    for start in range(0, out_refs[0].shape[1], chunk):
        out = mixed(mix, stacked(pieces, start, chunk))
        for g, ref in enumerate(out_refs):
            at = start - (pieces[0].shape[1] - ref.shape[1])
            if at >= 0:
                ref[:, at : at + chunk] = out[PAD * g : PAD * g + PAD]


def update(here, mix, stack, chunk=1024):
    cols = stack[0].shape[1]
    sizes = (cols, cols, cols - SHARED, cols)
    return pl.pallas_call(
        functools.partial(update_kernel, chunk=chunk),
        in_specs=[SMEM_SPEC] + [VMEM_SPEC] * 6,
        out_specs=[VMEM_SPEC] * 4,
        out_shape=[pltpu.VMEM((PAD, size), jnp.float32) for size in sizes],
        compiler_params=pltpu.CompilerParams(vmem_limit_bytes=8 << 20),
        name="update",
    )(here, near(mix), *[near(x) for x in stack])


def own_kernel(here_ref, mix_ref, *refs, cols, chunk):
    hi_ref, over_ref, lo_ref = refs[:3]
    basis_hbm, out_hbm, mine, snap, buf, in_sem, out_sem = refs[3:]
    here = here_ref[0]
    tiles = SHARED // LANES
    spot = pl.ds(pl.multiple_of(lax.rem(here + 2, 4) * cols, LANES), SHARED)
    read = pltpu.make_async_copy(basis_hbm.at[:, spot], mine, in_sem)
    read.start()
    mix = turned_mix(mix_rows(mix_ref, here, 0), here)
    snap[...] = jnp.zeros((PAD, SHARED), jnp.float32)
    for k in range(2 * tiles):
        which, tile = divmod(k, tiles)
        at = SHARED + k // 8 * LANES
        line = over_ref[k % 8 : k % 8 + 1, at : at + LANES]
        snap[which : which + 1, tile * LANES : (tile + 1) * LANES] = line
    read.wait()
    for start in range(0, SHARED, chunk):
        at = slice(start, start + chunk)
        rows = [snap, mine, hi_ref, over_ref, lo_ref]
        stack = jnp.concatenate([ref[:, at] for ref in rows], axis=0)
        buf[:, at] = mixed(mix, stack)
    write = pltpu.make_async_copy(buf, out_hbm.at[:, spot], out_sem)
    write.start()
    write.wait()


def own(here, mix, received, basis, chunk=1024):
    cols = basis.shape[1] // 4
    return pl.pallas_call(
        functools.partial(own_kernel, cols=cols, chunk=chunk),
        in_specs=[SMEM_SPEC] + [VMEM_SPEC] * 4 + [HBM_SPEC],
        out_specs=HBM_SPEC,
        out_shape=pltpu.HBM(basis.shape, jnp.float32),
        scratch_shapes=[pltpu.VMEM((PAD, SHARED), jnp.float32)] * 3
        + [pltpu.SemaphoreType.DMA(())] * 2,
        compiler_params=pltpu.CompilerParams(vmem_limit_bytes=10 << 20),
        name="own",
    )(here, *[near(x) for x in (mix, *received)], far(basis))


def join_kernel(here_ref, *refs, sources):
    parts, (_, out_hbm, sems) = refs[: len(sources)], refs[len(sources) :]
    cols = out_hbm.shape[1] // 4
    copies = []
    for g, part in zip(sources, parts):
        size = part.shape[1]
        at = pl.multiple_of(lax.rem(here_ref[0] + g, 4) * cols + cols - size, LANES)
        target = out_hbm.at[:, pl.ds(at, size)]
        copies.append(pltpu.make_async_copy(part, target, sems.at[g]))
        copies[-1].start()
    for copy in copies:
        copy.wait()


def join(here, parts, whole):
    count = len(parts)
    return pl.pallas_call(
        functools.partial(join_kernel, sources=tuple(parts)),
        in_specs=[SMEM_SPEC] + [VMEM_SPEC] * count + [HBM_SPEC],
        out_specs=HBM_SPEC,
        out_shape=pltpu.HBM(whole.shape, jnp.float32),
        scratch_shapes=[pltpu.SemaphoreType.DMA((4,))],
        input_output_aliases={1 + count: 0},
        compiler_params=pltpu.CompilerParams(vmem_limit_bytes=2 << 20),
        name="join",
    )(here, *[near(x) for x in parts.values()], far(whole))


def program(velocity, basis, levels, profile_index, advect):
    n_space, n_mode = lax.axis_size("space"), lax.axis_size("mode")
    comps, cx, _, _ = velocity.shape
    here = lax.axis_index("mode").astype(jnp.int32).reshape(1)
    core = lax.rem(lax.axis_index("space").astype(jnp.int32), 2).reshape(1)

    def shifted(x, axis, by):
        size = lax.axis_size(axis)
        return lax.ppermute(x, axis, [(i, (i + by) % size) for i in range(size)])

    face_lo, face_hi, outer, inner, *blocks = pack(here, core, velocity, basis)
    block_own, block_next, block_far, block_prev = blocks
    zlo = shifted(face_hi, "mode", 1)
    zhi = shifted(face_lo, "mode", -1)
    lo = shifted(block_next, "mode", 1)
    hi = shifted(block_prev, "mode", -1)
    over = shifted(block_far, "mode", 2)
    outer, inner = add_corners(core, zlo, zhi, outer, inner, cx, comps)
    pairs = [(i, (i + (1 if i % 2 else -1)) % n_space) for i in range(n_space)]
    outer = lax.ppermute(outer, "space", pairs)
    inner = lax.ppermute(inner, "space", [(i, i ^ 1) for i in range(n_space)])
    state = inner_planes(velocity, levels, profile_index, advect, zlo, zhi)
    snap, plus, minus, across = snapshots(
        levels,
        profile_index,
        advect,
        here,
        core,
        basis,
        (zlo, zhi, face_lo, face_hi, outer, inner),
        state,
    )
    lo_early = shifted(plus, "mode", 1)
    hi_early = shifted(minus, "mode", -1)
    stack = (snap, block_own, hi, over, lo)
    total = gram(here, stack)
    total = ring_sum(total, ring_parts(total, "space", n_space, 1, 2))
    total = ring_sum(total, ring_parts(total, "space", n_space, 2, 4))
    total = ring_sum(total, ring_parts(total, "mode", n_mode, 1, n_mode))
    parts = [total] + ring_parts(total, "space", n_space, 8, 4)
    over_early = shifted(across, "mode", 2)
    mix, sigma = factor(parts)
    out_own, out_next, out_over, out_prev = update(here, mix, stack)
    back_lo = shifted(out_next, "mode", 1)
    back_hi = shifted(out_prev, "mode", -1)
    back_over = shifted(out_over, "mode", 2)
    mine = own(here, mix, (hi_early, over_early, lo_early), basis)
    modes = join(here, {0: out_own, 1: back_hi, 3: back_lo}, mine)
    modes = join(here, {2: back_over}, modes)
    return (modes, sigma[0, :MODES])


def solution(mesh):
    return jax.shard_map(
        program,
        mesh=mesh,
        in_specs=(P(None, "space", "mode", None), P("mode", "space"), P(), P(), P()),
        out_specs=(P("mode", "space"), P()),
        check_vma=False,
    )
```
